32 devices in a mesh: seq: 4 (over x, core), row: 4 (over z), col: 2 (over y).
Axes of the slice: x: 2, y: 2, z: 4, core: 2. Of those that a mesh axis runs over, the one named last changes fastest.
Arguments:
- tokens: bfloat16 [8192, 768], P(('seq', 'row')), may hold values from -6 to 6
- cotangent: bfloat16 [8192, 768], P(('seq', 'row'), 'col'), may hold values from -6 to 6
- lengths: int32 [3], replicated, may hold values from 1024 to 4096, as said below
- block_order: int32 [16], replicated, may hold values from 0 to 15, each once
- attention_gain: float32 [768], P('col'), may hold values from 0.5 to 1.5
- attention_shift: float32 [768], P('col'), may hold values from -1.75 to 1.75
- feedforward_gain: float32 [768], P('col'), may hold values from 0.5 to 1.5
- feedforward_shift: float32 [768], P('col'), may hold values from -1.75 to 1.75
- query_weight: bfloat16 [768, 768], P('col', 'row'), may hold values from -0.21875 to 0.21875
- query_bias: float32 [768], P('row'), may hold values from -1.75 to 1.75
- keyval_weight: bfloat16 [768, 128], P('col'), may hold values from -0.21875 to 0.21875
- keyval_bias: float32 [128], replicated, may hold values from -1.75 to 1.75
- upward_weight: bfloat16 [768, 3072], P('col', 'row'), may hold values from -0.21875 to 0.21875
- upward_bias: float32 [3072], P('row'), may hold values from -1.75 to 1.75
- output_weight: bfloat16 [768, 768], P('row', 'col'), may hold values from -0.75 to 0.75
- output_bias: float32 [768], P('col'), may hold values from -1.75 to 1.75
- down_weight: bfloat16 [3072, 768], P('row', 'col'), may hold values from -0.109375 to 0.109375
- down_bias: float32 [768], P('col'), may hold values from -1.75 to 1.75
Outputs:
- layer_output: bfloat16 [8192, 768], P(('seq', 'row'), 'col')
- keyval_cache: bfloat16 [8192, 128], P(('seq', 'col'))
- tokens_grad: bfloat16 [8192, 768], P(('seq', 'row'), 'col')
- attention_gain_grad: float32 [768], P('col')
- attention_shift_grad: float32 [768], P('col')
- feedforward_gain_grad: float32 [768], P('col')
- feedforward_shift_grad: float32 [768], P('col')
- query_weight_grad: float32 [768, 768], P('col', 'row')
- query_bias_grad: float32 [768], P('row')
- keyval_weight_grad: float32 [768, 128], P('col', 'row')
- keyval_bias_grad: float32 [128], P('row')
- upward_weight_grad: float32 [768, 3072], P('col', 'row')
- upward_bias_grad: float32 [3072], P('row')
- output_weight_grad: float32 [768, 768], P('row', 'col')
- output_bias_grad: float32 [768], P('col')
- down_weight_grad: float32 [3072, 768], P('row', 'col')
- down_bias_grad: float32 [768], P('col')
The draws below stay inside these ranges and needn't reach their ends.
Inputs may be any that keep to these rules, and one draw needn't show every extreme that they name: Every length is a whole multiple of 512, the lengths sum to 8192, and the longest is exactly 4096. `block_order`: each block number appears once.
All inputs are finite; a program needn't handle non-finite values.
Results may differ from the reference program's by a relative error of at most 0.025.
Values may be sent and summed in bfloat16 or wider, within the bound.
No kernel may reach another device: no remote copies, remote signals or barrier semaphores. Data moves between devices by JAX's collectives and lax.ppermute only.
A program may use at most 256 MiB of HBM per device.

```python
import jax
import jax.numpy as jnp
from jax import lax

D = 768
HQ = 12
HD = 64
ROT = 16
FF = 3072
BLOCK = 512
NB = 16
MAXB = 8
TOKENS = 8192
GROUPS = 4


def draw_lengths(key, part):
    pair_count = (NB - MAXB) // MAXB
    shorter = jax.random.randint(jax.random.fold_in(key, 11), (pair_count,), 2, MAXB - 1)
    paired = jnp.stack([shorter, MAXB - shorter], axis=1).reshape(-1)
    counts = jnp.concatenate([jnp.full((1,), MAXB, jnp.int32), paired.astype(jnp.int32)])
    shuffle = jax.random.permutation(jax.random.fold_in(key, 12), counts.shape[0])
    return (counts[shuffle] * BLOCK).astype(jnp.int32)


def block_scale(own_key, dims, pieces, low, top_value):
    def one(axis_at, parts):
        steps = jax.random.uniform(jax.random.fold_in(jax.random.fold_in(own_key, 6), axis_at), (parts,), jnp.float32, low / len(pieces), top_value / len(pieces))
        return jnp.repeat(jnp.exp(steps), dims[axis_at] // parts).reshape((-1,) + (1,) * (len(dims) - axis_at - 1))

    loudness = one(*pieces[0])
    for cut in pieces[1:]:
        loudness = loudness * one(*cut)
    return loudness


def normal_values(rng, extent, scale, bound, split=(), kind=jnp.bfloat16):
    array = scale * jax.random.normal(rng, extent, jnp.float32)
    if split:
        array = array * block_scale(rng, extent, split, -0.22, 0.18)
    return jnp.clip(array, -bound, bound).astype(kind)


def setup_inputs(seed: int = 0) -> dict:
    seeds = jax.random.split(jax.random.key(seed), 19)
    tokens = normal_values(seeds[0], (TOKENS, D), 1.0, 6.0, ((0, 16),))
    cotangent = normal_values(seeds[1], (TOKENS, D), 1.0, 6.0, ((0, 16), (1, 2)))
    lengths = draw_lengths(jax.random.fold_in(seeds[18], 71), 0)
    block_order = jax.random.permutation(seeds[3], NB).astype(jnp.int32)
    attention_gain = jnp.clip(1.0 + 0.1 * jax.random.normal(seeds[4], (D,), jnp.float32), 0.5, 1.5)
    attention_shift = normal_values(seeds[5], (D,), 0.3, 1.75, ((0, 2),), jnp.float32)
    feedforward_gain = jnp.clip(1.0 + 0.1 * jax.random.normal(seeds[6], (D,), jnp.float32), 0.5, 1.5)
    feedforward_shift = normal_values(seeds[7], (D,), 0.3, 1.75, ((0, 2),), jnp.float32)
    query_weight = normal_values(seeds[8], (D, HQ * HD), D ** -0.5, 0.21875, ((0, 2), (1, 4)))
    query_bias = normal_values(seeds[9], (HQ * HD,), 0.3, 1.75, ((0, 4),), jnp.float32)
    keyval_weight = normal_values(seeds[10], (D, 2 * HD), D ** -0.5, 0.21875, ((0, 2),))
    keyval_bias = normal_values(seeds[11], (2 * HD,), 0.3, 1.75, (), jnp.float32)
    upward_weight = normal_values(seeds[12], (D, FF), D ** -0.5, 0.21875, ((0, 2), (1, 4)))
    upward_bias = normal_values(seeds[13], (FF,), 0.3, 1.75, ((0, 4),), jnp.float32)
    output_weight = normal_values(seeds[14], (HQ * HD, D), HD ** -0.5, 0.75, ((0, 4), (1, 2)))
    output_bias = normal_values(seeds[15], (D,), 0.3, 1.75, ((0, 2),), jnp.float32)
    down_weight = normal_values(seeds[16], (FF, D), FF ** -0.5, 0.109375, ((0, 4), (1, 2)))
    down_bias = normal_values(seeds[17], (D,), 0.3, 1.75, ((0, 2),), jnp.float32)
    return {"tokens": tokens, "cotangent": cotangent, "lengths": lengths, "block_order": block_order, "attention_gain": attention_gain, "attention_shift": attention_shift, "feedforward_gain": feedforward_gain, "feedforward_shift": feedforward_shift, "query_weight": query_weight, "query_bias": query_bias, "keyval_weight": keyval_weight, "keyval_bias": keyval_bias, "upward_weight": upward_weight, "upward_bias": upward_bias, "output_weight": output_weight, "output_bias": output_bias, "down_weight": down_weight, "down_bias": down_bias}


EPS = 1e-05

@jax.custom_vjp
def low(v):
    return lax.optimization_barrier(v.astype(jnp.bfloat16)).astype(jnp.float32)

@jax.custom_vjp
def low_back(v):
    return v

def low_keep(v):
    return (low(v), None)

def low_pass(kept, grad):
    return (grad,)

def back_keep(v):
    return (v, None)

def back_low(kept, grad):
    return (low(grad),)
low.defvjp(low_keep, low_pass)
low_back.defvjp(back_keep, back_low)

def spin_tables(positions, half_rot):
    exponent = jnp.arange(half_rot, dtype=jnp.float32) * (1.0 / half_rot)
    frequency = 1.0 / 10000.0 ** exponent
    angles = positions.astype(jnp.float32)[:, None] * frequency[None, :]
    return (jnp.cos(angles), jnp.sin(angles))

def spin(values_in, cosine_table, sine_table, half_rot):
    front_half = values_in[..., :half_rot]
    behind = values_in[..., half_rot:2 * half_rot]
    return jnp.concatenate([front_half * cosine_table - behind * sine_table, behind * cosine_table + front_half * sine_table, values_in[..., 2 * half_rot:]], axis=-1)

def standardize(values_in):
    row_mean = lax.optimization_barrier(jnp.mean(values_in, axis=-1, keepdims=True))
    spread = lax.optimization_barrier(jnp.mean(values_in * values_in, axis=-1, keepdims=True)) - row_mean * row_mean
    return (values_in - row_mean) * lax.rsqrt(spread + EPS)

def dot_high(left_side, right_side):
    return jnp.dot(left_side, right_side, precision=lax.Precision.HIGHEST)

def reference(tokens, cotangent, lengths, block_order, attention_gain, attention_shift, feedforward_gain, feedforward_shift, query_weight, query_bias, keyval_weight, keyval_bias, upward_weight, upward_bias, output_weight, output_bias, down_weight, down_bias):
    half_rot = ROT // 2
    score_scale = HD ** (-0.5)
    window = MAXB * BLOCK
    group_heads = HQ // GROUPS
    seq_starts = (jnp.cumsum(lengths) - lengths).astype(jnp.int32)
    token_index = jnp.arange(TOKENS, dtype=jnp.int32)
    token_start = lax.optimization_barrier(jnp.max(jnp.where(seq_starts[None, :] <= token_index[:, None], seq_starts[None, :], 0), axis=1)).astype(jnp.int32)
    cosine_table, sine_table = spin_tables(token_index - token_start, half_rot)

    def forward(hidden_in, gain_one, shift_one, gain_two, shift_two, query_w, query_b, keyval_w, keyval_b, upward_w, upward_b, output_w, output_b, down_w, down_b):
        normed = standardize(hidden_in)
        first_in = low(normed * gain_one + shift_one)
        second_in = low(normed * gain_two + shift_two)
        query_pre = dot_high(first_in, query_w) + query_b
        keyval_pre = dot_high(first_in, keyval_w) + keyval_b
        upward = low_back(dot_high(second_in, upward_w) + upward_b)
        activated = low(jax.nn.gelu(upward, approximate=False))
        queries = low(spin(low_back(query_pre).reshape(TOKENS, HQ, HD), cosine_table[:, None, :], sine_table[:, None, :], half_rot))
        key_list = []
        value_list = []
        for group in range(GROUPS):
            pair_pre = low_back(keyval_pre)
            key_list.append(low(spin(pair_pre[:, :HD], cosine_table, sine_table, half_rot)))
            value_list.append(low(pair_pre[:, HD:]))
        key_stack = jnp.stack(key_list)
        value_stack = jnp.stack(value_list)
        padding = jnp.zeros((GROUPS, window - BLOCK, HD), jnp.float32)
        key_pad = jnp.concatenate([padding, key_stack], axis=1)
        value_pad = jnp.concatenate([padding, value_stack], axis=1)

        def attend(block_index):
            block_first = block_index * BLOCK
            query_block = lax.dynamic_slice_in_dim(queries, block_first, BLOCK, 0).reshape(BLOCK, GROUPS, group_heads, HD)
            key_block = low_back(lax.dynamic_slice_in_dim(key_pad, block_first, window, 1))
            value_block = low_back(lax.dynamic_slice_in_dim(value_pad, block_first, window, 1))
            key_index = block_first - (window - BLOCK) + jnp.arange(window, dtype=jnp.int32)
            query_index = block_first + jnp.arange(BLOCK, dtype=jnp.int32)
            seq_begin = lax.dynamic_slice_in_dim(token_start, block_first, 1, 0)[0]
            allowed = (key_index[None, :] >= seq_begin) & (key_index[None, :] <= query_index[:, None])
            scores = low_back(score_scale * jnp.einsum('igjd,gkd->gjik', query_block, key_block, precision=lax.Precision.HIGHEST))
            scores = jnp.where(allowed[None, None], scores, -1e+30)
            weights = low(jax.nn.softmax(scores, axis=-1))
            mixed = jnp.einsum('gjik,gkd->igjd', weights, value_block, precision=lax.Precision.HIGHEST)
            return mixed.reshape(BLOCK, HQ * HD)
        mixed_rows = lax.map(jax.checkpoint(attend), jnp.arange(NB, dtype=jnp.int32))
        mixed_rows = low(low_back(mixed_rows.reshape(TOKENS, HQ * HD)))
        layer_out = hidden_in + dot_high(mixed_rows, output_w) + output_b + dot_high(activated, down_w) + down_b
        return (layer_out, jnp.concatenate([key_list[0], value_list[0]], axis=1))
    floats = (tokens.astype(jnp.float32), attention_gain, attention_shift, feedforward_gain, feedforward_shift, query_weight.astype(jnp.float32), query_bias, keyval_weight.astype(jnp.float32), keyval_bias, upward_weight.astype(jnp.float32), upward_bias, output_weight.astype(jnp.float32), output_bias, down_weight.astype(jnp.float32), down_bias)
    (layer_out, key_cache), pull_back = jax.vjp(forward, *floats)
    gradients = pull_back((cotangent.astype(jnp.float32), jnp.zeros_like(key_cache)))
    dealt_cache = key_cache.reshape(NB, BLOCK, 2 * HD)[block_order].reshape(TOKENS, 2 * HD).astype(jnp.bfloat16)
    return (layer_out.astype(jnp.bfloat16), dealt_cache, gradients[0].astype(jnp.bfloat16), gradients[1], gradients[2], gradients[3], gradients[4], gradients[5], gradients[6], gradients[7], gradients[8], gradients[9], gradients[10], gradients[11], gradients[12], gradients[13], gradients[14])
```

```python
import collections
import functools

import jax
import jax.numpy as jnp
from jax import lax
from jax.experimental import pallas as pl
from jax.experimental.pallas import tpu as pltpu
from jax.sharding import PartitionSpec as P

HD = 64
ROT = 16
BLOCK = 512
LONGEST = 16
VMEM = 60 * 1024 * 1024
Shape = collections.namedtuple("Shape", "seq_count row_count sequences heads")
HALF = 256
EPS = 1e-05
NEGATIVE = -1e30
F32 = jnp.float32
BF16 = jnp.bfloat16

NN = (((1,), (0,)), ((), ()))
NT = (((1,), (1,)), ((), ()))
TN = (((0,), (0,)), ((), ()))


def dot(left, right, dims=NN):
    return lax.dot_general(left, right, dims, preferred_element_type=F32)


def swap(value, axis, bit):
    count = lax.axis_size(axis)
    return lax.ppermute(value, axis, [(i, i ^ bit) for i in range(count)])


def swap_odd_rows(value):
    seq_count, row_count = lax.axis_size("seq"), lax.axis_size("row")
    pairs = []
    for s in range(1, seq_count, 2):
        for r in range(row_count):
            pairs.append((s * row_count + r, s * row_count + (r ^ 2)))
    moved = lax.ppermute(value, ("seq", "row"), pairs)
    return jnp.where(lax.rem(lax.axis_index("seq"), 2) == 0, value, moved)


def swap_add(value, axis, bit):
    rounded = lax.reduce_precision(value, 8, 7)
    return rounded + swap(rounded.astype(BF16), axis, bit).astype(F32)


def split_rows(vector):
    high = lax.reduce_precision(vector, 8, 7)
    return high.astype(BF16), (vector - high).astype(BF16)


def first_of(meta_ref, block, shape):
    start = jnp.int32(0)
    first = jnp.int32(0)
    for i in range(shape.sequences):
        first = jnp.where(start <= block, start, first)
        start = start + meta_ref[3 + i] // BLOCK
    return first


def attention_kernel(
    meta_ref,
    first_ref,
    dy_ref,
    cos_ref,
    sin_ref,
    small0_ref,
    small1_ref,
    kv0_ref,
    kv1_ref,
    kv2_ref,
    kv3_ref,
    *rest,
    shape,
    second,
):
    heads = shape.heads
    rest = list(rest)
    if second:
        dqw_in_ref, dow_in_ref, dqb_in_ref, dkv_in_ref = rest[:4]
        rest = rest[4:]
    out_ref, dx_ref, dqw_ref, dow_ref, dqb_ref, dkv_out_ref, last_ref = rest[:7]
    (
        qd_ref,
        probs_ref,
        high_ref,
        sums_ref,
        dots_ref,
        acc_ref,
        dq_ref,
        dkv_ref,
        kv_ref,
        low_ref,
        qw_ref,
        ow_ref,
        copy_sem,
    ) = rest[7:]
    blocks = kv_ref.shape[0]
    half = blocks // 2
    slot = pl.program_id(0)
    lanes = 2 * HD
    rows = heads * HALF
    seq, row, second_half = meta_ref[0], meta_ref[1], meta_ref[2]
    own_block = lax.bitwise_xor(seq, slot) * shape.row_count + lax.bitwise_xor(
        row, 1 - slot if second else slot
    )
    first_block = first_of(meta_ref, own_block, shape)
    before = own_block - first_block

    def slot_of(block):
        apart_row = lax.bitwise_xor(lax.rem(block, shape.row_count), row)
        apart_seq = lax.bitwise_xor(block // shape.row_count, seq)
        return apart_row + shape.row_count * (
            apart_seq // 2 + (shape.seq_count // 2) * lax.rem(apart_seq, 2)
        )

    @pl.when(slot == 0)
    def _():
        copies = [
            pltpu.make_async_copy(
                piece,
                kv_ref.at[
                    (i // 2) * half : (i // 2 + 1) * half, (i % 2) * HALF : (i % 2 + 1) * HALF, :
                ],
                copy_sem.at[i],
            )
            for i, piece in enumerate((kv0_ref, kv1_ref, kv2_ref, kv3_ref))
        ]
        if second:
            copies.append(pltpu.make_async_copy(dkv_in_ref, dkv_ref, copy_sem.at[4]))
        for copy in copies:
            copy.start()
        span = small0_ref.shape[1]
        count = heads * HD
        for i, small in enumerate((small0_ref, small1_ref)):
            part = slice(i * span, (i + 1) * span)
            qw_ref[:count, part] = small[:count, :]
            ow_ref[:count, part] = small[count : 2 * count, :]
        qw_ref[count:, :] = jnp.zeros_like(qw_ref[count:, :])
        ow_ref[count:, :] = jnp.zeros_like(ow_ref[count:, :])
        if second:
            dqw_ref[...] = dqw_in_ref[...]
            dow_ref[...] = dow_in_ref[...]
            dqb_ref[...] = dqb_in_ref[...]
        else:
            dkv_ref[...] = jnp.zeros_like(dkv_ref)
            dqw_ref[...] = jnp.zeros_like(dqw_ref)
            dow_ref[...] = jnp.zeros_like(dow_ref)
            dqb_ref[...] = jnp.zeros_like(dqb_ref)
        for copy in copies:
            copy.wait()
        if not second:
            copies = []
            dealt = last_ref.shape[0]
            group = seq * 2 + second_half
            for i in range(dealt):
                owner = meta_ref[3 + shape.sequences + group * dealt + i]
                for part in (0, 1):
                    take = jnp.where(second_half > 0, 1 - part, part) * HALF
                    copies.append(
                        pltpu.make_async_copy(
                            kv_ref.at[slot_of(owner), pl.ds(take, HALF), :],
                            last_ref.at[i, part * HALF : (part + 1) * HALF, :],
                            copy_sem.at[5 + 2 * i + part],
                        )
                    )
            for copy in copies:
                copy.start()
            for copy in copies:
                copy.wait()

    cosine = cos_ref[0]
    sine = sin_ref[0]
    lane = lax.broadcasted_iota(jnp.int32, (HALF, lanes), 1)
    front = lane < HD

    def rolled(values):
        return jnp.where(
            lane < ROT // 2,
            pltpu.roll(values, lanes - ROT // 2, 1),
            pltpu.roll(values, ROT // 2, 1),
        )

    def head_of(joined, h):
        return joined[:, (h // 2) * lanes : (h // 2 + 1) * lanes]

    def join(parts):
        tiles = []
        for h in range(0, heads, 2):
            other = parts[h + 1] if h + 1 < heads else jnp.zeros_like(parts[h])
            tiles.append(jnp.where(front, parts[h], other))
        return jnp.concatenate(tiles, axis=1)

    padded = qw_ref.shape[0]
    base = 2 * heads * HD + 7
    query_b = (
        small0_ref[base : base + 1, :padded].astype(F32)
        + small0_ref[base + 8 : base + 9, :padded].astype(F32)
    )
    pre_all = dot(first_ref[0], qw_ref[...], NT) + query_b
    d_all = dot(dy_ref[0], ow_ref[...], NT)
    for h in range(heads):
        pre = head_of(pre_all, h)
        grad = head_of(d_all, h)
        if h % 2:
            pre = pltpu.roll(pre, HD, 1)
        else:
            grad = pltpu.roll(grad, HD, 1)
        turned = jnp.where(front, pre * cosine + rolled(pre) * sine, 0.0)
        mine = slice(h * HALF, (h + 1) * HALF)
        qd_ref[mine, :] = turned.astype(BF16) * BF16(HD**-0.5)
        qd_ref[rows + h * HALF : rows + (h + 1) * HALF, :] = jnp.where(front, 0.0, grad).astype(BF16)

    high_ref[...] = jnp.full_like(high_ref, NEGATIVE)
    sums_ref[...] = jnp.zeros_like(sums_ref)

    def block_at(step):
        return slot_of(first_block + step)

    def weigh(step, mask):
        scores = dot(kv_ref[block_at(step)], qd_ref[:rows, :], NT)
        if mask:
            row_in = lax.rem(lax.broadcasted_iota(jnp.int32, (BLOCK, rows), 1), HALF)
            key_in = lax.broadcasted_iota(jnp.int32, (BLOCK, rows), 0)
            limit = jnp.where(second_half > 0, BLOCK, 0)
            keep = (key_in <= row_in) | ((key_in >= HALF) & (key_in < limit))
            scores = jnp.where(keep, scores, NEGATIVE)
        high = jnp.max(scores, axis=0, keepdims=True)
        probs = jnp.exp(scores - high)
        probs_ref[step] = probs.astype(BF16)
        high_ref[pl.ds(step, 1), :] = high
        sums_ref[pl.ds(step, 1), :] = jnp.sum(probs, axis=0, keepdims=True)

    weigh(before, True)
    lax.fori_loop(0, before, lambda step, c: (weigh(step, False), c)[1], 0)

    share = jnp.exp(high_ref[...] - jnp.max(high_ref[...], axis=0, keepdims=True))
    high_ref[...] = share / jnp.sum(share * sums_ref[...], axis=0, keepdims=True)

    def mix(step, first):
        probs = (probs_ref[step].astype(F32) * high_ref[pl.ds(step, 1), :]).astype(BF16)
        probs_ref[step] = probs
        part = dot(probs, kv_ref[block_at(step)], TN)
        if first:
            acc_ref[...] = part
        else:
            acc_ref[...] += part

    mix(before, True)
    lax.fori_loop(0, before, lambda step, c: (mix(step, False), c)[1], 0)

    parts = []
    for h in range(heads):
        mine = slice(h * HALF, (h + 1) * HALF)
        mixed = acc_ref[mine, :]
        grad = qd_ref[rows + h * HALF : rows + (h + 1) * HALF, :].astype(F32)
        dots_ref[:, mine] = jnp.sum(jnp.transpose(mixed * grad), axis=0, keepdims=True)
        parts.append(mixed if h % 2 else pltpu.roll(mixed, HD, 1))
    joined = join(parts).astype(BF16)
    out_ref[0] = dot(joined, ow_ref[...])
    dow_ref[...] += dot(joined, dy_ref[0], TN)

    def backward(step, first):
        where = block_at(step)
        block = kv_ref[where]
        probs = probs_ref[step]
        grad_probs = dot(block, qd_ref[rows:, :], NT)
        grad_scores = (probs.astype(F32) * (grad_probs - dots_ref[...])).astype(BF16)
        total = dot(jnp.concatenate([grad_scores, probs], axis=1), qd_ref[...])
        grad_q = dot(grad_scores, block, TN)
        if first:
            dq_ref[...] = grad_q
        else:
            dq_ref[...] += grad_q
        dkv_ref[where] = (dkv_ref[where].astype(F32) + total).astype(dkv_ref.dtype)

    backward(before, True)
    lax.fori_loop(0, before, lambda step, c: (backward(step, False), c)[1], 0)

    parts = []
    for h in range(heads):
        part = dq_ref[h * HALF : (h + 1) * HALF, :] * (HD**-0.5)
        part = part * cosine - rolled(part) * sine
        parts.append(pltpu.roll(part, HD, 1) if h % 2 else part)
    joined = join(parts)
    dqb_ref[...] += jnp.sum(joined, axis=0, keepdims=True)
    joined = joined.astype(BF16)
    dx_ref[0] = dot(joined, qw_ref[...])
    dqw_ref[...] += dot(joined, first_ref[0], TN)

    @pl.when(slot == 1)
    def _():
        if not second:
            copies = [pltpu.make_async_copy(dkv_ref, dkv_out_ref, copy_sem.at[0])]
            copies[0].start()
        else:
            copies = [pltpu.make_async_copy(dkv_ref.at[:half], dkv_out_ref, copy_sem.at[0])]
            copies[0].start()
            if dkv_ref.dtype == BF16:
                copies.append(pltpu.make_async_copy(dkv_ref.at[half:], last_ref, copy_sem.at[1]))
            else:
                low_ref[...] = dkv_ref[half:].astype(BF16)
                copies.append(pltpu.make_async_copy(low_ref, last_ref, copy_sem.at[1]))
            copies[1].start()
        for copy in copies:
            copy.wait()


def attention(meta, first_in, dy, cosine, sine, small, pieces, so_far, shape):
    second = so_far is not None
    _, _, width = first_in.shape
    half = pieces[0].shape[0]
    blocks = 2 * half
    lanes = 2 * HD
    heads = shape.heads
    padded = -(-heads // 2) * lanes
    rows = heads * HALF
    longest = min(LONGEST, blocks // 2)
    total_type = F32 if blocks <= 32 else BF16
    dealt = blocks // (2 * shape.seq_count)
    offset = 2 if second else 0

    def per_slot(lanes):
        return pl.BlockSpec((1, HALF, lanes), lambda i, m: (i + offset, 0, 0))

    def out_slot(lanes):
        return pl.BlockSpec((1, HALF, lanes), lambda i, m: (i, 0, 0))

    def whole(array):
        return pl.BlockSpec(
            array.shape, lambda i, m: (0,) * len(array.shape), pipeline_mode=pl.Buffered(buffer_count=1)
        )

    far = pl.BlockSpec(memory_space=pltpu.MemorySpace.HBM)
    arrays = [first_in, dy, cosine, sine, *small, *pieces]
    in_specs = [per_slot(width), per_slot(width), per_slot(lanes), per_slot(lanes)]
    in_specs += [whole(a) for a in small] + [far] * 4
    if second:
        arrays += list(so_far)
        in_specs += [whole(a) for a in so_far[:3]] + [far]
    weight = jax.ShapeDtypeStruct((padded, width), F32)
    bias = jax.ShapeDtypeStruct((1, padded), F32)
    out_shape = [
        jax.ShapeDtypeStruct((2, HALF, width), F32),
        jax.ShapeDtypeStruct((2, HALF, width), F32),
        weight,
        weight,
        bias,
        jax.ShapeDtypeStruct((half if second else blocks, BLOCK, lanes), total_type),
        jax.ShapeDtypeStruct((half if second else dealt, BLOCK, lanes), BF16),
    ]
    out_specs = [out_slot(width), out_slot(width), whole(weight), whole(weight), whole(bias), far, far]
    return pl.pallas_call(
        functools.partial(attention_kernel, shape=shape, second=second),
        grid_spec=pltpu.PrefetchScalarGridSpec(
            num_scalar_prefetch=1,
            grid=(2,),
            in_specs=in_specs,
            out_specs=out_specs,
            scratch_shapes=[
                pltpu.VMEM((2 * rows, lanes), BF16),
                pltpu.VMEM((longest, BLOCK, rows), BF16),
                pltpu.VMEM((longest, rows), F32),
                pltpu.VMEM((longest, rows), F32),
                pltpu.VMEM((1, rows), F32),
                pltpu.VMEM((rows, lanes), F32),
                pltpu.VMEM((rows, lanes), F32),
                pltpu.VMEM((blocks, BLOCK, lanes), total_type),
                pltpu.VMEM((blocks, BLOCK, lanes), BF16),
                pltpu.VMEM((half if second and blocks <= 32 else 1, BLOCK, lanes), BF16),
                pltpu.VMEM((padded, width), BF16),
                pltpu.VMEM((padded, width), BF16),
                pltpu.SemaphoreType.DMA((5 + 2 * dealt,)),
            ],
        ),
        out_shape=out_shape,
        cost_estimate=pl.CostEstimate(
            flops=12_000_000_000, bytes_accessed=15_000_000, transcendentals=15_000_000
        ),
        compiler_params=pltpu.CompilerParams(
            vmem_limit_bytes=67_043_328 if blocks > 32 else VMEM
        ),
        name="attention",
    )(meta, *arrays)


ORDER = (0, 3, 1, 2)


def tables_kernel(meta_ref, cos_ref, sin_ref, *, shape):
    seq, row, col = meta_ref[0], meta_ref[1], meta_ref[2]
    lane = lax.broadcasted_iota(jnp.int32, (HALF, 2 * HD), 1)
    inside = lax.broadcasted_iota(jnp.int32, (HALF, 2 * HD), 0) + col * HALF
    half_rot = ROT // 2
    exponent = lax.rem(lane, half_rot).astype(F32) * (1.0 / half_rot)
    frequency = jnp.where(lane < ROT, 1.0 / jnp.exp(exponent * jnp.log(jnp.full_like(exponent, 10000.0))), 0.0)
    for i, slot in enumerate(ORDER):
        block = lax.bitwise_xor(seq, slot // 2) * shape.row_count + lax.bitwise_xor(row, slot % 2)
        start = (block - first_of(meta_ref, block, shape)) * BLOCK
        angles = (inside + start).astype(F32) * frequency
        cos_ref[i] = jnp.cos(angles)
        turned = jnp.sin(angles)
        sin_ref[i] = jnp.where(lane < half_rot, -turned, jnp.where(lane < ROT, turned, 0.0))


def tables(meta, shape):
    table = jax.ShapeDtypeStruct((4, HALF, 2 * HD), F32)
    return pl.pallas_call(
        functools.partial(tables_kernel, shape=shape),
        in_specs=[pl.BlockSpec(memory_space=pltpu.SMEM)],
        out_specs=[pl.BlockSpec(memory_space=pltpu.VMEM)] * 2,
        out_shape=[table, table],
        name="tables",
    )(meta)


def forward_kernel(
    both0_ref,
    both3_ref,
    both1_ref,
    both2_ref,
    vec_ref,
    small_ref,
    up0_ref,
    up1_ref,
    down0_ref,
    down1_ref,
    first_ref,
    dy_ref,
    out_ref,
    dx_ref,
    keep_ref,
    send_ref,
    stat_ref,
    x_ref,
    up_ref,
    down_ref,
    second_ref,
    hidden_ref,
    grad_ref,
    dys_ref,
    bias_ref,
):
    step = pl.program_id(0)
    span = up0_ref.shape[0]
    here = pl.ds(pl.multiple_of(step * HALF, HALF), HALF)

    @pl.when(step == 0)
    def _():
        up_ref[:span, :] = up0_ref[...]
        up_ref[span:, :] = up1_ref[...]
        down_ref[:, :span] = down0_ref[...]
        down_ref[:, span:] = down1_ref[...]
        bias_ref[...] = jnp.zeros_like(bias_ref)

    for i, piece in enumerate((both0_ref, both3_ref, both1_ref, both2_ref)):

        @pl.when(step == i)
        def _():
            x_ref[...] = piece[0]
            dys_ref[here, :] = piece[1]

    base = small_ref.shape[0] - 16
    bias = small_ref[base : base + 8, :].astype(F32) + small_ref[base + 8 :, :].astype(F32)
    upward_b = jnp.concatenate([bias[5:6], bias[6:7]], axis=1)
    wide = x_ref[...].astype(F32)
    mean = jnp.mean(wide, axis=1, keepdims=True)
    spread = jnp.mean(wide * wide, axis=1, keepdims=True) - mean * mean
    normed = (wide - mean) * lax.rsqrt(spread + EPS)
    first_ref[0] = (normed * vec_ref[0:1, :] + vec_ref[1:2, :]).astype(BF16)
    second = (normed * vec_ref[2:3, :] + vec_ref[3:4, :]).astype(BF16)
    dy = dys_ref[here, :]
    dy_ref[0] = dy
    second_ref[here, :] = second
    upward = dot(second, up_ref[...]) + upward_b
    bell = lax.erf(upward * (2.0**-0.5)) * 0.5 + 0.5
    hidden = (upward * bell).astype(BF16)
    slope = bell + upward * jnp.exp(upward * upward * -0.5) * ((2.0 * 3.141592653589793) ** -0.5)
    grad = dot(dy, down_ref[...], NT) * slope
    bias_ref[0:1, :] += jnp.sum(grad, axis=0, keepdims=True)
    grad = grad.astype(BF16)
    hidden_ref[here, :] = hidden
    grad_ref[here, :] = grad
    out_ref[0] = dot(hidden, down_ref[...])
    dx_ref[0] = dot(grad, up_ref[...], NT) * vec_ref[2:3, :]

    @pl.when(step == 3)
    def _():
        down_grad = dot(hidden_ref[...], dys_ref[...], TN)
        keep_ref[2 * span :, :] = down_grad[:, :span].astype(BF16)
        send_ref[2 * span :, :] = down_grad[:, span:].astype(BF16)
        up_grad = dot(second_ref[...], grad_ref[...], TN)
        for i in (0, 1):
            part = slice(i * span, (i + 1) * span)
            keep_ref[part, :] = up_grad[:span, part].astype(BF16)
            send_ref[part, :] = up_grad[span:, part].astype(BF16)
        weight = up_ref[...].astype(F32)
        bias_grad = bias_ref[0:1, :]

        def as_row(values):
            column = jnp.sum(values, axis=1, keepdims=True)
            return jnp.transpose(jnp.broadcast_to(column, (2 * span, 128)))[0:1, :]

        plain = as_row(weight * bias_grad)
        stat_ref[0:1, :] = (as_row(weight * up_grad) - vec_ref[3:4, :] * plain) / vec_ref[2:3, :]
        stat_ref[1:2, :] = plain
        stat_ref[2:3, :] = bias_grad
        stat_ref[3:8, :] = jnp.zeros((5, 2 * span), F32)


def feed_forward(both, vectors, small, up, down):
    width = vectors.shape[1]
    span = width // 2
    hidden = up[0].shape[1]

    def whole(array):
        return pl.BlockSpec(
            array.shape, lambda i: (0,) * len(array.shape), pipeline_mode=pl.Buffered(buffer_count=1)
        )

    slot = pl.BlockSpec((1, HALF, width), lambda i: (i, 0, 0))
    arrays = [*both, vectors, small, *up, *down]
    half = jax.ShapeDtypeStruct((2 * span + hidden, span), BF16)
    stat = jax.ShapeDtypeStruct((8, width), F32)
    tokens = lambda kind: jax.ShapeDtypeStruct((4, HALF, width), kind)
    return pl.pallas_call(
        forward_kernel,
        grid=(4,),
        in_specs=[whole(a) for a in arrays],
        out_specs=[slot] * 4 + [whole(half), whole(half), whole(stat)],
        out_shape=[tokens(BF16), tokens(BF16), tokens(F32), tokens(F32), half, half, stat],
        scratch_shapes=[
            pltpu.VMEM((HALF, width), BF16),
            pltpu.VMEM((width, hidden), BF16),
            pltpu.VMEM((hidden, width), BF16),
            pltpu.VMEM((4 * HALF, width), BF16),
            pltpu.VMEM((4 * HALF, hidden), BF16),
            pltpu.VMEM((4 * HALF, hidden), BF16),
            pltpu.VMEM((4 * HALF, width), BF16),
            pltpu.VMEM((8, hidden), F32),
        ],
        cost_estimate=pl.CostEstimate(
            flops=7_000_000_000, bytes_accessed=20_000_000, transcendentals=3_000_000
        ),
        compiler_params=pltpu.CompilerParams(vmem_limit_bytes=VMEM),
        name="feed_forward",
    )(*arrays)


def prologue_kernel(
    where_ref, tokens_ref, dy_ref, kvw_ref, qw_ref, ow_ref, vec_ref, pack_ref, x_ref, mine_ref, small_ref
):
    col = where_ref[2]
    span = dy_ref.shape[1]
    width = tokens_ref.shape[1]
    here = pl.ds(pl.multiple_of(col * HALF, HALF), HALF)
    there = pl.ds(pl.multiple_of((1 - col) * HALF, HALF), HALF)
    pack_ref[:HALF, :] = dy_ref[there, :]
    base = HALF + 2 * HD
    pack_ref[HALF:base, :] = jnp.transpose(kvw_ref[...].astype(F32)).astype(BF16)
    vectors = vec_ref[...]
    high = vectors.astype(BF16).astype(F32)
    both = jnp.concatenate([high, vectors - high], axis=0).astype(BF16)
    pack_ref[base:, :] = both
    x_ref[:, :span] = tokens_ref[here, pl.ds(pl.multiple_of(col * span, 128), span)]
    x_ref[:, span:] = tokens_ref[here, pl.ds(pl.multiple_of((1 - col) * span, 128), span)]
    mine_ref[...] = dy_ref[here, :]
    count = qw_ref.shape[0]
    small_ref[:count, :] = qw_ref[...]
    small_ref[count : 2 * count, :] = ow_ref[...]
    small_ref[2 * count :, :] = both


def prologue(col, tokens, cotangent, keyval_weight, query_weight, output_weight, vectors):
    width = tokens.shape[1]
    span = width // 2
    rows = vectors.shape[0]
    count = query_weight.shape[0]
    vmem = pl.BlockSpec(memory_space=pltpu.VMEM)
    return pl.pallas_call(
        prologue_kernel,
        in_specs=[pl.BlockSpec(memory_space=pltpu.SMEM)] + [vmem] * 6,
        out_specs=[vmem] * 4,
        out_shape=[
            jax.ShapeDtypeStruct((HALF + 2 * HD + 2 * rows, span), BF16),
            jax.ShapeDtypeStruct((HALF, width), BF16),
            jax.ShapeDtypeStruct((HALF, span), BF16),
            jax.ShapeDtypeStruct((2 * count + 2 * rows, span), BF16),
        ],
        name="prologue",
    )(col, tokens, cotangent, keyval_weight, query_weight, output_weight, vectors)


def own_kernel(
    x_ref, mine_ref, pack_ref, got_ref, vec_ref, cos_ref, sin_ref, bias_ref, pair_ref, both_ref, kvw_ref, full_ref
):
    span = mine_ref.shape[1]
    rows = vec_ref.shape[0]
    base = HALF + 2 * HD
    other = got_ref[base : base + 2 * rows, :].astype(F32)
    full = jnp.concatenate([vec_ref[...], other[:rows] + other[rows:]], axis=1)
    full_ref[...] = full
    both_ref[0] = x_ref[...]
    both_ref[1, :, :span] = mine_ref[...]
    both_ref[1, :, span:] = got_ref[:HALF, :]
    kvw_ref[:, :span] = pack_ref[HALF:base, :]
    kvw_ref[:, span:] = got_ref[HALF:base, :]
    wide = x_ref[...].astype(F32)
    mean = jnp.mean(wide, axis=1, keepdims=True)
    spread = jnp.mean(wide * wide, axis=1, keepdims=True) - mean * mean
    normed = (wide - mean) * lax.rsqrt(spread + EPS)
    first = (normed * full[0:1, :] + full[1:2, :]).astype(BF16)
    pre = dot(first, kvw_ref[...], NT) + bias_ref[...]
    lane = lax.broadcasted_iota(jnp.int32, pre.shape, 1)
    lanes = pre.shape[1]
    rolled = jnp.where(
        lane < ROT // 2, pltpu.roll(pre, lanes - ROT // 2, 1), pltpu.roll(pre, ROT // 2, 1)
    )
    pair_ref[0] = (pre * cos_ref[0] + rolled * sin_ref[0]).astype(BF16)


def own_pairs(x_own, mine, pack, got, vectors, cosine, sine, bias):
    width = x_own.shape[1]
    vmem = pl.BlockSpec(memory_space=pltpu.VMEM)
    return pl.pallas_call(
        own_kernel,
        in_specs=[vmem] * 8,
        out_specs=[vmem] * 4,
        out_shape=[
            jax.ShapeDtypeStruct((1, HALF, 2 * HD), BF16),
            jax.ShapeDtypeStruct((2, HALF, width), BF16),
            jax.ShapeDtypeStruct((2 * HD, width), BF16),
            jax.ShapeDtypeStruct((vectors.shape[0], width), F32),
        ],
        name="own_pairs",
    )(x_own, mine, pack, got, vectors, cosine, sine, bias)


def after(value, *others):
    return lax.optimization_barrier((value,) + others)[0]


def weights_over_col(partial):
    half = partial.shape[1] // 2
    received = swap(partial[:, half:].astype(BF16), "col", 1)
    return (partial[:, :half].astype(F32) + received.astype(F32)).astype(BF16)


def weights_over_rest(moved):
    core = lax.rem(lax.axis_index("seq"), 2)
    half = moved.shape[0] // 2
    keep = lax.dynamic_slice_in_dim(moved, core * half, half, 0).astype(F32)
    send = lax.dynamic_slice_in_dim(moved, (1 - core) * half, half, 0)
    total = keep + swap(send, "seq", 1).astype(F32)
    bit = 2
    while bit < lax.axis_size("seq"):
        total = swap_add(total, "seq", bit)
        bit = bit * 2
    total = total.astype(BF16)
    other = swap(total, "seq", 1)
    first = jnp.where(core == 0, total, other)
    second = jnp.where(core == 0, other, total)
    return jnp.concatenate([first, second], axis=0).astype(F32)


def on_device(
    tokens,
    cotangent,
    lengths,
    block_order,
    attention_gain,
    attention_shift,
    feedforward_gain,
    feedforward_shift,
    query_weight,
    query_bias,
    keyval_weight,
    keyval_bias,
    upward_weight,
    upward_bias,
    output_weight,
    output_bias,
    down_weight,
    down_bias,
):
    seq_count = lax.axis_size("seq")
    row_count = lax.axis_size("row")
    col_count = lax.axis_size("col")
    seq_me = lax.axis_index("seq")
    row_me = lax.axis_index("row")
    col_me = lax.axis_index("col")
    block_total = block_order.shape[0]
    width = tokens.shape[1]
    span = width // 2
    heads = query_weight.shape[1] // HD
    head_width = heads * HD
    pair_width = 2 * HD

    shape = Shape(seq_count, row_count, lengths.shape[0], heads)
    meta = jnp.concatenate(
        [jnp.stack([seq_me, row_me, col_me]).astype(jnp.int32), lengths, block_order]
    )

    vectors = jnp.concatenate(
        [
            attention_gain,
            attention_shift,
            feedforward_gain,
            feedforward_shift,
            output_bias + down_bias,
            upward_bias,
            query_bias,
            jnp.zeros((span - head_width,), F32),
        ]
    ).reshape(8, span)
    pack, x_own, dy_mine, small = prologue(
        meta, tokens, cotangent, keyval_weight, jnp.transpose(query_weight), output_weight, vectors
    )
    received = swap(pack, "col", 1)
    cosine, sine = tables(after(meta, pack), shape)
    half_rot = ROT // 2

    def norm(values):
        wide = values.astype(F32)
        mean = jnp.mean(wide, axis=-1, keepdims=True)
        spread = jnp.mean(wide * wide, axis=-1, keepdims=True) - mean * mean
        root = lax.rsqrt(spread + EPS)
        return (wide - mean) * root, root

    def turn(values, cosine, sine):
        rolled = jnp.concatenate(
            [
                values[:, half_rot:ROT],
                values[:, :half_rot],
                jnp.zeros((values.shape[0], pair_width - ROT), F32),
            ],
            axis=1,
        )
        return values * cosine + rolled * sine

    pairs, both, keyval_full, vec_full = own_pairs(
        x_own, dy_mine, pack, received, vectors, cosine, sine, keyval_bias[None]
    )
    gain_a, shift_a, gain_f, shift_f, bias_out = [vec_full[i][None] for i in range(5)]
    steps = [("row", 1), ("row", 2)]
    bit = 2
    while bit < seq_count:
        steps.append(("seq", bit))
        bit = bit * 2
    small_own = swap_odd_rows(small)
    up_own = swap_odd_rows(upward_weight)
    small_full = (small_own, swap(small_own, "col", 1))
    both_got = None
    for i, (axis, bit) in enumerate(steps):
        got = swap(pairs, axis, bit)
        if i == 0:
            both_got = swap(after(both, got), "row", 1)
            down_own = swap_odd_rows(after(down_weight, got))
        if i == 1:
            up_full = (up_own, swap(after(up_own, got), "col", 1))
        pairs = jnp.concatenate([pairs, got], axis=0)
    pairs_col = swap(pairs, "col", 1)
    pieces = (pairs, pairs_col, swap(pairs, "seq", 1), swap(pairs_col, "seq", 1))

    first_in, dy_all, ff_out, ff_grad, ff_keep, ff_send, ff_stats = feed_forward(
        (both, swap(both_got, "seq", 1), both_got, swap(both, "seq", 1)),
        vec_full,
        small_own,
        up_full,
        (down_own, swap(after(down_own, pairs_col), "col", 1)),
    )

    ff_got = swap(ff_send, "col", 1)
    ff_sum = (ff_keep.astype(F32) + ff_got.astype(F32)).astype(BF16)
    out_a, dx_a, dquery_w, doutput_w, dquery_b, dpairs, cache_rows = attention(
        after(meta, ff_send), first_in, dy_all, cosine, sine, small_full, pieces, None, shape
    )
    ff_moved = swap_odd_rows(ff_sum)
    out_b, dx_b, dquery_w, doutput_w, dquery_b, keep_pairs, send_pairs = attention(
        after(meta, ff_sum),
        first_in,
        dy_all,
        cosine,
        sine,
        small_full,
        pieces,
        (dquery_w, doutput_w, dquery_b, dpairs),
        shape,
    )

    total = keep_pairs.astype(F32) + swap(after(send_pairs, ff_moved), "seq", 1).astype(F32)
    first_total = total
    total = total[:, :HALF] + swap(total[:, HALF:].astype(BF16), "col", 1).astype(F32)
    col_total = total
    for axis, bit in reversed(steps[1:]):
        half = total.shape[0] // 2
        total = total[:half] + swap(total[half:].astype(BF16), axis, bit).astype(F32)
    own_total = total[0] + swap(total[1].astype(BF16), "row", 1).astype(F32)
    grad_pair = turn(
        total.reshape(2 * HALF, pair_width),
        jnp.concatenate([cosine[0], cosine[2]], axis=0),
        -jnp.concatenate([sine[0], sine[2]], axis=0),
    )
    grad_keyval = dot(grad_pair.astype(BF16), jnp.concatenate([first_in[0], first_in[2]], axis=0), TN)
    own_pair = turn(own_total, cosine[0], -sine[0]).astype(BF16)
    grad_first_kv = dot(own_pair, keyval_full)

    send = jnp.stack(
        [
            out_b[1] + ff_out[3],
            out_a[1] + ff_out[1],
            dx_b[1] * gain_a + ff_grad[3],
            dx_a[1] * gain_a + ff_grad[1],
        ]
    ).astype(BF16)
    got = swap(send, "seq", 1).astype(F32)
    away = jnp.stack(
        [out_b[0] + ff_out[2] + got[1], dx_b[0] * gain_a + ff_grad[2] + got[3]]
    ).astype(BF16)
    back = swap(after(away, col_total), "row", 1).astype(F32)
    out_one = out_a[0] + ff_out[0] + got[0] + back[0]
    grad_one = dx_a[0] * gain_a + ff_grad[0] + got[2] + back[1]
    x_wide = x_own.astype(F32)
    out_rows = (x_wide + out_one + bias_out).astype(BF16)
    grad_one = grad_one + grad_first_kv * gain_a
    normed_own, root_own = norm(x_own)
    moment_one = jnp.mean(grad_one, axis=1, keepdims=True)
    moment_two = jnp.mean(grad_one * normed_own, axis=1, keepdims=True)
    dy_own = dy_all[0]
    grad_rows = (
        dy_own.astype(F32) + root_own * (grad_one - moment_one - normed_own * moment_two)
    ).astype(BF16)

    def give(rows):
        mine = rows[:, :span]
        other = swap(rows[:, span:], "col", 1)
        return jnp.concatenate(
            [jnp.where(col_me == 0, mine, other), jnp.where(col_me == 0, other, mine)], axis=0
        )

    layer_out = give(out_rows)
    grad_tokens = give(grad_rows)

    sum_ff = weights_over_rest(ff_moved)
    sum_up = jnp.concatenate([sum_ff[:span], sum_ff[span : 2 * span]], axis=1)
    sum_down = sum_ff[2 * span :]
    bias_query = jnp.pad(dquery_b[:, :head_width], ((0, 0), (0, span - head_width)))
    bias_part = jnp.concatenate([ff_stats[2].reshape(2, span), bias_query], axis=0)
    bias_part = lax.reduce_precision(jnp.concatenate([bias_part, bias_part], axis=1), 8, 7)
    small_part = jnp.concatenate(
        [
            dquery_w[:head_width],
            doutput_w[:head_width],
            jnp.pad(bias_part, ((0, 29), (0, 0))),
        ],
        axis=0,
    )
    small_part = after(small_part, first_total)
    sum_small = weights_over_rest(swap_odd_rows(after(weights_over_col(small_part), col_total)))
    sum_query = jnp.transpose(sum_small[:head_width])
    sum_output = sum_small[head_width : 2 * head_width]
    base = 2 * head_width
    sum_bias_up = sum_small[base : base + 2].reshape(-1)
    sum_bias_query = sum_small[base + 2, :head_width]

    query_wide = jnp.concatenate([part[:head_width] for part in small_full], axis=1).astype(F32)
    keyval_wide = keyval_full.astype(F32)
    bias_q = dquery_b[0, :head_width][:, None]
    pair_bias = jnp.sum(grad_pair, axis=0)
    stat_a = (
        jnp.sum(query_wide * (dquery_w[:head_width] - bias_q * shift_a), axis=0)
        + jnp.sum(keyval_wide * (grad_keyval - pair_bias[:, None] * shift_a), axis=0)
    ) / gain_a[0]
    stat_as = jnp.sum(query_wide * bias_q, axis=0) + jnp.sum(keyval_wide * pair_bias[:, None], axis=0)
    stats = jnp.concatenate([stat_a[None], stat_as[None], ff_stats[:2]], axis=0)
    pair_row = jnp.pad(pair_bias[None], ((0, 0), (0, span - pair_width)))
    pair_row = lax.reduce_precision(pair_row, 8, 7)
    dy_sum = jnp.sum(cotangent.astype(F32), axis=0)[None]
    extra = jnp.concatenate(
        [
            grad_keyval,
            stats,
            jnp.concatenate([pair_row, pair_row], axis=1),
            jnp.concatenate([dy_sum, jnp.zeros_like(dy_sum)], axis=1),
            jnp.zeros((10, width), F32),
        ],
        axis=0,
    )
    extra = extra[:, :span] + swap(extra[:, span:].astype(BF16), "col", 1).astype(F32)
    bit = 1
    while bit < seq_count:
        extra = swap_add(extra, "seq", bit)
        bit = bit * 2
    for bit in (1, 2):
        extra = swap_add(extra, "row", bit)
    part = pair_width // row_count
    keyval_weight_out = jnp.transpose(lax.dynamic_slice_in_dim(extra, row_me * part, part, 0))
    keyval_bias_out = lax.dynamic_slice_in_dim(extra[pair_width + 4], row_me * part, part, 0)
    bias_out_grad = extra[pair_width + 5]
    cache_rows = cache_rows.reshape(-1, pair_width)

    return (
        layer_out,
        cache_rows,
        grad_tokens,
        extra[pair_width],
        extra[pair_width + 1],
        extra[pair_width + 2],
        extra[pair_width + 3],
        sum_query,
        sum_bias_query,
        keyval_weight_out,
        keyval_bias_out,
        sum_up,
        sum_bias_up,
        sum_output,
        bias_out_grad,
        sum_down,
        bias_out_grad,
    )


def solution(mesh):
    in_specs = (
        P(("seq", "row"), None),
        P(("seq", "row"), "col"),
        P(),
        P(),
        P("col"),
        P("col"),
        P("col"),
        P("col"),
        P("col", "row"),
        P("row"),
        P("col", None),
        P(),
        P("col", "row"),
        P("row"),
        P("row", "col"),
        P("col"),
        P("row", "col"),
        P("col"),
    )
    out_specs = (
        P(("seq", "row"), "col"),
        P(("seq", "col"), None),
        P(("seq", "row"), "col"),
        P("col"),
        P("col"),
        P("col"),
        P("col"),
        P("col", "row"),
        P("row"),
        P("col", "row"),
        P("row"),
        P("col", "row"),
        P("row"),
        P("row", "col"),
        P("col"),
        P("row", "col"),
        P("col"),
    )
    return jax.shard_map(
        on_device, mesh=mesh, in_specs=in_specs, out_specs=out_specs, check_vma=False
    )
```

```python
import collections
import functools

import jax
import jax.numpy as jnp
from jax import lax
from jax.experimental import pallas as pl
from jax.experimental.pallas import tpu as pltpu
from jax.sharding import PartitionSpec as P

HD = 64
ROT = 16
BLOCK = 512
LONGEST = 16
VMEM = 60 * 1024 * 1024
Shape = collections.namedtuple("Shape", "seq_count row_count sequences heads")
HALF = 256
EPS = 1e-05
NEGATIVE = -1e30
F32 = jnp.float32
BF16 = jnp.bfloat16

NN = (((1,), (0,)), ((), ()))
NT = (((1,), (1,)), ((), ()))
TN = (((0,), (0,)), ((), ()))


def dot(left, right, dims=NN):
    return lax.dot_general(left, right, dims, preferred_element_type=F32)


def swap(value, axis, bit):
    count = lax.axis_size(axis)
    return lax.ppermute(value, axis, [(i, i ^ bit) for i in range(count)])


def swap_odd_rows(value):
    seq_count, row_count = lax.axis_size("seq"), lax.axis_size("row")
    pairs = []
    for s in range(1, seq_count, 2):
        for r in range(row_count):
            pairs.append((s * row_count + r, s * row_count + (r ^ 2)))
    moved = lax.ppermute(value, ("seq", "row"), pairs)
    return jnp.where(lax.rem(lax.axis_index("seq"), 2) == 0, value, moved)


def fetch_quarter(value):
    seq_count, row_count = lax.axis_size("seq"), lax.axis_size("row")
    seq_me = lax.axis_index("seq")
    odd = range(1, seq_count, 2)
    over_z = [(s * row_count + r, s * row_count + (r ^ 2)) for s in odd for r in range(row_count)]
    over_x = [(s, s ^ 2) for s in odd]
    side = lax.rem(seq_me // 2, 2)
    half = value.shape[0] // 2
    got = lax.ppermute(lax.dynamic_slice_in_dim(value, side * half, half, 0), ("seq", "row"), over_z)
    other = lax.ppermute(got, "seq", over_x)
    low = jnp.where(side == 0, got, other)
    high = jnp.where(side == 0, other, got)
    moved = jnp.concatenate([low, high], axis=0)
    return jnp.where(lax.rem(seq_me, 2) == 0, value, moved)


def swap_add(value, axis, bit):
    rounded = lax.reduce_precision(value, 8, 7)
    return rounded + swap(rounded.astype(BF16), axis, bit).astype(F32)


def split_rows(vector):
    high = lax.reduce_precision(vector, 8, 7)
    return high.astype(BF16), (vector - high).astype(BF16)


def first_of(meta_ref, block, shape):
    start = jnp.int32(0)
    first = jnp.int32(0)
    for i in range(shape.sequences):
        first = jnp.where(start <= block, start, first)
        start = start + meta_ref[3 + i] // BLOCK
    return first


def attention_kernel(
    meta_ref,
    first_ref,
    dy_ref,
    cos_ref,
    sin_ref,
    ff_out_ref,
    ff_grad_ref,
    vec_ref,
    small0_ref,
    small1_ref,
    kv0_ref,
    kv1_ref,
    *rest,
    shape,
    second,
):
    heads = shape.heads
    rest = list(rest)
    if second:
        stats_ref, dqw_in_ref, dow_in_ref, dqb_in_ref, dkv_in_ref = rest[:5]
        rest = rest[5:]
        stay_ref, go_ref, keep_ref, send_ref, stat_ref, dkv_out_ref, last_ref = rest[:7]
        dqw_ref, dow_ref, dqb_ref = rest[7:10]
        rest = rest[10:]
    else:
        stay_ref, go_ref, dqw_ref, dow_ref, dqb_ref, dkv_out_ref, last_ref = rest[:7]
        rest = rest[7:]
    (
    qd_ref,
        probs_ref,
        high_ref,
        sums_ref,
        dots_ref,
        acc_ref,
        dq_ref,
        dkv_ref,
        kv_ref,
        low_ref,
        qw_ref,
        ow_ref,
        copy_sem,
        late_sem,
    ) = rest
    blocks = kv_ref.shape[0]
    half = blocks // 2
    slot = pl.program_id(0)
    lanes = 2 * HD
    rows = heads * HALF
    seq, row, second_half = meta_ref[0], meta_ref[1], meta_ref[2]
    own_block = lax.bitwise_xor(seq, slot) * shape.row_count + lax.bitwise_xor(
        row, 1 - slot if second else slot
    )
    first_block = first_of(meta_ref, own_block, shape)
    before = own_block - first_block

    def slot_of(block):
        apart_row = lax.bitwise_xor(lax.rem(block, shape.row_count), row)
        apart_seq = lax.bitwise_xor(block // shape.row_count, seq)
        return apart_row + shape.row_count * (
            apart_seq // 2 + (shape.seq_count // 2) * lax.rem(apart_seq, 2)
        )

    def put(index, rows):
        @pl.when(slot == 0)
        def _():
            stay_ref[index] = rows

        @pl.when(slot == 1)
        def _():
            go_ref[index] = rows.astype(BF16)

    pieces = [
        pltpu.make_async_copy(piece, kv_ref.at[i * half : (i + 1) * half], copy_sem.at[i])
        for i, piece in enumerate((kv0_ref, kv1_ref))
    ]
    if second:
        late = [
            pltpu.make_async_copy(source, target, late_sem.at[i])
            for i, (source, target) in enumerate(
                (
                    (dkv_in_ref, dkv_ref),
                    (dqw_in_ref, dqw_ref),
                    (dow_in_ref, dow_ref),
                    (dqb_in_ref, dqb_ref),
                )
            )
        ]
    else:
        late = [
            pltpu.make_async_copy(low_ref, dkv_ref.at[i : i + 1], late_sem.at[i]) for i in range(blocks)
        ]

    @pl.when(slot == 0)
    def _():
        for copy in pieces:
            copy.start()
        if not second:
            low_ref[...] = jnp.zeros_like(low_ref)
            dqw_ref[...] = jnp.zeros_like(dqw_ref)
            dow_ref[...] = jnp.zeros_like(dow_ref)
            dqb_ref[...] = jnp.zeros_like(dqb_ref)
        for copy in late:
            copy.start()
        span = small0_ref.shape[1]
        count = heads * HD
        for i, small in enumerate((small0_ref, small1_ref)):
            part = slice(i * span, (i + 1) * span)
            qw_ref[:count, part] = small[:count, :]
            ow_ref[:count, part] = small[count : 2 * count, :]
        qw_ref[count:, :] = jnp.zeros_like(qw_ref[count:, :])
        ow_ref[count:, :] = jnp.zeros_like(ow_ref[count:, :])

    cosine = cos_ref[0]
    sine = sin_ref[0]
    lane = lax.broadcasted_iota(jnp.int32, (HALF, lanes), 1)
    front = lane < HD

    def rolled(values):
        return jnp.where(
            lane < ROT // 2,
            pltpu.roll(values, lanes - ROT // 2, 1),
            pltpu.roll(values, ROT // 2, 1),
        )

    def head_of(joined, h):
        return joined[:, (h // 2) * lanes : (h // 2 + 1) * lanes]

    def join(parts):
        tiles = []
        for h in range(0, heads, 2):
            other = parts[h + 1] if h + 1 < heads else jnp.zeros_like(parts[h])
            tiles.append(jnp.where(front, parts[h], other))
        return jnp.concatenate(tiles, axis=1)

    padded = qw_ref.shape[0]
    base = 2 * heads * HD + 7
    query_b = (
        small0_ref[base : base + 1, :padded].astype(F32)
        + small0_ref[base + 8 : base + 9, :padded].astype(F32)
    )
    pre_all = dot(first_ref[0], qw_ref[...], NT) + query_b
    d_all = dot(dy_ref[0], ow_ref[...], NT)
    for h in range(heads):
        pre = head_of(pre_all, h)
        grad = head_of(d_all, h)
        if h % 2:
            pre = pltpu.roll(pre, HD, 1)
        else:
            grad = pltpu.roll(grad, HD, 1)
        turned = jnp.where(front, pre * cosine + rolled(pre) * sine, 0.0)
        mine = slice(h * HALF, (h + 1) * HALF)
        qd_ref[mine, :] = turned.astype(BF16) * BF16(HD**-0.5)
        qd_ref[rows + h * HALF : rows + (h + 1) * HALF, :] = jnp.where(front, 0.0, grad).astype(BF16)

    @pl.when(slot == 0)
    def _():
        for copy in pieces:
            copy.wait()

    high_ref[...] = jnp.full_like(high_ref, NEGATIVE)
    sums_ref[...] = jnp.zeros_like(sums_ref)

    def block_at(step):
        return slot_of(first_block + step)

    def weigh(step, mask):
        scores = dot(kv_ref[block_at(step)], qd_ref[:rows, :], NT)
        if mask:
            row_in = lax.rem(lax.broadcasted_iota(jnp.int32, (BLOCK, rows), 1), HALF)
            key_in = lax.broadcasted_iota(jnp.int32, (BLOCK, rows), 0)
            limit = jnp.where(second_half > 0, BLOCK, 0)
            keep = (key_in <= row_in) | ((key_in >= HALF) & (key_in < limit))
            scores = jnp.where(keep, scores, NEGATIVE)
        high = jnp.max(scores, axis=0, keepdims=True)
        probs = jnp.exp(scores - high)
        probs_ref[step] = probs.astype(BF16)
        high_ref[pl.ds(step, 1), :] = high
        sums_ref[pl.ds(step, 1), :] = jnp.sum(probs, axis=0, keepdims=True)

    weigh(before, True)
    lax.fori_loop(0, before, lambda step, c: (weigh(step, False), c)[1], 0)

    share = jnp.exp(high_ref[...] - jnp.max(high_ref[...], axis=0, keepdims=True))
    high_ref[...] = share / jnp.sum(share * sums_ref[...], axis=0, keepdims=True)

    def mix(step, first):
        probs = (probs_ref[step].astype(F32) * high_ref[pl.ds(step, 1), :]).astype(BF16)
        probs_ref[step] = probs
        part = dot(probs, kv_ref[block_at(step)], TN)
        if first:
            acc_ref[...] = part
        else:
            acc_ref[...] += part

    mix(before, True)
    lax.fori_loop(0, before, lambda step, c: (mix(step, False), c)[1], 0)

    @pl.when(slot == 0)
    def _():
        for copy in late:
            copy.wait()

    parts = []
    for h in range(heads):
        mine = slice(h * HALF, (h + 1) * HALF)
        mixed = acc_ref[mine, :]
        grad = qd_ref[rows + h * HALF : rows + (h + 1) * HALF, :].astype(F32)
        dots_ref[:, mine] = jnp.sum(jnp.transpose(mixed * grad), axis=0, keepdims=True)
        parts.append(mixed if h % 2 else pltpu.roll(mixed, HD, 1))
    joined = join(parts).astype(BF16)
    put(0, ff_out_ref[0] + dot(joined, ow_ref[...]))
    dow_ref[...] += dot(joined, dy_ref[0], TN)

    def backward(step, first):
        where = block_at(step)
        block = kv_ref[where]
        probs = probs_ref[step]
        grad_probs = dot(block, qd_ref[rows:, :], NT)
        grad_scores = (probs.astype(F32) * (grad_probs - dots_ref[...])).astype(BF16)
        total = dot(jnp.concatenate([grad_scores, probs], axis=1), qd_ref[...])
        grad_q = dot(grad_scores, block, TN)
        if first:
            dq_ref[...] = grad_q
        else:
            dq_ref[...] += grad_q
        dkv_ref[where] = (dkv_ref[where].astype(F32) + total).astype(dkv_ref.dtype)

    backward(before, True)
    lax.fori_loop(0, before, lambda step, c: (backward(step, False), c)[1], 0)

    parts = []
    for h in range(heads):
        part = dq_ref[h * HALF : (h + 1) * HALF, :] * (HD**-0.5)
        part = part * cosine - rolled(part) * sine
        parts.append(pltpu.roll(part, HD, 1) if h % 2 else part)
    joined = join(parts)
    dqb_ref[...] += jnp.sum(joined, axis=0, keepdims=True)
    joined = joined.astype(BF16)
    put(1, ff_grad_ref[0] + dot(joined, qw_ref[...]) * vec_ref[0:1, :])
    dqw_ref[...] += dot(joined, first_ref[0], TN)

    @pl.when(slot == 1)
    def _():
        if not second:
            copies = [pltpu.make_async_copy(dkv_ref, dkv_out_ref, copy_sem.at[0])]
            dealt = last_ref.shape[0]
            group = seq * 2 + second_half
            for i in range(dealt):
                owner = meta_ref[3 + shape.sequences + group * dealt + i]
                for part in (0, 1):
                    take = jnp.where(second_half > 0, 1 - part, part) * HALF
                    copies.append(
                        pltpu.make_async_copy(
                            kv_ref.at[slot_of(owner), pl.ds(take, HALF), :],
                            last_ref.at[i, part * HALF : (part + 1) * HALF, :],
                            copy_sem.at[1 + 2 * i + part],
                        )
                    )
            for copy in copies:
                copy.start()
        else:
            copies = [pltpu.make_async_copy(dkv_ref.at[:half], dkv_out_ref, copy_sem.at[0])]
            copies[0].start()
            if dkv_ref.dtype == BF16:
                copies.append(pltpu.make_async_copy(dkv_ref.at[half:], last_ref, copy_sem.at[1]))
            else:
                low_ref[...] = dkv_ref[half:].astype(BF16)
                copies.append(pltpu.make_async_copy(low_ref, last_ref, copy_sem.at[1]))
            copies[1].start()
            count = heads * HD
            span = small0_ref.shape[1]
            bias_up = stats_ref[2:3, :]
            bias_q = dqb_ref[...]
            for i, target in enumerate((keep_ref, send_ref)):
                part = slice(i * span, (i + 1) * span)
                target[:count, :] = dqw_ref[:count, part].astype(BF16)
                target[count : 2 * count, :] = dow_ref[:count, part].astype(BF16)
                rows_of = jnp.concatenate(
                    [
                        bias_up[:, :span],
                        bias_up[:, span:],
                        jnp.concatenate([bias_q, jnp.zeros((1, span - padded), F32)], axis=1),
                        jnp.zeros((5, span), F32),
                    ],
                    axis=0,
                )
                target[2 * count :, :] = jnp.concatenate(
                    [rows_of, jnp.zeros((target.shape[0] - 2 * count - 8, span), F32)], axis=0
                ).astype(BF16)
            weight = qw_ref[...].astype(F32)
            column = jnp.transpose(jnp.broadcast_to(bias_q, (8, padded)))[:, 0:1]
            plain = jnp.sum(weight * column, axis=0, keepdims=True)
            stat_ref[0:1, :] = (
                jnp.sum(weight * dqw_ref[...], axis=0, keepdims=True) - vec_ref[1:2, :] * plain
            ) / vec_ref[0:1, :]
            stat_ref[1:2, :] = plain
            stat_ref[2:8, :] = jnp.zeros((6, 2 * span), F32)
        for copy in copies:
            copy.wait()


def attention(meta, first_in, dy, cosine, sine, ff, vectors, small, pieces, so_far, shape):
    second = so_far is not None
    _, _, width = first_in.shape
    half = pieces[0].shape[0]
    blocks = 2 * half
    lanes = 2 * HD
    heads = shape.heads
    padded = -(-heads // 2) * lanes
    rows = heads * HALF
    longest = min(LONGEST, blocks // 2)
    total_type = F32 if blocks <= 32 else BF16
    dealt = blocks // (2 * shape.seq_count)
    offset = 2 if second else 0

    def per_slot(lanes):
        return pl.BlockSpec((1, HALF, lanes), lambda i, m: (i + offset, 0, 0))

    def whole(array):
        return pl.BlockSpec(
            array.shape, lambda i, m: (0,) * len(array.shape), pipeline_mode=pl.Buffered(buffer_count=1)
        )

    far = pl.BlockSpec(memory_space=pltpu.MemorySpace.HBM)
    arrays = [first_in, dy, cosine, sine, *ff, vectors, *small, *pieces]
    in_specs = [per_slot(width), per_slot(width), per_slot(lanes), per_slot(lanes)]
    in_specs += [per_slot(width)] * 2 + [whole(vectors)] + [whole(a) for a in small] + [far] * 2
    weight = jax.ShapeDtypeStruct((padded, width), F32)
    bias = jax.ShapeDtypeStruct((1, padded), F32)
    tokens = jax.ShapeDtypeStruct((2, HALF, width), F32)
    if second:
        arrays += list(so_far)
        in_specs += [whole(so_far[0])] + [far] * 4
        part = jax.ShapeDtypeStruct((2 * heads * HD + 32, width // 2), BF16)
        sums = [part, part, jax.ShapeDtypeStruct((8, width), F32)]
        kept = [pltpu.VMEM(a.shape, F32) for a in (weight, weight, bias)]
    else:
        sums = [weight, weight, bias]
        kept = []
    out_shape = [
        tokens,
        jax.ShapeDtypeStruct(tokens.shape, BF16),
        *sums,
        jax.ShapeDtypeStruct((half if second else blocks, BLOCK, lanes), total_type),
        jax.ShapeDtypeStruct((half if second else dealt, BLOCK, lanes), BF16),
    ]
    out_specs = [whole(tokens)] * 2 + [whole(a) for a in sums] + [far, far]
    low = BF16 if second else total_type
    return pl.pallas_call(
        functools.partial(attention_kernel, shape=shape, second=second),
        grid_spec=pltpu.PrefetchScalarGridSpec(
            num_scalar_prefetch=1,
            grid=(2,),
            in_specs=in_specs,
            out_specs=out_specs,
            scratch_shapes=kept
            + [
                pltpu.VMEM((2 * rows, lanes), BF16),
                pltpu.VMEM((longest, BLOCK, rows), BF16),
                pltpu.VMEM((longest, rows), F32),
                pltpu.VMEM((longest, rows), F32),
                pltpu.VMEM((1, rows), F32),
                pltpu.VMEM((rows, lanes), F32),
                pltpu.VMEM((rows, lanes), F32),
                pltpu.VMEM((blocks, BLOCK, lanes), total_type),
                pltpu.VMEM((blocks, BLOCK, lanes), BF16),
                pltpu.VMEM((half if second and blocks <= 32 else 1, BLOCK, lanes), low),
                pltpu.VMEM((padded, width), BF16),
                pltpu.VMEM((padded, width), BF16),
                pltpu.SemaphoreType.DMA((2 + 2 * dealt,)),
                pltpu.SemaphoreType.DMA((4 if second else blocks,)),
            ],
        ),
        out_shape=out_shape,
        cost_estimate=pl.CostEstimate(
            flops=12_000_000_000, bytes_accessed=15_000_000, transcendentals=15_000_000
        ),
        compiler_params=pltpu.CompilerParams(
            vmem_limit_bytes=67_043_328 if blocks > 32 else VMEM
        ),
        name="attention",
    )(meta, *arrays)


ORDER = (0, 3, 1, 2)


def tables_kernel(meta_ref, cos_ref, sin_ref, *, shape):
    seq, row, col = meta_ref[0], meta_ref[1], meta_ref[2]
    lane = lax.broadcasted_iota(jnp.int32, (HALF, 2 * HD), 1)
    inside = lax.broadcasted_iota(jnp.int32, (HALF, 2 * HD), 0)
    half_rot = ROT // 2
    exponent = lax.rem(lane, half_rot).astype(F32) * (1.0 / half_rot)
    frequency = jnp.where(lane < ROT, 1.0 / jnp.exp(exponent * jnp.log(jnp.full_like(exponent, 10000.0))), 0.0)
    for i, (slot, half) in enumerate([(slot, col) for slot in ORDER] + [(0, 1 - col)]):
        block = lax.bitwise_xor(seq, slot // 2) * shape.row_count + lax.bitwise_xor(row, slot % 2)
        start = (block - first_of(meta_ref, block, shape)) * BLOCK
        angles = (inside + (start + half * HALF)).astype(F32) * frequency
        cos_ref[i] = jnp.cos(angles)
        turned = jnp.sin(angles)
        sin_ref[i] = jnp.where(lane < half_rot, -turned, jnp.where(lane < ROT, turned, 0.0))


def tables(meta, shape):
    table = jax.ShapeDtypeStruct((5, HALF, 2 * HD), F32)
    return pl.pallas_call(
        functools.partial(tables_kernel, shape=shape),
        in_specs=[pl.BlockSpec(memory_space=pltpu.SMEM)],
        out_specs=[pl.BlockSpec(memory_space=pltpu.VMEM)] * 2,
        out_shape=[table, table],
        name="tables",
    )(meta)


def forward_kernel(
    both0_ref,
    both3_ref,
    both1_ref,
    both2_ref,
    vec_ref,
    small_ref,
    up0_ref,
    up1_ref,
    down0_ref,
    down1_ref,
    first_ref,
    dy_ref,
    out_ref,
    dx_ref,
    keep_ref,
    send_ref,
    stat_ref,
    x_ref,
    up_ref,
    down_ref,
    second_ref,
    hidden_ref,
    grad_ref,
    dys_ref,
    bias_ref,
):
    step = pl.program_id(0)
    span = up0_ref.shape[0]
    here = pl.ds(pl.multiple_of(step * HALF, HALF), HALF)

    @pl.when(step == 0)
    def _():
        up_ref[:span, :] = up0_ref[...]
        up_ref[span:, :] = up1_ref[...]
        down_ref[:, :span] = down0_ref[...]
        down_ref[:, span:] = down1_ref[...]
        bias_ref[...] = jnp.zeros_like(bias_ref)

    for i, piece in enumerate((both0_ref, both3_ref, both1_ref, both2_ref)):

        @pl.when(step == i)
        def _():
            x_ref[...] = piece[0]
            dys_ref[here, :] = piece[1]

    base = small_ref.shape[0] - 16
    bias = small_ref[base : base + 8, :].astype(F32) + small_ref[base + 8 :, :].astype(F32)
    upward_b = jnp.concatenate([bias[5:6], bias[6:7]], axis=1)
    wide = x_ref[...].astype(F32)
    mean = jnp.mean(wide, axis=1, keepdims=True)
    spread = jnp.mean(wide * wide, axis=1, keepdims=True) - mean * mean
    normed = (wide - mean) * lax.rsqrt(spread + EPS)
    first_ref[0] = (normed * vec_ref[0:1, :] + vec_ref[1:2, :]).astype(BF16)
    second = (normed * vec_ref[2:3, :] + vec_ref[3:4, :]).astype(BF16)
    dy = dys_ref[here, :]
    dy_ref[0] = dy
    second_ref[here, :] = second
    upward = dot(second, up_ref[...]) + upward_b
    bell = lax.erf(upward * (2.0**-0.5)) * 0.5 + 0.5
    hidden = (upward * bell).astype(BF16)
    slope = bell + upward * jnp.exp(upward * upward * -0.5) * ((2.0 * 3.141592653589793) ** -0.5)
    grad = dot(dy, down_ref[...], NT) * slope
    bias_ref[0:1, :] += jnp.sum(grad, axis=0, keepdims=True)
    grad = grad.astype(BF16)
    hidden_ref[here, :] = hidden
    grad_ref[here, :] = grad
    out_ref[0] = dot(hidden, down_ref[...])
    dx_ref[0] = dot(grad, up_ref[...], NT) * vec_ref[2:3, :]

    @pl.when(step == 3)
    def _():
        down_grad = dot(hidden_ref[...], dys_ref[...], TN)
        keep_ref[2 * span :, :] = down_grad[:, :span].astype(BF16)
        send_ref[2 * span :, :] = down_grad[:, span:].astype(BF16)
        up_grad = dot(second_ref[...], grad_ref[...], TN)
        for i in (0, 1):
            part = slice(i * span, (i + 1) * span)
            keep_ref[part, :] = up_grad[:span, part].astype(BF16)
            send_ref[part, :] = up_grad[span:, part].astype(BF16)
        weight = up_ref[...].astype(F32)
        bias_grad = bias_ref[0:1, :]

        def as_row(values):
            column = jnp.sum(values, axis=1, keepdims=True)
            return jnp.transpose(jnp.broadcast_to(column, (2 * span, 128)))[0:1, :]

        plain = as_row(weight * bias_grad)
        stat_ref[0:1, :] = (as_row(weight * up_grad) - vec_ref[3:4, :] * plain) / vec_ref[2:3, :]
        stat_ref[1:2, :] = plain
        stat_ref[2:3, :] = bias_grad
        stat_ref[3:8, :] = jnp.zeros((5, 2 * span), F32)


def feed_forward(both, vectors, small, up, down):
    width = vectors.shape[1]
    span = width // 2
    hidden = up[0].shape[1]

    def whole(array):
        return pl.BlockSpec(
            array.shape, lambda i: (0,) * len(array.shape), pipeline_mode=pl.Buffered(buffer_count=1)
        )

    slot = pl.BlockSpec((1, HALF, width), lambda i: (i, 0, 0))
    arrays = [*both, vectors, small, *up, *down]
    half = jax.ShapeDtypeStruct((2 * span + hidden, span), BF16)
    stat = jax.ShapeDtypeStruct((8, width), F32)
    tokens = lambda kind: jax.ShapeDtypeStruct((4, HALF, width), kind)
    return pl.pallas_call(
        forward_kernel,
        grid=(4,),
        in_specs=[whole(a) for a in arrays],
        out_specs=[slot] * 4 + [whole(half), whole(half), whole(stat)],
        out_shape=[tokens(BF16), tokens(BF16), tokens(F32), tokens(F32), half, half, stat],
        scratch_shapes=[
            pltpu.VMEM((HALF, width), BF16),
            pltpu.VMEM((width, hidden), BF16),
            pltpu.VMEM((hidden, width), BF16),
            pltpu.VMEM((4 * HALF, width), BF16),
            pltpu.VMEM((4 * HALF, hidden), BF16),
            pltpu.VMEM((4 * HALF, hidden), BF16),
            pltpu.VMEM((4 * HALF, width), BF16),
            pltpu.VMEM((8, hidden), F32),
        ],
        cost_estimate=pl.CostEstimate(
            flops=7_000_000_000, bytes_accessed=20_000_000, transcendentals=3_000_000
        ),
        compiler_params=pltpu.CompilerParams(vmem_limit_bytes=VMEM),
        name="feed_forward",
    )(*arrays)


def prologue_kernel(
    where_ref, tokens_ref, dy_ref, kvw_ref, qw_ref, ow_ref, vec_ref, pack_ref, x_ref, mine_ref, small_ref
):
    col = where_ref[2]
    span = dy_ref.shape[1]
    width = tokens_ref.shape[1]
    here = pl.ds(pl.multiple_of(col * HALF, HALF), HALF)
    there = pl.ds(pl.multiple_of((1 - col) * HALF, HALF), HALF)
    pack_ref[:HALF, :] = dy_ref[there, :]
    base = HALF + 2 * HD
    pack_ref[HALF:base, :] = jnp.transpose(kvw_ref[...].astype(F32)).astype(BF16)
    vectors = vec_ref[...]
    high = vectors.astype(BF16).astype(F32)
    both = jnp.concatenate([high, vectors - high], axis=0).astype(BF16)
    pack_ref[base:, :] = both
    for i, rows in enumerate((here, there)):
        part = slice(i * HALF, (i + 1) * HALF)
        x_ref[part, :span] = tokens_ref[rows, pl.ds(pl.multiple_of(col * span, 128), span)]
        x_ref[part, span:] = tokens_ref[rows, pl.ds(pl.multiple_of((1 - col) * span, 128), span)]
    mine_ref[...] = dy_ref[here, :]
    count = qw_ref.shape[0]
    small_ref[:count, :] = qw_ref[...]
    small_ref[count : 2 * count, :] = ow_ref[...]
    small_ref[2 * count :, :] = both


def prologue(col, tokens, cotangent, keyval_weight, query_weight, output_weight, vectors):
    width = tokens.shape[1]
    span = width // 2
    rows = vectors.shape[0]
    count = query_weight.shape[0]
    vmem = pl.BlockSpec(memory_space=pltpu.VMEM)
    return pl.pallas_call(
        prologue_kernel,
        in_specs=[pl.BlockSpec(memory_space=pltpu.SMEM)] + [vmem] * 6,
        out_specs=[vmem] * 4,
        out_shape=[
            jax.ShapeDtypeStruct((HALF + 2 * HD + 2 * rows, span), BF16),
            jax.ShapeDtypeStruct((2 * HALF, width), BF16),
            jax.ShapeDtypeStruct((HALF, span), BF16),
            jax.ShapeDtypeStruct((2 * count + 2 * rows, span), BF16),
        ],
        name="prologue",
    )(col, tokens, cotangent, keyval_weight, query_weight, output_weight, vectors)


def own_kernel(
    x_ref, mine_ref, pack_ref, got_ref, vec_ref, cos_ref, sin_ref, bias_ref, pair_ref, both_ref, kvw_ref, full_ref
):
    span = mine_ref.shape[1]
    rows = vec_ref.shape[0]
    base = HALF + 2 * HD
    other = got_ref[base : base + 2 * rows, :].astype(F32)
    full = jnp.concatenate([vec_ref[...], other[:rows] + other[rows:]], axis=1)
    full_ref[...] = full
    both_ref[0] = x_ref[:HALF, :]
    both_ref[1, :, :span] = mine_ref[...]
    both_ref[1, :, span:] = got_ref[:HALF, :]
    kvw_ref[:, :span] = pack_ref[HALF:base, :]
    kvw_ref[:, span:] = got_ref[HALF:base, :]
    wide = x_ref[...].astype(F32)
    mean = jnp.mean(wide, axis=1, keepdims=True)
    spread = jnp.mean(wide * wide, axis=1, keepdims=True) - mean * mean
    normed = (wide - mean) * lax.rsqrt(spread + EPS)
    first = (normed * full[0:1, :] + full[1:2, :]).astype(BF16)
    pre_all = dot(first, kvw_ref[...], NT) + bias_ref[...]
    lanes = pre_all.shape[1]
    lane = lax.broadcasted_iota(jnp.int32, (HALF, lanes), 1)
    for i in (0, 1):
        pre = pre_all[i * HALF : (i + 1) * HALF, :]
        rolled = jnp.where(
            lane < ROT // 2, pltpu.roll(pre, lanes - ROT // 2, 1), pltpu.roll(pre, ROT // 2, 1)
        )
        pair_ref[0, i * HALF : (i + 1) * HALF, :] = (
            pre * cos_ref[4 * i] + rolled * sin_ref[4 * i]
        ).astype(BF16)


def own_pairs(x_own, mine, pack, got, vectors, cosine, sine, bias):
    width = x_own.shape[1]
    vmem = pl.BlockSpec(memory_space=pltpu.VMEM)
    return pl.pallas_call(
        own_kernel,
        in_specs=[vmem] * 8,
        out_specs=[vmem] * 4,
        out_shape=[
            jax.ShapeDtypeStruct((1, 2 * HALF, 2 * HD), BF16),
            jax.ShapeDtypeStruct((2, HALF, width), BF16),
            jax.ShapeDtypeStruct((2 * HD, width), BF16),
            jax.ShapeDtypeStruct((vectors.shape[0], width), F32),
        ],
        name="own_pairs",
    )(x_own, mine, pack, got, vectors, cosine, sine, bias)


def pairs_kernel(
    keep_ref, got_ref, cos_ref, sin_ref, first_ref, kvw_ref, vec_ref, stat_ref, ff_ref, dys_ref, mine_ref, send_ref
):
    span = mine_ref.shape[1]
    lanes = 2 * HD
    lane = lax.broadcasted_iota(jnp.int32, (HALF, lanes), 1)
    total = keep_ref[...] + got_ref[...].astype(F32)
    weight = jnp.zeros((lanes, 2 * span), F32)
    bias = jnp.zeros((1, lanes), F32)
    for i in (0, 1):
        part = total[i]
        rolled = jnp.where(
            lane < ROT // 2, pltpu.roll(part, lanes - ROT // 2, 1), pltpu.roll(part, ROT // 2, 1)
        )
        turned = part * cos_ref[2 * i] - rolled * sin_ref[2 * i]
        bias = bias + jnp.sum(turned, axis=0, keepdims=True)
        weight = weight + dot(turned.astype(BF16), first_ref[2 * i], TN)
    kvw = kvw_ref[...].astype(F32)
    column = jnp.transpose(jnp.broadcast_to(bias, (8, lanes)))[:, 0:1]
    plain = jnp.sum(kvw * column, axis=0, keepdims=True)
    gain = (jnp.sum(kvw * weight, axis=0, keepdims=True) - vec_ref[1:2, :] * plain) / vec_ref[0:1, :]
    fill = jnp.zeros((1, span - lanes), F32)
    bias = jnp.concatenate([bias.astype(BF16).astype(F32), fill], axis=1)
    for i, target in enumerate((mine_ref, send_ref)):
        part = slice(i * span, (i + 1) * span)
        target[:lanes, :] = weight[:, part].astype(target.dtype)
        rows = jnp.concatenate(
            [
                stat_ref[0:1, part] + gain[:, part],
                stat_ref[1:2, part] + plain[:, part],
                ff_ref[0:2, part],
                bias,
                dys_ref[...] if i == 0 else jnp.zeros((1, span), F32),
                jnp.zeros((10, span), F32),
            ],
            axis=0,
        )
        target[lanes:, :] = rows.astype(target.dtype)


def pair_sums(keep, got, cosine, sine, first_in, keyval, vectors, stats, ff_stats, dy_sum):
    width = keyval.shape[1]
    vmem = pl.BlockSpec(memory_space=pltpu.VMEM)
    return pl.pallas_call(
        pairs_kernel,
        in_specs=[vmem] * 10,
        out_specs=[vmem] * 2,
        out_shape=[
            jax.ShapeDtypeStruct((2 * HD + 16, width // 2), F32),
            jax.ShapeDtypeStruct((2 * HD + 16, width // 2), BF16),
        ],
        name="pair_sums",
    )(keep, got, cosine, sine, first_in, keyval, vectors, stats, ff_stats, dy_sum)


def rows_kernel(
    own_ref,
    got_ref,
    cos_ref,
    sin_ref,
    kvw_ref,
    vec_ref,
    x_ref,
    dy_ref,
    keep_ref,
    core_ref,
    back_ref,
    mine_ref,
    send_ref,
):
    span = mine_ref.shape[2]
    lanes = 2 * HD
    lane = lax.broadcasted_iota(jnp.int32, (HALF, lanes), 1)
    part = own_ref[0] + got_ref[...].astype(F32)
    rolled = jnp.where(
        lane < ROT // 2, pltpu.roll(part, lanes - ROT // 2, 1), pltpu.roll(part, ROT // 2, 1)
    )
    turned = (part * cos_ref[0] - rolled * sin_ref[0]).astype(BF16)
    wide = x_ref[:HALF, :].astype(F32)
    mean = jnp.mean(wide, axis=1, keepdims=True)
    spread = jnp.mean(wide * wide, axis=1, keepdims=True) - mean * mean
    root = lax.rsqrt(spread + EPS)
    normed = (wide - mean) * root
    grad = keep_ref[1] + core_ref[1].astype(F32) + back_ref[1].astype(F32) + dot(turned, kvw_ref[...]) * vec_ref[0:1, :]
    one = jnp.mean(grad, axis=1, keepdims=True)
    two = jnp.mean(grad * normed, axis=1, keepdims=True)
    grad = dy_ref[0].astype(F32) + root * (grad - one - normed * two)
    out = wide + keep_ref[0] + core_ref[0].astype(F32) + back_ref[0].astype(F32) + vec_ref[4:5, :]
    for i, rows in enumerate((out.astype(BF16), grad.astype(BF16))):
        mine_ref[i] = rows[:, :span]
        send_ref[i] = rows[:, span:]


def own_rows(own, got, cosine, sine, keyval, vectors, x_block, dy, keep, core, back):
    width = keyval.shape[1]
    vmem = pl.BlockSpec(memory_space=pltpu.VMEM)
    half = jax.ShapeDtypeStruct((2, HALF, width // 2), BF16)
    return pl.pallas_call(
        rows_kernel,
        in_specs=[vmem] * 11,
        out_specs=[vmem] * 2,
        out_shape=[half, half],
        name="own_rows",
    )(own, got, cosine, sine, keyval, vectors, x_block, dy, keep, core, back)


def after(value, *others):
    return lax.optimization_barrier((value,) + others)[0]


def on_device(
    tokens,
    cotangent,
    lengths,
    block_order,
    attention_gain,
    attention_shift,
    feedforward_gain,
    feedforward_shift,
    query_weight,
    query_bias,
    keyval_weight,
    keyval_bias,
    upward_weight,
    upward_bias,
    output_weight,
    output_bias,
    down_weight,
    down_bias,
):
    seq_count = lax.axis_size("seq")
    row_count = lax.axis_size("row")
    col_count = lax.axis_size("col")
    seq_me = lax.axis_index("seq")
    row_me = lax.axis_index("row")
    col_me = lax.axis_index("col")
    block_total = block_order.shape[0]
    width = tokens.shape[1]
    span = width // 2
    heads = query_weight.shape[1] // HD
    head_width = heads * HD
    pair_width = 2 * HD

    shape = Shape(seq_count, row_count, lengths.shape[0], heads)
    meta = jnp.concatenate(
        [jnp.stack([seq_me, row_me, col_me]).astype(jnp.int32), lengths, block_order]
    )

    vectors = jnp.concatenate(
        [
            attention_gain,
            attention_shift,
            feedforward_gain,
            feedforward_shift,
            output_bias + down_bias,
            upward_bias,
            query_bias,
            jnp.zeros((span - head_width,), F32),
        ]
    ).reshape(8, span)
    pack, x_block, dy_mine, small = prologue(
        meta, tokens, cotangent, keyval_weight, jnp.transpose(query_weight), output_weight, vectors
    )
    received = swap(pack, "col", 1)
    cosine, sine = tables(after(meta, pack), shape)

    small_own = swap_odd_rows(small)
    up_own = fetch_quarter(upward_weight)
    pairs, both, keyval_full, vec_full = own_pairs(
        x_block, dy_mine, pack, received, vectors, cosine, sine, keyval_bias[None]
    )
    steps = [("row", 1), ("row", 2)]
    bit = 2
    while bit < seq_count:
        steps.append(("seq", bit))
        bit = bit * 2
    small_full = (small_own, swap(small_own, "col", 1))
    for i, (axis, bit) in enumerate(steps):
        got = swap(pairs, axis, bit)
        if i == 0:
            both_got = swap(after(both, got), "row", 1)
            down_own = fetch_quarter(after(down_weight, got))
        pairs = jnp.concatenate([pairs, got], axis=0)
    pieces = (pairs, swap(pairs, "seq", 1))
    up_full = (up_own, swap(up_own, "col", 1))

    first_in, dy_all, ff_out, ff_grad, ff_keep, ff_send, ff_stats = feed_forward(
        (both, swap(both_got, "seq", 1), both_got, swap(both, "seq", 1)),
        after(vec_full, got, small_full[1]),
        small_own,
        up_full,
        (down_own, swap(down_own, "col", 1)),
    )

    ff_got = swap(ff_send, "col", 1)
    ff = (ff_out, ff_grad)
    stay_a, go_a, dquery_w, doutput_w, dquery_b, dpairs, cache_rows = attention(
        after(meta, ff_send), first_in, dy_all, cosine, sine, ff, vec_full, small_full, pieces, None, shape
    )
    ff_sum = (after(ff_keep, go_a).astype(F32) + ff_got.astype(F32)).astype(BF16)
    ff_moved = swap_odd_rows(ff_sum)
    core_a = swap(go_a, "seq", 1)
    stay_b, go_b, small_keep, small_send, stats, keep_pairs, send_pairs = attention(
        after(meta, ff_sum),
        first_in,
        dy_all,
        cosine,
        sine,
        ff,
        vec_full,
        small_full,
        pieces,
        (ff_stats, dquery_w, doutput_w, dquery_b, dpairs),
        shape,
    )

    send_pairs = after(send_pairs, ff_moved, core_a)
    got = swap(send_pairs, "seq", 1)
    col_send = (keep_pairs[:, HALF:].astype(F32) + got[:, HALF:].astype(F32)).astype(BF16)
    col_got = swap(col_send, "col", 1)
    away = (stay_b + core_a.astype(F32)).astype(BF16)
    back = swap(after(away, got), "row", 1)
    core_b = swap(after(go_b, col_send), "seq", 1)
    core = lax.rem(seq_me, 2)

    def core_halves(moved):
        half = moved.shape[0] // 2
        keep = lax.dynamic_slice_in_dim(moved, core * half, half, 0)
        return keep, lax.dynamic_slice_in_dim(moved, (1 - core) * half, half, 0)

    def over_seq(value):
        bit = 2
        while bit < seq_count:
            value = swap_add(value, "seq", bit)
            bit = bit * 2
        return value.astype(BF16)

    def both_halves(value):
        other = swap(value, "seq", 1)
        first = jnp.where(core == 0, value, other)
        second = jnp.where(core == 0, other, value)
        return jnp.concatenate([first, second], axis=0).astype(F32)

    ff_keep, ff_away = core_halves(after(ff_moved, col_send))
    ff_part = over_seq(ff_keep.astype(F32) + swap(ff_away, "seq", 1).astype(F32))
    total = keep_pairs[:, :HALF].astype(F32) + got[:, :HALF].astype(F32) + col_got.astype(F32)
    small_got = swap(after(small_send, total), "col", 1)
    small_sum = (small_keep.astype(F32) + small_got.astype(F32)).astype(BF16)
    for axis, bit in reversed(steps[2:]):
        half = total.shape[0] // 2
        total = total[:half] + swap(total[half:].astype(BF16), axis, bit).astype(F32)
    row_got = swap(total[2:].astype(BF16), "row", 2)
    small_moved = swap_odd_rows(after(small_sum, total))
    keep_two = total[:2]
    dy_sum = jnp.sum(cotangent.astype(F32), axis=0)[None]
    z_send = (keep_two[1] + row_got[1].astype(F32)).astype(BF16)
    z_got = swap(z_send, "row", 1)
    extra_mine, extra_send = pair_sums(
        keep_two, row_got, cosine, sine, first_in, keyval_full, vec_full, stats, ff_stats, dy_sum
    )
    extra = extra_mine + swap(extra_send, "col", 1).astype(F32)
    own_total = (keep_two[0] + row_got[0].astype(F32))[None]
    mine, away_rows = own_rows(
        own_total, z_got, cosine, sine, keyval_full, vec_full, x_block, dy_all, stay_a, core_b, back
    )
    other = swap(away_rows, "col", 1)
    first = jnp.where(col_me == 0, mine, other)
    second = jnp.where(col_me == 0, other, mine)
    layer_out = jnp.concatenate([first[0], second[0]], axis=0)
    grad_tokens = jnp.concatenate([first[1], second[1]], axis=0)

    sum_ff = both_halves(ff_part)
    sum_up = jnp.concatenate([sum_ff[:span], sum_ff[span : 2 * span]], axis=1)
    sum_down = sum_ff[2 * span :]
    keep, send = core_halves(small_moved)
    sum_small = both_halves(over_seq(keep.astype(F32) + swap(send, "seq", 1).astype(F32)))
    sum_query = jnp.transpose(sum_small[:head_width])
    sum_output = sum_small[head_width : 2 * head_width]
    base = 2 * head_width
    sum_bias_up = sum_small[base : base + 2].reshape(-1)
    sum_bias_query = sum_small[base + 2, :head_width]

    bit = 1
    while bit < seq_count:
        extra = swap_add(extra, "seq", bit)
        bit = bit * 2
    for bit in (1, 2):
        extra = swap_add(extra, "row", bit)
    part = pair_width // row_count
    keyval_weight_out = jnp.transpose(lax.dynamic_slice_in_dim(extra, row_me * part, part, 0))
    keyval_bias_out = lax.dynamic_slice_in_dim(extra[pair_width + 4], row_me * part, part, 0)
    bias_out_grad = extra[pair_width + 5]
    cache_rows = cache_rows.reshape(-1, pair_width)

    return (
        layer_out,
        cache_rows,
        grad_tokens,
        extra[pair_width],
        extra[pair_width + 1],
        extra[pair_width + 2],
        extra[pair_width + 3],
        sum_query,
        sum_bias_query,
        keyval_weight_out,
        keyval_bias_out,
        sum_up,
        sum_bias_up,
        sum_output,
        bias_out_grad,
        sum_down,
        bias_out_grad,
    )


def solution(mesh):
    in_specs = (
        P(("seq", "row"), None),
        P(("seq", "row"), "col"),
        P(),
        P(),
        P("col"),
        P("col"),
        P("col"),
        P("col"),
        P("col", "row"),
        P("row"),
        P("col", None),
        P(),
        P("col", "row"),
        P("row"),
        P("row", "col"),
        P("col"),
        P("row", "col"),
        P("col"),
    )
    out_specs = (
        P(("seq", "row"), "col"),
        P(("seq", "col"), None),
        P(("seq", "row"), "col"),
        P("col"),
        P("col"),
        P("col"),
        P("col"),
        P("col", "row"),
        P("row"),
        P("col", "row"),
        P("row"),
        P("col", "row"),
        P("row"),
        P("row", "col"),
        P("col"),
        P("row", "col"),
        P("col"),
    )
    return jax.shard_map(
        on_device, mesh=mesh, in_specs=in_specs, out_specs=out_specs, check_vma=False
    )
```

```python
import collections
import functools

import jax
import jax.numpy as jnp
from jax import lax
from jax.experimental import pallas as pl
from jax.experimental.pallas import tpu as pltpu
from jax.sharding import PartitionSpec as P

HD = 64
ROT = 16
BLOCK = 512
LONGEST = 16
VMEM = 60 * 1024 * 1024
Shape = collections.namedtuple("Shape", "seq_count row_count sequences heads")
HALF = 256
EPS = 1e-05
NEGATIVE = -1e30
F32 = jnp.float32
BF16 = jnp.bfloat16

NN = (((1,), (0,)), ((), ()))
NT = (((1,), (1,)), ((), ()))
TN = (((0,), (0,)), ((), ()))


def dot(left, right, dims=NN):
    return lax.dot_general(left, right, dims, preferred_element_type=F32)


def swap(value, axis, bit):
    count = lax.axis_size(axis)
    return lax.ppermute(value, axis, [(i, i ^ bit) for i in range(count)])


def swap_odd_rows(value):
    seq_count, row_count = lax.axis_size("seq"), lax.axis_size("row")
    pairs = []
    for s in range(1, seq_count, 2):
        for r in range(row_count):
            pairs.append((s * row_count + r, s * row_count + (r ^ 2)))
    moved = lax.ppermute(value, ("seq", "row"), pairs)
    return jnp.where(lax.rem(lax.axis_index("seq"), 2) == 0, value, moved)


def swap_some(value, axis, bit, parity):
    sizes = [lax.axis_size(name) for name in ("seq", "row", "col")]
    pairs = []
    for s in range(parity, sizes[0], 2):
        for r in range(sizes[1]):
            for c in range(sizes[2]):
                index = {"seq": s, "row": r, "col": c}
                source = (s * sizes[1] + r) * sizes[2] + c
                index[axis] ^= bit
                pairs.append((source, (index["seq"] * sizes[1] + index["row"]) * sizes[2] + index["col"]))
    return lax.ppermute(value, ("seq", "row", "col"), pairs)


def swap_add(value, axis, bit):
    rounded = lax.reduce_precision(value, 8, 7)
    return rounded + swap(rounded.astype(BF16), axis, bit).astype(F32)


def split_rows(vector):
    high = lax.reduce_precision(vector, 8, 7)
    return high.astype(BF16), (vector - high).astype(BF16)


def first_of(meta_ref, block, shape):
    start = jnp.int32(0)
    first = jnp.int32(0)
    for i in range(shape.sequences):
        first = jnp.where(start <= block, start, first)
        start = start + meta_ref[3 + i] // BLOCK
    return first


def attention_kernel(
    meta_ref,
    first_ref,
    dy_ref,
    cos_ref,
    sin_ref,
    ff_out_ref,
    ff_grad_ref,
    vec_ref,
    small0_ref,
    small1_ref,
    stats_ref,
    kv0_ref,
    kv1_ref,
    *rest,
    shape,
):
    heads = shape.heads
    stay_ref, go_ref, keep_ref, send_ref, stat_ref, dkv_out_ref, dkv_low_ref, cache_ref = rest[:8]
    dqw_ref, dow_ref, dqb_ref = rest[8:11]
    rest = rest[11:]
    (
        qd_ref,
        probs_ref,
        high_ref,
        sums_ref,
        dots_ref,
        acc_ref,
        dq_ref,
        dkv_ref,
        kv_ref,
        low_ref,
        zero_ref,
        qw_ref,
        ow_ref,
        copy_sem,
        late_sem,
    ) = rest
    blocks = kv_ref.shape[0]
    half = blocks // 2
    slot = pl.program_id(0)
    lanes = 2 * HD
    rows = heads * HALF
    seq, row, second_half = meta_ref[0], meta_ref[1], meta_ref[2]
    own_block = lax.bitwise_xor(seq, slot // 2) * shape.row_count + lax.bitwise_xor(row, slot % 2)
    first_block = first_of(meta_ref, own_block, shape)
    before = own_block - first_block

    def slot_of(block):
        apart_row = lax.bitwise_xor(lax.rem(block, shape.row_count), row)
        apart_seq = lax.bitwise_xor(block // shape.row_count, seq)
        return apart_row + shape.row_count * (
            apart_seq // 2 + (shape.seq_count // 2) * lax.rem(apart_seq, 2)
        )

    def put(index, rows):
        @pl.when(slot < 2)
        def _():
            stay_ref[slot, index] = rows

        @pl.when(slot >= 2)
        def _():
            go_ref[slot - 2, index] = rows.astype(BF16)

    def cache_copies(dealt, group):
        copies = []
        for i in range(dealt):
            owner = meta_ref[3 + shape.sequences + group * dealt + i]
            for part in (0, 1):
                take = jnp.where(second_half > 0, 1 - part, part) * HALF
                copies.append(
                    pltpu.make_async_copy(
                        kv_ref.at[slot_of(owner), pl.ds(take, HALF), :],
                        cache_ref.at[i, part * HALF : (part + 1) * HALF, :],
                        copy_sem.at[2 + 2 * i + part],
                    )
                )
        return copies

    pieces = [
        pltpu.make_async_copy(piece, kv_ref.at[i * half : (i + 1) * half], copy_sem.at[i])
        for i, piece in enumerate((kv0_ref, kv1_ref))
    ]
    late = [
        pltpu.make_async_copy(zero_ref, dkv_ref.at[i : i + 1], late_sem.at[i]) for i in range(blocks)
    ]

    @pl.when(slot == 0)
    def _():
        for copy in pieces:
            copy.start()
        zero_ref[...] = jnp.zeros_like(zero_ref)
        dqw_ref[...] = jnp.zeros_like(dqw_ref)
        dow_ref[...] = jnp.zeros_like(dow_ref)
        dqb_ref[...] = jnp.zeros_like(dqb_ref)
        for copy in late:
            copy.start()
        span = small0_ref.shape[1]
        count = heads * HD
        for i, small in enumerate((small0_ref, small1_ref)):
            part = slice(i * span, (i + 1) * span)
            qw_ref[:count, part] = small[:count, :]
            ow_ref[:count, part] = small[count : 2 * count, :]
        qw_ref[count:, :] = jnp.zeros_like(qw_ref[count:, :])
        ow_ref[count:, :] = jnp.zeros_like(ow_ref[count:, :])

    cosine = cos_ref[0]
    sine = sin_ref[0]
    lane = lax.broadcasted_iota(jnp.int32, (HALF, lanes), 1)
    front = lane < HD

    def rolled(values):
        return jnp.where(
            lane < ROT // 2,
            pltpu.roll(values, lanes - ROT // 2, 1),
            pltpu.roll(values, ROT // 2, 1),
        )

    def head_of(joined, h):
        return joined[:, (h // 2) * lanes : (h // 2 + 1) * lanes]

    def join(parts):
        tiles = []
        for h in range(0, heads, 2):
            other = parts[h + 1] if h + 1 < heads else jnp.zeros_like(parts[h])
            tiles.append(jnp.where(front, parts[h], other))
        return jnp.concatenate(tiles, axis=1)

    padded = qw_ref.shape[0]
    base = 2 * heads * HD + 7
    query_b = (
        small0_ref[base : base + 1, :padded].astype(F32)
        + small0_ref[base + 8 : base + 9, :padded].astype(F32)
    )
    pre_all = dot(first_ref[0], qw_ref[...], NT) + query_b
    d_all = dot(dy_ref[0], ow_ref[...], NT)
    for h in range(heads):
        pre = head_of(pre_all, h)
        grad = head_of(d_all, h)
        if h % 2:
            pre = pltpu.roll(pre, HD, 1)
        else:
            grad = pltpu.roll(grad, HD, 1)
        turned = jnp.where(front, pre * cosine + rolled(pre) * sine, 0.0)
        mine = slice(h * HALF, (h + 1) * HALF)
        qd_ref[mine, :] = turned.astype(BF16) * BF16(HD**-0.5)
        qd_ref[rows + h * HALF : rows + (h + 1) * HALF, :] = jnp.where(front, 0.0, grad).astype(BF16)

    @pl.when(slot == 0)
    def _():
        for copy in pieces:
            copy.wait()

    high_ref[...] = jnp.full_like(high_ref, NEGATIVE)
    sums_ref[...] = jnp.zeros_like(sums_ref)

    def block_at(step):
        return slot_of(first_block + step)

    def weigh(step, mask):
        scores = dot(kv_ref[block_at(step)], qd_ref[:rows, :], NT)
        if mask:
            row_in = lax.rem(lax.broadcasted_iota(jnp.int32, (BLOCK, rows), 1), HALF)
            key_in = lax.broadcasted_iota(jnp.int32, (BLOCK, rows), 0)
            limit = jnp.where(second_half > 0, BLOCK, 0)
            keep = (key_in <= row_in) | ((key_in >= HALF) & (key_in < limit))
            scores = jnp.where(keep, scores, NEGATIVE)
        high = jnp.max(scores, axis=0, keepdims=True)
        probs = jnp.exp(scores - high)
        probs_ref[step] = probs.astype(BF16)
        high_ref[pl.ds(step, 1), :] = high
        sums_ref[pl.ds(step, 1), :] = jnp.sum(probs, axis=0, keepdims=True)

    weigh(before, True)
    lax.fori_loop(0, before, lambda step, c: (weigh(step, False), c)[1], 0)

    share = jnp.exp(high_ref[...] - jnp.max(high_ref[...], axis=0, keepdims=True))
    high_ref[...] = share / jnp.sum(share * sums_ref[...], axis=0, keepdims=True)

    def mix(step, first):
        probs = (probs_ref[step].astype(F32) * high_ref[pl.ds(step, 1), :]).astype(BF16)
        probs_ref[step] = probs
        part = dot(probs, kv_ref[block_at(step)], TN)
        if first:
            acc_ref[...] = part
        else:
            acc_ref[...] += part

    mix(before, True)
    lax.fori_loop(0, before, lambda step, c: (mix(step, False), c)[1], 0)

    @pl.when(slot == 0)
    def _():
        for copy in late:
            copy.wait()

    parts = []
    for h in range(heads):
        mine = slice(h * HALF, (h + 1) * HALF)
        mixed = acc_ref[mine, :]
        grad = qd_ref[rows + h * HALF : rows + (h + 1) * HALF, :].astype(F32)
        dots_ref[:, mine] = jnp.sum(jnp.transpose(mixed * grad), axis=0, keepdims=True)
        parts.append(mixed if h % 2 else pltpu.roll(mixed, HD, 1))
    joined = join(parts).astype(BF16)
    put(0, ff_out_ref[0] + dot(joined, ow_ref[...]))
    dow_ref[...] += dot(joined, dy_ref[0], TN)

    def backward(step, first):
        where = block_at(step)
        block = kv_ref[where]
        probs = probs_ref[step]
        grad_probs = dot(block, qd_ref[rows:, :], NT)
        grad_scores = (probs.astype(F32) * (grad_probs - dots_ref[...])).astype(BF16)
        total = dot(jnp.concatenate([grad_scores, probs], axis=1), qd_ref[...])
        grad_q = dot(grad_scores, block, TN)
        if first:
            dq_ref[...] = grad_q
        else:
            dq_ref[...] += grad_q
        dkv_ref[where] = (dkv_ref[where].astype(F32) + total).astype(dkv_ref.dtype)

    backward(before, True)
    lax.fori_loop(0, before, lambda step, c: (backward(step, False), c)[1], 0)

    parts = []
    for h in range(heads):
        part = dq_ref[h * HALF : (h + 1) * HALF, :] * (HD**-0.5)
        part = part * cosine - rolled(part) * sine
        parts.append(pltpu.roll(part, HD, 1) if h % 2 else part)
    joined = join(parts)
    dqb_ref[...] += jnp.sum(joined, axis=0, keepdims=True)
    joined = joined.astype(BF16)
    put(1, ff_grad_ref[0] + dot(joined, qw_ref[...]) * vec_ref[0:1, :])
    dqw_ref[...] += dot(joined, first_ref[0], TN)

    @pl.when(slot == 0)
    def _():
        dealt = cache_ref.shape[0]
        group = seq * 2 + second_half
        for copy in cache_copies(dealt, group):
            copy.start()

    @pl.when(slot == 3)
    def _():
        copies = [pltpu.make_async_copy(dkv_ref.at[:half], dkv_out_ref, copy_sem.at[0])]
        copies[0].start()
        if dkv_ref.dtype == BF16:
            copies.append(pltpu.make_async_copy(dkv_ref.at[half:], dkv_low_ref, copy_sem.at[1]))
        else:
            low_ref[...] = dkv_ref[half:].astype(BF16)
            copies.append(pltpu.make_async_copy(low_ref, dkv_low_ref, copy_sem.at[1]))
        copies[1].start()
        copies += cache_copies(cache_ref.shape[0], seq * 2 + second_half)
        count = heads * HD
        span = small0_ref.shape[1]
        bias_up = stats_ref[2:3, :]
        bias_q = dqb_ref[...]
        for i, target in enumerate((keep_ref, send_ref)):
            part = slice(i * span, (i + 1) * span)
            target[:count, :] = dqw_ref[:count, part].astype(BF16)
            target[count : 2 * count, :] = dow_ref[:count, part].astype(BF16)
            rows_of = jnp.concatenate(
                [
                    bias_up[:, :span],
                    bias_up[:, span:],
                    jnp.concatenate([bias_q, jnp.zeros((1, span - padded), F32)], axis=1),
                    jnp.zeros((5, span), F32),
                ],
                axis=0,
            )
            target[2 * count :, :] = jnp.concatenate(
                [rows_of, jnp.zeros((target.shape[0] - 2 * count - 8, span), F32)], axis=0
            ).astype(BF16)
        weight = qw_ref[...].astype(F32)
        column = jnp.transpose(jnp.broadcast_to(bias_q, (8, padded)))[:, 0:1]
        plain = jnp.sum(weight * column, axis=0, keepdims=True)
        stat_ref[0:1, :] = (
            jnp.sum(weight * dqw_ref[...], axis=0, keepdims=True) - vec_ref[1:2, :] * plain
        ) / vec_ref[0:1, :]
        stat_ref[1:2, :] = plain
        stat_ref[2:8, :] = jnp.zeros((6, 2 * span), F32)
        for copy in copies:
            copy.wait()


def attention(meta, first_in, dy, cosine, sine, ff, vectors, small, stats, pieces, shape):
    _, _, width = first_in.shape
    half = pieces[0].shape[0]
    blocks = 2 * half
    lanes = 2 * HD
    heads = shape.heads
    padded = -(-heads // 2) * lanes
    rows = heads * HALF
    longest = min(LONGEST, blocks // 2)
    total_type = F32 if blocks <= 32 else BF16
    dealt = blocks // (2 * shape.seq_count)

    def per_slot(lanes):
        return pl.BlockSpec((1, HALF, lanes), lambda i, m: (i, 0, 0))

    def whole(array):
        return pl.BlockSpec(
            array.shape, lambda i, m: (0,) * len(array.shape), pipeline_mode=pl.Buffered(buffer_count=1)
        )

    far = pl.BlockSpec(memory_space=pltpu.MemorySpace.HBM)
    arrays = [first_in, dy, cosine, sine, *ff, vectors, *small, stats, *pieces]
    in_specs = [per_slot(width), per_slot(width), per_slot(lanes), per_slot(lanes)]
    in_specs += [per_slot(width)] * 2 + [whole(a) for a in (vectors, *small, stats)] + [far] * 2
    part = jax.ShapeDtypeStruct((2 * heads * HD + 32, width // 2), BF16)
    results = [
        jax.ShapeDtypeStruct((2, 2, HALF, width), F32),
        jax.ShapeDtypeStruct((2, 2, HALF, width), BF16),
        part,
        part,
        jax.ShapeDtypeStruct((8, width), F32),
    ]
    out_shape = [
        *results,
        jax.ShapeDtypeStruct((half, BLOCK, lanes), total_type),
        jax.ShapeDtypeStruct((half, BLOCK, lanes), BF16),
        jax.ShapeDtypeStruct((dealt, BLOCK, lanes), BF16),
    ]
    out_specs = [whole(a) for a in results] + [far] * 3
    return pl.pallas_call(
        functools.partial(attention_kernel, shape=shape),
        grid_spec=pltpu.PrefetchScalarGridSpec(
            num_scalar_prefetch=1,
            grid=(4,),
            in_specs=in_specs,
            out_specs=out_specs,
            scratch_shapes=[
                pltpu.VMEM((padded, width), F32),
                pltpu.VMEM((padded, width), F32),
                pltpu.VMEM((1, padded), F32),
                pltpu.VMEM((2 * rows, lanes), BF16),
                pltpu.VMEM((longest, BLOCK, rows), BF16),
                pltpu.VMEM((longest, rows), F32),
                pltpu.VMEM((longest, rows), F32),
                pltpu.VMEM((1, rows), F32),
                pltpu.VMEM((rows, lanes), F32),
                pltpu.VMEM((rows, lanes), F32),
                pltpu.VMEM((blocks, BLOCK, lanes), total_type),
                pltpu.VMEM((blocks, BLOCK, lanes), BF16),
                pltpu.VMEM((half if blocks <= 32 else 1, BLOCK, lanes), BF16),
                pltpu.VMEM((1, BLOCK, lanes), total_type),
                pltpu.VMEM((padded, width), BF16),
                pltpu.VMEM((padded, width), BF16),
                pltpu.SemaphoreType.DMA((2 + 2 * dealt,)),
                pltpu.SemaphoreType.DMA((blocks,)),
            ],
        ),
        out_shape=out_shape,
        cost_estimate=pl.CostEstimate(
            flops=24_000_000_000, bytes_accessed=30_000_000, transcendentals=30_000_000
        ),
        compiler_params=pltpu.CompilerParams(
            vmem_limit_bytes=67_043_328 if blocks > 32 else VMEM
        ),
        name="attention",
    )(meta, *arrays)


ORDER = (0, 1, 2, 3)


def tables_kernel(meta_ref, cos_ref, sin_ref, *, shape):
    seq, row, col = meta_ref[0], meta_ref[1], meta_ref[2]
    lane = lax.broadcasted_iota(jnp.int32, (HALF, 2 * HD), 1)
    inside = lax.broadcasted_iota(jnp.int32, (HALF, 2 * HD), 0)
    half_rot = ROT // 2
    exponent = lax.rem(lane, half_rot).astype(F32) * (1.0 / half_rot)
    frequency = jnp.where(lane < ROT, 1.0 / jnp.exp(exponent * jnp.log(jnp.full_like(exponent, 10000.0))), 0.0)
    for i, (slot, half) in enumerate([(slot, col) for slot in ORDER] + [(0, 1 - col)]):
        block = lax.bitwise_xor(seq, slot // 2) * shape.row_count + lax.bitwise_xor(row, slot % 2)
        start = (block - first_of(meta_ref, block, shape)) * BLOCK
        angles = (inside + (start + half * HALF)).astype(F32) * frequency
        cos_ref[i] = jnp.cos(angles)
        turned = jnp.sin(angles)
        sin_ref[i] = jnp.where(lane < half_rot, -turned, jnp.where(lane < ROT, turned, 0.0))


def tables(meta, shape):
    table = jax.ShapeDtypeStruct((5, HALF, 2 * HD), F32)
    return pl.pallas_call(
        functools.partial(tables_kernel, shape=shape),
        in_specs=[pl.BlockSpec(memory_space=pltpu.SMEM)],
        out_specs=[pl.BlockSpec(memory_space=pltpu.VMEM)] * 2,
        out_shape=[table, table],
        name="tables",
    )(meta)


def forward_kernel(
    meta_ref,
    both0_ref,
    both1_ref,
    both2_ref,
    both3_ref,
    vec_ref,
    pack_ref,
    even_ref,
    z_ref,
    x_got_ref,
    odd0_ref,
    odd1_ref,
    first_ref,
    dy_ref,
    out_ref,
    dx_ref,
    grads_ref,
    stat_ref,
    small0_ref,
    small1_ref,
    x_ref,
    own_ref,
    other_ref,
    up_ref,
    down_ref,
    second_ref,
    hidden_ref,
    grad_ref,
    dys_ref,
    bias_ref,
    sem,
):
    step = pl.program_id(0)
    span = pack_ref.shape[1]
    total = pack_ref.shape[0]
    here = pl.ds(pl.multiple_of(step * HALF, HALF), HALF)
    core = lax.rem(meta_ref[0], 2)
    side = lax.rem(meta_ref[0] // 2, 2)

    def run(copies):
        for copy in copies:
            copy.start()
        for copy in copies:
            copy.wait()

    @pl.when((step == 0) & (core == 0))
    def _():
        run(
            [
                pltpu.make_async_copy(pack_ref, own_ref, sem.at[0]),
                pltpu.make_async_copy(even_ref, other_ref, sem.at[1]),
            ]
        )

    @pl.when((step == 0) & (core == 1))
    def _():
        half = total // 2
        near = pl.ds(pl.multiple_of(side * half, half), half)
        far = pl.ds(pl.multiple_of((1 - side) * half, half), half)
        run(
            [
                pltpu.make_async_copy(z_ref, own_ref.at[near, :], sem.at[0]),
                pltpu.make_async_copy(x_got_ref, own_ref.at[far, :], sem.at[1]),
                pltpu.make_async_copy(odd0_ref, other_ref.at[near, :], sem.at[2]),
                pltpu.make_async_copy(odd1_ref, other_ref.at[far, :], sem.at[3]),
            ]
        )

    @pl.when(step == 0)
    def _():
        base = small0_ref.shape[0]
        for i, held in enumerate((own_ref, other_ref)):
            part = slice(i * span, (i + 1) * span)
            (small0_ref, small1_ref)[i][...] = held[:base, :]
            up_ref[part, :span] = held[base : base + span, :]
            up_ref[part, span:] = held[base + span : base + 2 * span, :]
            down_ref[:, part] = held[base + 2 * span : base + 4 * span, :]
        bias_ref[...] = jnp.zeros_like(bias_ref)

    for i, piece in enumerate((both0_ref, both1_ref, both2_ref, both3_ref)):

        @pl.when(step == i)
        def _():
            x_ref[...] = piece[0]
            dys_ref[here, :] = piece[1]

    base = small0_ref.shape[0] - 32
    bias = own_ref[base : base + 8, :].astype(F32) + own_ref[base + 8 : base + 16, :].astype(F32)
    upward_b = jnp.concatenate([bias[5:6], bias[6:7]], axis=1)
    wide = x_ref[...].astype(F32)
    mean = jnp.mean(wide, axis=1, keepdims=True)
    spread = jnp.mean(wide * wide, axis=1, keepdims=True) - mean * mean
    normed = (wide - mean) * lax.rsqrt(spread + EPS)
    first_ref[0] = (normed * vec_ref[0:1, :] + vec_ref[1:2, :]).astype(BF16)
    second = (normed * vec_ref[2:3, :] + vec_ref[3:4, :]).astype(BF16)
    dy = dys_ref[here, :]
    dy_ref[0] = dy
    second_ref[here, :] = second
    upward = dot(second, up_ref[...]) + upward_b
    bell = lax.erf(upward * (2.0**-0.5)) * 0.5 + 0.5
    hidden = (upward * bell).astype(BF16)
    slope = bell + upward * jnp.exp(upward * upward * -0.5) * ((2.0 * 3.141592653589793) ** -0.5)
    grad = dot(dy, down_ref[...], NT) * slope
    bias_ref[0:1, :] += jnp.sum(grad, axis=0, keepdims=True)
    grad = grad.astype(BF16)
    hidden_ref[here, :] = hidden
    grad_ref[here, :] = grad
    out_ref[0] = dot(hidden, down_ref[...])
    dx_ref[0] = dot(grad, up_ref[...], NT) * vec_ref[2:3, :]

    @pl.when(step == 3)
    def _():
        down_grad = dot(hidden_ref[...], dys_ref[...], TN)
        grads_ref[0, 2 * span :, :] = down_grad[:, :span].astype(BF16)
        grads_ref[1, 2 * span :, :] = down_grad[:, span:].astype(BF16)
        up_grad = dot(second_ref[...], grad_ref[...], TN)
        for i in (0, 1):
            part = slice(i * span, (i + 1) * span)
            grads_ref[0, part, :] = up_grad[:span, part].astype(BF16)
            grads_ref[1, part, :] = up_grad[span:, part].astype(BF16)
        weight = up_ref[...].astype(F32)
        bias_grad = bias_ref[0:1, :]

        def as_row(values):
            column = jnp.sum(values, axis=1, keepdims=True)
            return jnp.transpose(jnp.broadcast_to(column, (2 * span, 128)))[0:1, :]

        plain = as_row(weight * bias_grad)
        stat_ref[0:1, :] = (as_row(weight * up_grad) - vec_ref[3:4, :] * plain) / vec_ref[2:3, :]
        stat_ref[1:2, :] = plain
        stat_ref[2:3, :] = bias_grad
        stat_ref[3:8, :] = jnp.zeros((5, 2 * span), F32)


def feed_forward(meta, both, vectors, weights, small_rows):
    width = vectors.shape[1]
    span = width // 2
    total = weights[0].shape[0]

    def whole(array):
        return pl.BlockSpec(
            array.shape, lambda i: (0,) * len(array.shape), pipeline_mode=pl.Buffered(buffer_count=1)
        )

    slot = pl.BlockSpec((1, HALF, width), lambda i: (i, 0, 0))
    arrays = [*both, vectors]
    grads = jax.ShapeDtypeStruct((2, 4 * span, span), BF16)
    stat = jax.ShapeDtypeStruct((8, width), F32)
    small = jax.ShapeDtypeStruct((small_rows, span), BF16)
    tokens = lambda kind: jax.ShapeDtypeStruct((4, HALF, width), kind)
    return pl.pallas_call(
        forward_kernel,
        grid=(4,),
        in_specs=[pl.BlockSpec(memory_space=pltpu.SMEM)]
        + [whole(a) for a in arrays]
        + [pl.BlockSpec(memory_space=pltpu.MemorySpace.HBM)] * len(weights),
        out_specs=[slot] * 4 + [whole(grads), whole(stat), whole(small), whole(small)],
        out_shape=[tokens(BF16), tokens(BF16), tokens(F32), tokens(F32), grads, stat, small, small],
        scratch_shapes=[
            pltpu.VMEM((HALF, width), BF16),
            pltpu.VMEM((total, span), BF16),
            pltpu.VMEM((total, span), BF16),
            pltpu.VMEM((width, width), BF16),
            pltpu.VMEM((width, width), BF16),
            pltpu.VMEM((4 * HALF, width), BF16),
            pltpu.VMEM((4 * HALF, width), BF16),
            pltpu.VMEM((4 * HALF, width), BF16),
            pltpu.VMEM((4 * HALF, width), BF16),
            pltpu.VMEM((8, width), F32),
            pltpu.SemaphoreType.DMA((4,)),
        ],
        cost_estimate=pl.CostEstimate(
            flops=7_000_000_000, bytes_accessed=20_000_000, transcendentals=3_000_000
        ),
        compiler_params=pltpu.CompilerParams(vmem_limit_bytes=VMEM),
        name="feed_forward",
    )(meta, *arrays, *weights)


def prologue_kernel(
    where_ref, tokens_ref, dy_ref, kvw_ref, vec_ref, pack_ref, x_ref, mine_ref
):
    col = where_ref[2]
    span = dy_ref.shape[1]
    width = tokens_ref.shape[1]
    here = pl.ds(pl.multiple_of(col * HALF, HALF), HALF)
    there = pl.ds(pl.multiple_of((1 - col) * HALF, HALF), HALF)
    pack_ref[:HALF, :] = dy_ref[there, :]
    base = HALF + 2 * HD
    pack_ref[HALF:base, :] = jnp.transpose(kvw_ref[...].astype(F32)).astype(BF16)
    vectors = vec_ref[...]
    high = vectors.astype(BF16).astype(F32)
    both = jnp.concatenate([high, vectors - high], axis=0).astype(BF16)
    pack_ref[base:, :] = both
    for i, rows in enumerate((here, there)):
        part = slice(i * HALF, (i + 1) * HALF)
        x_ref[part, :span] = tokens_ref[rows, pl.ds(pl.multiple_of(col * span, 128), span)]
        x_ref[part, span:] = tokens_ref[rows, pl.ds(pl.multiple_of((1 - col) * span, 128), span)]
    mine_ref[...] = dy_ref[here, :]


def prologue(meta, tokens, cotangent, keyval_weight, vectors):
    width = tokens.shape[1]
    span = width // 2
    rows = vectors.shape[0]
    vmem = pl.BlockSpec(memory_space=pltpu.VMEM)
    return pl.pallas_call(
        prologue_kernel,
        in_specs=[pl.BlockSpec(memory_space=pltpu.SMEM)] + [vmem] * 4,
        out_specs=[vmem] * 3,
        out_shape=[
            jax.ShapeDtypeStruct((HALF + 2 * HD + 2 * rows, span), BF16),
            jax.ShapeDtypeStruct((2 * HALF, width), BF16),
            jax.ShapeDtypeStruct((HALF, span), BF16),
        ],
        name="prologue",
    )(meta, tokens, cotangent, keyval_weight, vectors)


def weights_kernel(where_ref, qw_ref, ow_ref, up_ref, down_ref, vec_ref, pack_ref, part_ref):
    count = qw_ref.shape[0]
    span = pack_ref.shape[1]
    total = pack_ref.shape[0]
    vectors = vec_ref[...]
    high = vectors.astype(BF16).astype(F32)
    both = jnp.concatenate([high, vectors - high], axis=0).astype(BF16)
    pack_ref[:count, :] = qw_ref[...]
    pack_ref[count : 2 * count, :] = ow_ref[...]
    pack_ref[2 * count : 2 * count + 16, :] = both
    pack_ref[2 * count + 16 : 2 * count + 32, :] = jnp.zeros((16, span), BF16)
    base = 2 * count + 32
    pack_ref[base : base + span, :] = up_ref[:, :span]
    pack_ref[base + span : base + 2 * span, :] = up_ref[:, span:]
    pack_ref[base + 2 * span :, :] = down_ref[...]
    side = lax.rem(where_ref[0] // 2, 2)
    part_ref[...] = pack_ref[pl.ds(pl.multiple_of(side * (total // 2), 16), total // 2), :]


def pack_weights(meta, query_t, output_weight, upward_weight, down_weight, vectors):
    span = output_weight.shape[1]
    total = 2 * query_t.shape[0] + 32 + 2 * upward_weight.shape[0] + down_weight.shape[0]
    vmem = pl.BlockSpec(memory_space=pltpu.VMEM)
    return pl.pallas_call(
        weights_kernel,
        in_specs=[pl.BlockSpec(memory_space=pltpu.SMEM)] + [vmem] * 5,
        out_specs=[vmem] * 2,
        out_shape=[
            jax.ShapeDtypeStruct((total, span), BF16),
            jax.ShapeDtypeStruct((total // 2, span), BF16),
        ],
        name="pack_weights",
    )(meta, query_t, output_weight, upward_weight, down_weight, vectors)


def own_kernel(
    x_ref, mine_ref, pack_ref, got_ref, vec_ref, cos_ref, sin_ref, bias_ref, pair_ref, both_ref, kvw_ref, full_ref
):
    span = mine_ref.shape[1]
    rows = vec_ref.shape[0]
    base = HALF + 2 * HD
    other = got_ref[base : base + 2 * rows, :].astype(F32)
    full = jnp.concatenate([vec_ref[...], other[:rows] + other[rows:]], axis=1)
    full_ref[...] = full
    both_ref[0] = x_ref[:HALF, :]
    both_ref[1, :, :span] = mine_ref[...]
    both_ref[1, :, span:] = got_ref[:HALF, :]
    kvw_ref[:, :span] = pack_ref[HALF:base, :]
    kvw_ref[:, span:] = got_ref[HALF:base, :]
    wide = x_ref[...].astype(F32)
    mean = jnp.mean(wide, axis=1, keepdims=True)
    spread = jnp.mean(wide * wide, axis=1, keepdims=True) - mean * mean
    normed = (wide - mean) * lax.rsqrt(spread + EPS)
    first = (normed * full[0:1, :] + full[1:2, :]).astype(BF16)
    pre_all = dot(first, kvw_ref[...], NT) + bias_ref[...]
    lanes = pre_all.shape[1]
    lane = lax.broadcasted_iota(jnp.int32, (HALF, lanes), 1)
    for i in (0, 1):
        pre = pre_all[i * HALF : (i + 1) * HALF, :]
        rolled = jnp.where(
            lane < ROT // 2, pltpu.roll(pre, lanes - ROT // 2, 1), pltpu.roll(pre, ROT // 2, 1)
        )
        pair_ref[0, i * HALF : (i + 1) * HALF, :] = (
            pre * cos_ref[4 * i] + rolled * sin_ref[4 * i]
        ).astype(BF16)


def own_pairs(x_own, mine, pack, got, vectors, cosine, sine, bias):
    width = x_own.shape[1]
    vmem = pl.BlockSpec(memory_space=pltpu.VMEM)
    return pl.pallas_call(
        own_kernel,
        in_specs=[vmem] * 8,
        out_specs=[vmem] * 4,
        out_shape=[
            jax.ShapeDtypeStruct((1, 2 * HALF, 2 * HD), BF16),
            jax.ShapeDtypeStruct((2, HALF, width), BF16),
            jax.ShapeDtypeStruct((2 * HD, width), BF16),
            jax.ShapeDtypeStruct((vectors.shape[0], width), F32),
        ],
        name="own_pairs",
    )(x_own, mine, pack, got, vectors, cosine, sine, bias)


def pairs_kernel(
    keep_ref, got_ref, cos_ref, sin_ref, first_ref, kvw_ref, vec_ref, stat_ref, ff_ref, dys_ref, mine_ref, send_ref
):
    span = mine_ref.shape[1]
    lanes = 2 * HD
    lane = lax.broadcasted_iota(jnp.int32, (HALF, lanes), 1)
    total = keep_ref[...] + got_ref[...].astype(F32)
    weight = jnp.zeros((lanes, 2 * span), F32)
    bias = jnp.zeros((1, lanes), F32)
    for i in (0, 1):
        part = total[i]
        rolled = jnp.where(
            lane < ROT // 2, pltpu.roll(part, lanes - ROT // 2, 1), pltpu.roll(part, ROT // 2, 1)
        )
        turned = part * cos_ref[i] - rolled * sin_ref[i]
        bias = bias + jnp.sum(turned, axis=0, keepdims=True)
        weight = weight + dot(turned.astype(BF16), first_ref[i], TN)
    kvw = kvw_ref[...].astype(F32)
    column = jnp.transpose(jnp.broadcast_to(bias, (8, lanes)))[:, 0:1]
    plain = jnp.sum(kvw * column, axis=0, keepdims=True)
    gain = (jnp.sum(kvw * weight, axis=0, keepdims=True) - vec_ref[1:2, :] * plain) / vec_ref[0:1, :]
    fill = jnp.zeros((1, span - lanes), F32)
    bias = jnp.concatenate([bias.astype(BF16).astype(F32), fill], axis=1)
    for i, target in enumerate((mine_ref, send_ref)):
        part = slice(i * span, (i + 1) * span)
        target[:lanes, :] = weight[:, part].astype(target.dtype)
        rows = jnp.concatenate(
            [
                stat_ref[0:1, part] + gain[:, part],
                stat_ref[1:2, part] + plain[:, part],
                ff_ref[0:2, part],
                bias,
                dys_ref[...] if i == 0 else jnp.zeros((1, span), F32),
                jnp.zeros((10, span), F32),
            ],
            axis=0,
        )
        target[lanes:, :] = rows.astype(target.dtype)


def pair_sums(keep, got, cosine, sine, first_in, keyval, vectors, stats, ff_stats, dy_sum):
    width = keyval.shape[1]
    vmem = pl.BlockSpec(memory_space=pltpu.VMEM)
    return pl.pallas_call(
        pairs_kernel,
        in_specs=[vmem] * 10,
        out_specs=[vmem] * 2,
        out_shape=[
            jax.ShapeDtypeStruct((2 * HD + 16, width // 2), F32),
            jax.ShapeDtypeStruct((2 * HD + 16, width // 2), BF16),
        ],
        name="pair_sums",
    )(keep, got, cosine, sine, first_in, keyval, vectors, stats, ff_stats, dy_sum)


def rows_kernel(
    own_ref,
    got_ref,
    cos_ref,
    sin_ref,
    kvw_ref,
    vec_ref,
    x_ref,
    dy_ref,
    keep_ref,
    core_ref,
    back_ref,
    mine_ref,
    send_ref,
):
    span = mine_ref.shape[2]
    lanes = 2 * HD
    lane = lax.broadcasted_iota(jnp.int32, (HALF, lanes), 1)
    part = own_ref[0] + got_ref[...].astype(F32)
    rolled = jnp.where(
        lane < ROT // 2, pltpu.roll(part, lanes - ROT // 2, 1), pltpu.roll(part, ROT // 2, 1)
    )
    turned = (part * cos_ref[0] - rolled * sin_ref[0]).astype(BF16)
    wide = x_ref[:HALF, :].astype(F32)
    mean = jnp.mean(wide, axis=1, keepdims=True)
    spread = jnp.mean(wide * wide, axis=1, keepdims=True) - mean * mean
    root = lax.rsqrt(spread + EPS)
    normed = (wide - mean) * root
    grad = keep_ref[0, 1] + core_ref[0, 1].astype(F32) + back_ref[1].astype(F32) + dot(turned, kvw_ref[...]) * vec_ref[0:1, :]
    one = jnp.mean(grad, axis=1, keepdims=True)
    two = jnp.mean(grad * normed, axis=1, keepdims=True)
    grad = dy_ref[0].astype(F32) + root * (grad - one - normed * two)
    out = wide + keep_ref[0, 0] + core_ref[0, 0].astype(F32) + back_ref[0].astype(F32) + vec_ref[4:5, :]
    for i, rows in enumerate((out.astype(BF16), grad.astype(BF16))):
        mine_ref[i] = rows[:, :span]
        send_ref[i] = rows[:, span:]


def own_rows(own, got, cosine, sine, keyval, vectors, x_block, dy, keep, core, back):
    width = keyval.shape[1]
    vmem = pl.BlockSpec(memory_space=pltpu.VMEM)
    half = jax.ShapeDtypeStruct((2, HALF, width // 2), BF16)
    return pl.pallas_call(
        rows_kernel,
        in_specs=[vmem] * 11,
        out_specs=[vmem] * 2,
        out_shape=[half, half],
        name="own_rows",
    )(own, got, cosine, sine, keyval, vectors, x_block, dy, keep, core, back)


def after(value, *others):
    return lax.optimization_barrier((value,) + others)[0]


def on_device(
    tokens,
    cotangent,
    lengths,
    block_order,
    attention_gain,
    attention_shift,
    feedforward_gain,
    feedforward_shift,
    query_weight,
    query_bias,
    keyval_weight,
    keyval_bias,
    upward_weight,
    upward_bias,
    output_weight,
    output_bias,
    down_weight,
    down_bias,
):
    seq_count = lax.axis_size("seq")
    row_count = lax.axis_size("row")
    col_count = lax.axis_size("col")
    seq_me = lax.axis_index("seq")
    row_me = lax.axis_index("row")
    col_me = lax.axis_index("col")
    block_total = block_order.shape[0]
    width = tokens.shape[1]
    span = width // 2
    heads = query_weight.shape[1] // HD
    head_width = heads * HD
    pair_width = 2 * HD

    shape = Shape(seq_count, row_count, lengths.shape[0], heads)
    meta = jnp.concatenate(
        [jnp.stack([seq_me, row_me, col_me]).astype(jnp.int32), lengths, block_order]
    )

    vectors = jnp.concatenate(
        [
            attention_gain,
            attention_shift,
            feedforward_gain,
            feedforward_shift,
            output_bias + down_bias,
            upward_bias,
            query_bias,
            jnp.zeros((span - head_width,), F32),
        ]
    ).reshape(8, span)
    pack, x_block, dy_mine = prologue(meta, tokens, cotangent, keyval_weight, vectors)
    received = swap(pack, "col", 1)
    weights, weights_half = pack_weights(
        after(meta, pack), jnp.transpose(query_weight), output_weight, upward_weight, down_weight, vectors
    )
    weights_z = swap_some(weights_half, "row", 2, 1)
    weights_even = swap_some(after(weights, received), "col", 1, 0)
    cosine, sine = tables(after(meta, weights), shape)

    pairs, both, keyval_full, vec_full = own_pairs(
        x_block, dy_mine, pack, received, vectors, cosine, sine, keyval_bias[None]
    )
    steps = [("row", 1), ("row", 2)]
    bit = 2
    while bit < seq_count:
        steps.append(("seq", bit))
        bit = bit * 2
    got = swap(pairs, "row", 1)
    weights_x = swap_some(after(weights_z, got), "seq", 2, 1)
    weights_odd0 = swap_some(after(weights_z, got), "col", 1, 1)
    both_got = swap(after(both, got), "row", 1)
    pairs = jnp.concatenate([pairs, got], axis=0)
    got = swap(pairs, "row", 2)
    weights_odd1 = swap_some(after(weights_x, got), "col", 1, 1)
    got = after(got, weights_x, weights_odd0, weights_even)
    for axis, bit in steps[2:]:
        pairs = jnp.concatenate([pairs, got], axis=0)
        got = swap(pairs, axis, bit)
    got = after(got, weights_odd1, both_got)
    both_two = swap(after(both, got), "seq", 1)
    both_three = swap(after(both_got, got), "seq", 1)
    pairs = jnp.concatenate([pairs, got], axis=0)
    pieces = (pairs, swap(pairs, "seq", 1))

    first_in, dy_all, ff_out, ff_grad, ff_grads, ff_stats, small0, small1 = feed_forward(
        meta,
        (both, both_got, both_two, both_three),
        vec_full,
        (weights, weights_even, weights_z, weights_x, weights_odd0, weights_odd1),
        2 * head_width + 32,
    )

    ff_z = swap_some(ff_grads, "row", 2, 1)
    stay, go, small_keep, small_send, stats, keep_pairs, send_pairs, cache_rows = attention(
        after(meta, ff_grads),
        first_in,
        dy_all,
        cosine,
        sine,
        (ff_out, ff_grad),
        vec_full,
        (small0, small1),
        ff_stats,
        pieces,
        shape,
    )

    got = swap(after(send_pairs, ff_z), "seq", 1)
    col_send = (keep_pairs[:, HALF:].astype(F32) + got[:, HALF:].astype(F32)).astype(BF16)
    col_got = swap(col_send, "col", 1)
    core_got = swap(after(go, col_send), "seq", 1)
    away = (stay[1] + core_got[1].astype(F32)).astype(BF16)
    back = swap(away, "row", 1)
    col_got = after(col_got, away)
    core = lax.rem(seq_me, 2)

    def core_halves(moved, axis=0):
        half = moved.shape[axis] // 2
        keep = lax.dynamic_slice_in_dim(moved, core * half, half, axis)
        return keep, lax.dynamic_slice_in_dim(moved, (1 - core) * half, half, axis)

    def over_seq(value):
        bit = 2
        while bit < seq_count:
            value = swap_add(value, "seq", bit)
            bit = bit * 2
        return value.astype(BF16)

    def both_halves(value):
        other = swap(value, "seq", 1)
        first = jnp.where(core == 0, value, other)
        second = jnp.where(core == 0, other, value)
        return jnp.concatenate([first, second], axis=0).astype(F32)

    ff_keep, ff_away = core_halves(jnp.where(core == 0, after(ff_grads, col_send), ff_z), 1)
    ff_core = swap(ff_away, "seq", 1)
    ff_col = swap(
        after((ff_keep[1].astype(F32) + ff_core[1].astype(F32)).astype(BF16), col_got), "col", 1
    )
    ff_sum = ff_keep[0].astype(F32) + ff_core[0].astype(F32) + ff_col.astype(F32)
    total = keep_pairs[:, :HALF].astype(F32) + got[:, :HALF].astype(F32) + col_got.astype(F32)
    small_got = swap(after(small_send, ff_col), "col", 1)
    small_sum = (small_keep.astype(F32) + small_got.astype(F32)).astype(BF16)
    for axis, bit in reversed(steps[2:]):
        half = total.shape[0] // 2
        total = total[:half] + swap(total[half:].astype(BF16), axis, bit).astype(F32)
    total = after(total, back)
    row_got = after(swap(total[2:].astype(BF16), "row", 2), ff_sum)
    small_moved = swap_odd_rows(after(small_sum, row_got))
    keep_two = total[:2]
    dy_sum = jnp.sum(cotangent.astype(F32), axis=0)[None]
    z_send = (keep_two[1] + row_got[1].astype(F32)).astype(BF16)
    z_got = swap(z_send, "row", 1)
    extra_mine, extra_send = pair_sums(
        keep_two, row_got, cosine, sine, first_in, keyval_full, vec_full, stats, ff_stats, dy_sum
    )
    extra = extra_mine + swap(extra_send, "col", 1).astype(F32)
    own_total = (keep_two[0] + row_got[0].astype(F32))[None]
    mine, away_rows = own_rows(
        own_total, z_got, cosine, sine, keyval_full, vec_full, x_block, dy_all, stay, core_got, back
    )
    other = swap(away_rows, "col", 1)
    first = jnp.where(col_me == 0, mine, other)
    second = jnp.where(col_me == 0, other, mine)
    layer_out = jnp.concatenate([first[0], second[0]], axis=0)
    grad_tokens = jnp.concatenate([first[1], second[1]], axis=0)

    sum_ff = both_halves(over_seq(ff_sum))
    sum_up = jnp.concatenate([sum_ff[:span], sum_ff[span : 2 * span]], axis=1)
    sum_down = sum_ff[2 * span :]
    keep, send = core_halves(small_moved)
    sum_small = both_halves(over_seq(keep.astype(F32) + swap(send, "seq", 1).astype(F32)))
    sum_query = jnp.transpose(sum_small[:head_width])
    sum_output = sum_small[head_width : 2 * head_width]
    base = 2 * head_width
    sum_bias_up = sum_small[base : base + 2].reshape(-1)
    sum_bias_query = sum_small[base + 2, :head_width]

    bit = 1
    while bit < seq_count:
        extra = swap_add(extra, "seq", bit)
        bit = bit * 2
    for bit in (1, 2):
        extra = swap_add(extra, "row", bit)
    part = pair_width // row_count
    keyval_weight_out = jnp.transpose(lax.dynamic_slice_in_dim(extra, row_me * part, part, 0))
    keyval_bias_out = lax.dynamic_slice_in_dim(extra[pair_width + 4], row_me * part, part, 0)
    bias_out_grad = extra[pair_width + 5]
    cache_rows = cache_rows.reshape(-1, pair_width)

    return (
        layer_out,
        cache_rows,
        grad_tokens,
        extra[pair_width],
        extra[pair_width + 1],
        extra[pair_width + 2],
        extra[pair_width + 3],
        sum_query,
        sum_bias_query,
        keyval_weight_out,
        keyval_bias_out,
        sum_up,
        sum_bias_up,
        sum_output,
        bias_out_grad,
        sum_down,
        bias_out_grad,
    )


def solution(mesh):
    in_specs = (
        P(("seq", "row"), None),
        P(("seq", "row"), "col"),
        P(),
        P(),
        P("col"),
        P("col"),
        P("col"),
        P("col"),
        P("col", "row"),
        P("row"),
        P("col", None),
        P(),
        P("col", "row"),
        P("row"),
        P("row", "col"),
        P("col"),
        P("row", "col"),
        P("col"),
    )
    out_specs = (
        P(("seq", "row"), "col"),
        P(("seq", "col"), None),
        P(("seq", "row"), "col"),
        P("col"),
        P("col"),
        P("col"),
        P("col"),
        P("col", "row"),
        P("row"),
        P("col", "row"),
        P("row"),
        P("col", "row"),
        P("row"),
        P("row", "col"),
        P("col"),
        P("row", "col"),
        P("col"),
    )
    return jax.shard_map(
        on_device, mesh=mesh, in_specs=in_specs, out_specs=out_specs, check_vma=False
    )
```

```python
import collections
import functools

import jax
import jax.numpy as jnp
from jax import lax
from jax.experimental import pallas as pl
from jax.experimental.pallas import tpu as pltpu
from jax.sharding import PartitionSpec as P

HD = 64
ROT = 16
BLOCK = 512
LONGEST = 16
VMEM = 60 * 1024 * 1024
Shape = collections.namedtuple("Shape", "seq_count row_count sequences heads")
HALF = 256
EPS = 1e-05
NEGATIVE = -1e30
F32 = jnp.float32
BF16 = jnp.bfloat16

NN = (((1,), (0,)), ((), ()))
NT = (((1,), (1,)), ((), ()))
TN = (((0,), (0,)), ((), ()))


def dot(left, right, dims=NN):
    return lax.dot_general(left, right, dims, preferred_element_type=F32)


def swap(value, axis, bit):
    count = lax.axis_size(axis)
    return lax.ppermute(value, axis, [(i, i ^ bit) for i in range(count)])


def swap_odd_rows(value):
    seq_count, row_count = lax.axis_size("seq"), lax.axis_size("row")
    pairs = []
    for s in range(1, seq_count, 2):
        for r in range(row_count):
            pairs.append((s * row_count + r, s * row_count + (r ^ 2)))
    moved = lax.ppermute(value, ("seq", "row"), pairs)
    return jnp.where(lax.rem(lax.axis_index("seq"), 2) == 0, value, moved)


def swap_some(value, axis, bit, parity):
    sizes = [lax.axis_size(name) for name in ("seq", "row", "col")]
    pairs = []
    for s in range(parity, sizes[0], 2):
        for r in range(sizes[1]):
            for c in range(sizes[2]):
                index = {"seq": s, "row": r, "col": c}
                source = (s * sizes[1] + r) * sizes[2] + c
                index[axis] ^= bit
                pairs.append((source, (index["seq"] * sizes[1] + index["row"]) * sizes[2] + index["col"]))
    return lax.ppermute(value, ("seq", "row", "col"), pairs)


def swap_add(value, axis, bit):
    rounded = lax.reduce_precision(value, 8, 7)
    return rounded + swap(rounded.astype(BF16), axis, bit).astype(F32)


def split_rows(vector):
    high = lax.reduce_precision(vector, 8, 7)
    return high.astype(BF16), (vector - high).astype(BF16)


def first_of(meta_ref, block, shape):
    start = jnp.int32(0)
    first = jnp.int32(0)
    for i in range(shape.sequences):
        first = jnp.where(start <= block, start, first)
        start = start + meta_ref[3 + i] // BLOCK
    return first


def attention_kernel(
    meta_ref,
    first_ref,
    dy_ref,
    cos_ref,
    sin_ref,
    ff_out_ref,
    ff_grad_ref,
    vec_ref,
    small0_ref,
    small1_ref,
    stats_ref,
    kv0_ref,
    kv1_ref,
    *rest,
    shape,
):
    heads = shape.heads
    stay_ref, go_ref, keep_ref, send_ref, stat_ref, dkv_out_ref, dkv_low_ref, cache_ref = rest[:8]
    dqw_ref, dow_ref, dqb_ref = rest[8:11]
    rest = rest[11:]
    (
        qd_ref,
        probs_ref,
        high_ref,
        sums_ref,
        dots_ref,
        acc_ref,
        dq_ref,
        dkv_ref,
        kv_ref,
        low_ref,
        zero_ref,
        qw_ref,
        ow_ref,
        copy_sem,
        late_sem,
    ) = rest
    blocks = kv_ref.shape[0]
    half = blocks // 2
    slot = pl.program_id(0)
    lanes = 2 * HD
    rows = heads * HALF
    seq, row, second_half = meta_ref[0], meta_ref[1], meta_ref[2]
    own_block = lax.bitwise_xor(seq, slot // 2) * shape.row_count + lax.bitwise_xor(row, slot % 2)
    first_block = first_of(meta_ref, own_block, shape)
    before = own_block - first_block

    def slot_of(block):
        apart_row = lax.bitwise_xor(lax.rem(block, shape.row_count), row)
        apart_seq = lax.bitwise_xor(block // shape.row_count, seq)
        return apart_row + shape.row_count * (
            apart_seq // 2 + (shape.seq_count // 2) * lax.rem(apart_seq, 2)
        )

    def put(index, rows):
        @pl.when(slot < 2)
        def _():
            stay_ref[slot, index] = rows

        @pl.when(slot >= 2)
        def _():
            go_ref[slot - 2, index] = rows.astype(BF16)

    def cache_copies(dealt, group):
        copies = []
        for i in range(dealt):
            owner = meta_ref[3 + shape.sequences + group * dealt + i]
            for part in (0, 1):
                take = jnp.where(second_half > 0, 1 - part, part) * HALF
                copies.append(
                    pltpu.make_async_copy(
                        kv_ref.at[slot_of(owner), pl.ds(take, HALF), :],
                        cache_ref.at[i, part * HALF : (part + 1) * HALF, :],
                        copy_sem.at[2 + 2 * i + part],
                    )
                )
        return copies

    pieces = [
        pltpu.make_async_copy(piece, kv_ref.at[i * half : (i + 1) * half], copy_sem.at[i])
        for i, piece in enumerate((kv0_ref, kv1_ref))
    ]
    late = [
        pltpu.make_async_copy(zero_ref, dkv_ref.at[i : i + 1], late_sem.at[i]) for i in range(blocks)
    ]

    @pl.when(slot == 0)
    def _():
        for copy in pieces:
            copy.start()
        zero_ref[...] = jnp.zeros_like(zero_ref)
        dqw_ref[...] = jnp.zeros_like(dqw_ref)
        dow_ref[...] = jnp.zeros_like(dow_ref)
        dqb_ref[...] = jnp.zeros_like(dqb_ref)
        for copy in late:
            copy.start()
        span = small0_ref.shape[1]
        count = heads * HD
        for i, small in enumerate((small0_ref, small1_ref)):
            part = slice(i * span, (i + 1) * span)
            qw_ref[:count, part] = small[:count, :]
            ow_ref[:count, part] = small[count : 2 * count, :]
        qw_ref[count:, :] = jnp.zeros_like(qw_ref[count:, :])
        ow_ref[count:, :] = jnp.zeros_like(ow_ref[count:, :])

    cosine = cos_ref[0]
    sine = sin_ref[0]
    lane = lax.broadcasted_iota(jnp.int32, (HALF, lanes), 1)
    front = lane < HD

    def rolled(values):
        return jnp.where(
            lane < ROT // 2,
            pltpu.roll(values, lanes - ROT // 2, 1),
            pltpu.roll(values, ROT // 2, 1),
        )

    def head_of(joined, h):
        return joined[:, (h // 2) * lanes : (h // 2 + 1) * lanes]

    def join(parts):
        tiles = []
        for h in range(0, heads, 2):
            other = parts[h + 1] if h + 1 < heads else jnp.zeros_like(parts[h])
            tiles.append(jnp.where(front, parts[h], other))
        return jnp.concatenate(tiles, axis=1)

    padded = qw_ref.shape[0]
    base = 2 * heads * HD + 7
    query_b = (
        small0_ref[base : base + 1, :padded].astype(F32)
        + small0_ref[base + 8 : base + 9, :padded].astype(F32)
    )
    pre_all = dot(first_ref[0], qw_ref[...], NT) + query_b
    d_all = dot(dy_ref[0], ow_ref[...], NT)
    for h in range(heads):
        pre = head_of(pre_all, h)
        grad = head_of(d_all, h)
        if h % 2:
            pre = pltpu.roll(pre, HD, 1)
        else:
            grad = pltpu.roll(grad, HD, 1)
        turned = jnp.where(front, pre * cosine + rolled(pre) * sine, 0.0)
        mine = slice(h * HALF, (h + 1) * HALF)
        qd_ref[mine, :] = turned.astype(BF16) * BF16(HD**-0.5)
        qd_ref[rows + h * HALF : rows + (h + 1) * HALF, :] = jnp.where(front, 0.0, grad).astype(BF16)

    @pl.when(slot == 0)
    def _():
        for copy in pieces:
            copy.wait()

    high_ref[...] = jnp.full_like(high_ref, NEGATIVE)
    sums_ref[...] = jnp.zeros_like(sums_ref)

    def block_at(step):
        return slot_of(first_block + step)

    def weigh(step, mask):
        scores = dot(kv_ref[block_at(step)], qd_ref[:rows, :], NT)
        if mask:
            row_in = lax.rem(lax.broadcasted_iota(jnp.int32, (BLOCK, rows), 1), HALF)
            key_in = lax.broadcasted_iota(jnp.int32, (BLOCK, rows), 0)
            limit = jnp.where(second_half > 0, BLOCK, 0)
            keep = (key_in <= row_in) | ((key_in >= HALF) & (key_in < limit))
            scores = jnp.where(keep, scores, NEGATIVE)
        high = jnp.max(scores, axis=0, keepdims=True)
        probs = jnp.exp(scores - high)
        probs_ref[step] = probs.astype(BF16)
        high_ref[pl.ds(step, 1), :] = high
        sums_ref[pl.ds(step, 1), :] = jnp.sum(probs, axis=0, keepdims=True)

    weigh(before, True)
    lax.fori_loop(0, before, lambda step, c: (weigh(step, False), c)[1], 0)

    share = jnp.exp(high_ref[...] - jnp.max(high_ref[...], axis=0, keepdims=True))
    high_ref[...] = share / jnp.sum(share * sums_ref[...], axis=0, keepdims=True)

    def mix(step, first):
        probs = (probs_ref[step].astype(F32) * high_ref[pl.ds(step, 1), :]).astype(BF16)
        probs_ref[step] = probs
        part = dot(probs, kv_ref[block_at(step)], TN)
        if first:
            acc_ref[...] = part
        else:
            acc_ref[...] += part

    mix(before, True)
    lax.fori_loop(0, before, lambda step, c: (mix(step, False), c)[1], 0)

    @pl.when(slot == 0)
    def _():
        for copy in late:
            copy.wait()

    parts = []
    for h in range(heads):
        mine = slice(h * HALF, (h + 1) * HALF)
        mixed = acc_ref[mine, :]
        grad = qd_ref[rows + h * HALF : rows + (h + 1) * HALF, :].astype(F32)
        dots_ref[:, mine] = jnp.sum(jnp.transpose(mixed * grad), axis=0, keepdims=True)
        parts.append(mixed if h % 2 else pltpu.roll(mixed, HD, 1))
    joined = join(parts).astype(BF16)
    put(0, ff_out_ref[0] + dot(joined, ow_ref[...]))
    dow_ref[...] += dot(joined, dy_ref[0], TN)

    def backward(step, first):
        where = block_at(step)
        block = kv_ref[where]
        probs = probs_ref[step]
        grad_probs = dot(block, qd_ref[rows:, :], NT)
        grad_scores = (probs.astype(F32) * (grad_probs - dots_ref[...])).astype(BF16)
        total = dot(jnp.concatenate([grad_scores, probs], axis=1), qd_ref[...])
        grad_q = dot(grad_scores, block, TN)
        if first:
            dq_ref[...] = grad_q
        else:
            dq_ref[...] += grad_q
        dkv_ref[where] = (dkv_ref[where].astype(F32) + total).astype(dkv_ref.dtype)

    backward(before, True)
    lax.fori_loop(0, before, lambda step, c: (backward(step, False), c)[1], 0)

    parts = []
    for h in range(heads):
        part = dq_ref[h * HALF : (h + 1) * HALF, :] * (HD**-0.5)
        part = part * cosine - rolled(part) * sine
        parts.append(pltpu.roll(part, HD, 1) if h % 2 else part)
    joined = join(parts)
    dqb_ref[...] += jnp.sum(joined, axis=0, keepdims=True)
    joined = joined.astype(BF16)
    put(1, ff_grad_ref[0] + dot(joined, qw_ref[...]) * vec_ref[0:1, :])
    dqw_ref[...] += dot(joined, first_ref[0], TN)

    @pl.when(slot == 0)
    def _():
        dealt = cache_ref.shape[0]
        group = seq * 2 + second_half
        for copy in cache_copies(dealt, group):
            copy.start()

    @pl.when(slot == 3)
    def _():
        copies = [pltpu.make_async_copy(dkv_ref.at[:half], dkv_out_ref, copy_sem.at[0])]
        copies[0].start()
        if dkv_ref.dtype == BF16:
            copies.append(pltpu.make_async_copy(dkv_ref.at[half:], dkv_low_ref, copy_sem.at[1]))
        else:
            low_ref[...] = dkv_ref[half:].astype(BF16)
            copies.append(pltpu.make_async_copy(low_ref, dkv_low_ref, copy_sem.at[1]))
        copies[1].start()
        copies += cache_copies(cache_ref.shape[0], seq * 2 + second_half)
        count = heads * HD
        span = small0_ref.shape[1]
        bias_up = stats_ref[2:3, :]
        bias_q = dqb_ref[...]
        for i, target in enumerate((keep_ref, send_ref)):
            part = slice(i * span, (i + 1) * span)
            target[:count, :] = dqw_ref[:count, part].astype(BF16)
            target[count : 2 * count, :] = dow_ref[:count, part].astype(BF16)
            rows_of = jnp.concatenate(
                [
                    bias_up[:, :span],
                    bias_up[:, span:],
                    jnp.concatenate([bias_q, jnp.zeros((1, span - padded), F32)], axis=1),
                    jnp.zeros((5, span), F32),
                ],
                axis=0,
            )
            target[2 * count :, :] = jnp.concatenate(
                [rows_of, jnp.zeros((target.shape[0] - 2 * count - 8, span), F32)], axis=0
            ).astype(BF16)
        weight = qw_ref[...].astype(F32)
        column = jnp.transpose(jnp.broadcast_to(bias_q, (8, padded)))[:, 0:1]
        plain = jnp.sum(weight * column, axis=0, keepdims=True)
        stat_ref[0:1, :] = (
            jnp.sum(weight * dqw_ref[...], axis=0, keepdims=True) - vec_ref[1:2, :] * plain
        ) / vec_ref[0:1, :]
        stat_ref[1:2, :] = plain
        stat_ref[2:8, :] = jnp.zeros((6, 2 * span), F32)
        for copy in copies:
            copy.wait()


def attention(meta, first_in, dy, cosine, sine, ff, vectors, small, stats, pieces, shape):
    _, _, width = first_in.shape
    half = pieces[0].shape[0]
    blocks = 2 * half
    lanes = 2 * HD
    heads = shape.heads
    padded = -(-heads // 2) * lanes
    rows = heads * HALF
    longest = min(LONGEST, blocks // 2)
    total_type = F32 if blocks <= 32 else BF16
    dealt = blocks // (2 * shape.seq_count)

    def per_slot(lanes):
        return pl.BlockSpec((1, HALF, lanes), lambda i, m: (i, 0, 0))

    def whole(array):
        return pl.BlockSpec(
            array.shape, lambda i, m: (0,) * len(array.shape), pipeline_mode=pl.Buffered(buffer_count=1)
        )

    far = pl.BlockSpec(memory_space=pltpu.MemorySpace.HBM)
    arrays = [first_in, dy, cosine, sine, *ff, vectors, *small, stats, *pieces]
    in_specs = [per_slot(width), per_slot(width), per_slot(lanes), per_slot(lanes)]
    in_specs += [per_slot(width)] * 2 + [whole(a) for a in (vectors, *small, stats)] + [far] * 2
    part = jax.ShapeDtypeStruct((2 * heads * HD + 32, width // 2), BF16)
    results = [
        jax.ShapeDtypeStruct((2, 2, HALF, width), F32),
        jax.ShapeDtypeStruct((2, 2, HALF, width), BF16),
        part,
        part,
        jax.ShapeDtypeStruct((8, width), F32),
    ]
    out_shape = [
        *results,
        jax.ShapeDtypeStruct((half, BLOCK, lanes), total_type),
        jax.ShapeDtypeStruct((half, BLOCK, lanes), BF16),
        jax.ShapeDtypeStruct((dealt, BLOCK, lanes), BF16),
    ]
    out_specs = [whole(a) for a in results] + [far] * 3
    return pl.pallas_call(
        functools.partial(attention_kernel, shape=shape),
        grid_spec=pltpu.PrefetchScalarGridSpec(
            num_scalar_prefetch=1,
            grid=(4,),
            in_specs=in_specs,
            out_specs=out_specs,
            scratch_shapes=[
                pltpu.VMEM((padded, width), F32),
                pltpu.VMEM((padded, width), F32),
                pltpu.VMEM((1, padded), F32),
                pltpu.VMEM((2 * rows, lanes), BF16),
                pltpu.VMEM((longest, BLOCK, rows), BF16),
                pltpu.VMEM((longest, rows), F32),
                pltpu.VMEM((longest, rows), F32),
                pltpu.VMEM((1, rows), F32),
                pltpu.VMEM((rows, lanes), F32),
                pltpu.VMEM((rows, lanes), F32),
                pltpu.VMEM((blocks, BLOCK, lanes), total_type),
                pltpu.VMEM((blocks, BLOCK, lanes), BF16),
                pltpu.VMEM((half if blocks <= 32 else 1, BLOCK, lanes), BF16),
                pltpu.VMEM((1, BLOCK, lanes), total_type),
                pltpu.VMEM((padded, width), BF16),
                pltpu.VMEM((padded, width), BF16),
                pltpu.SemaphoreType.DMA((2 + 2 * dealt,)),
                pltpu.SemaphoreType.DMA((blocks,)),
            ],
        ),
        out_shape=out_shape,
        cost_estimate=pl.CostEstimate(
            flops=24_000_000_000, bytes_accessed=30_000_000, transcendentals=30_000_000
        ),
        compiler_params=pltpu.CompilerParams(
            vmem_limit_bytes=67_043_328 if blocks > 32 else VMEM
        ),
        name="attention",
    )(meta, *arrays)


ORDER = (0, 1, 2, 3)


def tables_kernel(meta_ref, cos_ref, sin_ref, *, shape):
    seq, row, col = meta_ref[0], meta_ref[1], meta_ref[2]
    lane = lax.broadcasted_iota(jnp.int32, (HALF, 2 * HD), 1)
    inside = lax.broadcasted_iota(jnp.int32, (HALF, 2 * HD), 0)
    half_rot = ROT // 2
    exponent = lax.rem(lane, half_rot).astype(F32) * (1.0 / half_rot)
    frequency = jnp.where(lane < ROT, 1.0 / jnp.exp(exponent * jnp.log(jnp.full_like(exponent, 10000.0))), 0.0)
    for i, (slot, half) in enumerate([(slot, col) for slot in ORDER] + [(0, 1 - col)]):
        block = lax.bitwise_xor(seq, slot // 2) * shape.row_count + lax.bitwise_xor(row, slot % 2)
        start = (block - first_of(meta_ref, block, shape)) * BLOCK
        angles = (inside + (start + half * HALF)).astype(F32) * frequency
        cos_ref[i] = jnp.cos(angles)
        turned = jnp.sin(angles)
        sin_ref[i] = jnp.where(lane < half_rot, -turned, jnp.where(lane < ROT, turned, 0.0))


def tables(meta, shape):
    table = jax.ShapeDtypeStruct((5, HALF, 2 * HD), F32)
    return pl.pallas_call(
        functools.partial(tables_kernel, shape=shape),
        in_specs=[pl.BlockSpec(memory_space=pltpu.SMEM)],
        out_specs=[pl.BlockSpec(memory_space=pltpu.VMEM)] * 2,
        out_shape=[table, table],
        name="tables",
    )(meta)


def forward_kernel(
    meta_ref,
    both0_ref,
    both1_ref,
    both2_ref,
    both3_ref,
    vec_ref,
    pack_ref,
    even_ref,
    z_ref,
    x_got_ref,
    odd0_ref,
    odd1_ref,
    first_ref,
    dy_ref,
    out_ref,
    dx_ref,
    grads_ref,
    stat_ref,
    small0_ref,
    small1_ref,
    x_ref,
    own_ref,
    other_ref,
    up_ref,
    down_ref,
    second_ref,
    hidden_ref,
    grad_ref,
    dys_ref,
    bias_ref,
    sem,
):
    step = pl.program_id(0)
    span = pack_ref.shape[1]
    total = pack_ref.shape[0]
    here = pl.ds(pl.multiple_of(step * HALF, HALF), HALF)
    core = lax.rem(meta_ref[0], 2)
    side = lax.rem(meta_ref[0] // 2, 2)

    def run(copies):
        for copy in copies:
            copy.start()
        for copy in copies:
            copy.wait()

    @pl.when((step == 0) & (core == 0))
    def _():
        run(
            [
                pltpu.make_async_copy(pack_ref, own_ref, sem.at[0]),
                pltpu.make_async_copy(even_ref, other_ref, sem.at[1]),
            ]
        )

    @pl.when((step == 0) & (core == 1))
    def _():
        half = total // 2
        near = pl.ds(pl.multiple_of(side * half, half), half)
        far = pl.ds(pl.multiple_of((1 - side) * half, half), half)
        run(
            [
                pltpu.make_async_copy(z_ref, own_ref.at[near, :], sem.at[0]),
                pltpu.make_async_copy(x_got_ref, own_ref.at[far, :], sem.at[1]),
                pltpu.make_async_copy(odd0_ref, other_ref.at[near, :], sem.at[2]),
                pltpu.make_async_copy(odd1_ref, other_ref.at[far, :], sem.at[3]),
            ]
        )

    @pl.when(step == 0)
    def _():
        base = small0_ref.shape[0]
        for i, held in enumerate((own_ref, other_ref)):
            part = slice(i * span, (i + 1) * span)
            (small0_ref, small1_ref)[i][...] = held[:base, :]
            up_ref[part, :span] = held[base : base + span, :]
            up_ref[part, span:] = held[base + span : base + 2 * span, :]
            down_ref[:, part] = held[base + 2 * span : base + 4 * span, :]
        bias_ref[...] = jnp.zeros_like(bias_ref)

    for i, piece in enumerate((both0_ref, both1_ref, both2_ref, both3_ref)):

        @pl.when(step == i)
        def _():
            x_ref[...] = piece[0]
            dys_ref[here, :] = piece[1]

    base = small0_ref.shape[0] - 32
    bias = own_ref[base : base + 8, :].astype(F32) + own_ref[base + 8 : base + 16, :].astype(F32)
    upward_b = jnp.concatenate([bias[5:6], bias[6:7]], axis=1)
    wide = x_ref[...].astype(F32)
    mean = jnp.mean(wide, axis=1, keepdims=True)
    spread = jnp.mean(wide * wide, axis=1, keepdims=True) - mean * mean
    normed = (wide - mean) * lax.rsqrt(spread + EPS)
    first_ref[0] = (normed * vec_ref[0:1, :] + vec_ref[1:2, :]).astype(BF16)
    second = (normed * vec_ref[2:3, :] + vec_ref[3:4, :]).astype(BF16)
    dy = dys_ref[here, :]
    dy_ref[0] = dy
    second_ref[here, :] = second
    upward = dot(second, up_ref[...]) + upward_b
    bell = lax.erf(upward * (2.0**-0.5)) * 0.5 + 0.5
    hidden = (upward * bell).astype(BF16)
    slope = bell + upward * jnp.exp(upward * upward * -0.5) * ((2.0 * 3.141592653589793) ** -0.5)
    grad = dot(dy, down_ref[...], NT) * slope
    bias_ref[0:1, :] += jnp.sum(grad, axis=0, keepdims=True)
    grad = grad.astype(BF16)
    hidden_ref[here, :] = hidden
    grad_ref[here, :] = grad
    out_ref[0] = dot(hidden, down_ref[...])
    dx_ref[0] = dot(grad, up_ref[...], NT) * vec_ref[2:3, :]

    @pl.when(step == 3)
    def _():
        down_grad = dot(hidden_ref[...], dys_ref[...], TN)
        grads_ref[0, 2 * span :, :] = down_grad[:, :span].astype(BF16)
        grads_ref[1, 2 * span :, :] = down_grad[:, span:].astype(BF16)
        up_grad = dot(second_ref[...], grad_ref[...], TN)
        for i in (0, 1):
            part = slice(i * span, (i + 1) * span)
            grads_ref[0, part, :] = up_grad[:span, part].astype(BF16)
            grads_ref[1, part, :] = up_grad[span:, part].astype(BF16)
        weight = up_ref[...].astype(F32)
        bias_grad = bias_ref[0:1, :]

        def as_row(values):
            column = jnp.sum(values, axis=1, keepdims=True)
            return jnp.transpose(jnp.broadcast_to(column, (2 * span, 128)))[0:1, :]

        plain = as_row(weight * bias_grad)
        stat_ref[0:1, :] = (as_row(weight * up_grad) - vec_ref[3:4, :] * plain) / vec_ref[2:3, :]
        stat_ref[1:2, :] = plain
        stat_ref[2:3, :] = bias_grad
        stat_ref[3:8, :] = jnp.zeros((5, 2 * span), F32)


def feed_forward(meta, both, vectors, weights, small_rows):
    width = vectors.shape[1]
    span = width // 2
    total = weights[0].shape[0]

    def whole(array):
        return pl.BlockSpec(
            array.shape, lambda i: (0,) * len(array.shape), pipeline_mode=pl.Buffered(buffer_count=1)
        )

    slot = pl.BlockSpec((1, HALF, width), lambda i: (i, 0, 0))
    arrays = [*both, vectors]
    grads = jax.ShapeDtypeStruct((2, 4 * span, span), BF16)
    stat = jax.ShapeDtypeStruct((8, width), F32)
    small = jax.ShapeDtypeStruct((small_rows, span), BF16)
    tokens = lambda kind: jax.ShapeDtypeStruct((4, HALF, width), kind)
    return pl.pallas_call(
        forward_kernel,
        grid=(4,),
        in_specs=[pl.BlockSpec(memory_space=pltpu.SMEM)]
        + [whole(a) for a in arrays]
        + [pl.BlockSpec(memory_space=pltpu.MemorySpace.HBM)] * len(weights),
        out_specs=[slot] * 4 + [whole(grads), whole(stat), whole(small), whole(small)],
        out_shape=[tokens(BF16), tokens(BF16), tokens(F32), tokens(F32), grads, stat, small, small],
        scratch_shapes=[
            pltpu.VMEM((HALF, width), BF16),
            pltpu.VMEM((total, span), BF16),
            pltpu.VMEM((total, span), BF16),
            pltpu.VMEM((width, width), BF16),
            pltpu.VMEM((width, width), BF16),
            pltpu.VMEM((4 * HALF, width), BF16),
            pltpu.VMEM((4 * HALF, width), BF16),
            pltpu.VMEM((4 * HALF, width), BF16),
            pltpu.VMEM((4 * HALF, width), BF16),
            pltpu.VMEM((8, width), F32),
            pltpu.SemaphoreType.DMA((4,)),
        ],
        cost_estimate=pl.CostEstimate(
            flops=7_000_000_000, bytes_accessed=20_000_000, transcendentals=3_000_000
        ),
        compiler_params=pltpu.CompilerParams(vmem_limit_bytes=VMEM),
        name="feed_forward",
    )(meta, *arrays, *weights)


def prologue_kernel(
    where_ref, tokens_ref, dy_ref, kvw_ref, vec_ref, pack_ref, x_ref, mine_ref
):
    col = where_ref[2]
    span = dy_ref.shape[1]
    width = tokens_ref.shape[1]
    here = pl.ds(pl.multiple_of(col * HALF, HALF), HALF)
    there = pl.ds(pl.multiple_of((1 - col) * HALF, HALF), HALF)
    pack_ref[:HALF, :] = dy_ref[there, :]
    base = HALF + 2 * HD
    pack_ref[HALF:base, :] = jnp.transpose(kvw_ref[...].astype(F32)).astype(BF16)
    vectors = vec_ref[...]
    high = vectors.astype(BF16).astype(F32)
    both = jnp.concatenate([high, vectors - high], axis=0).astype(BF16)
    pack_ref[base:, :] = both
    for i, rows in enumerate((here, there)):
        part = slice(i * HALF, (i + 1) * HALF)
        x_ref[part, :span] = tokens_ref[rows, pl.ds(pl.multiple_of(col * span, 128), span)]
        x_ref[part, span:] = tokens_ref[rows, pl.ds(pl.multiple_of((1 - col) * span, 128), span)]
    mine_ref[...] = dy_ref[here, :]


def prologue(meta, tokens, cotangent, keyval_weight, vectors):
    width = tokens.shape[1]
    span = width // 2
    rows = vectors.shape[0]
    vmem = pl.BlockSpec(memory_space=pltpu.VMEM)
    return pl.pallas_call(
        prologue_kernel,
        in_specs=[pl.BlockSpec(memory_space=pltpu.SMEM)] + [vmem] * 4,
        out_specs=[vmem] * 3,
        out_shape=[
            jax.ShapeDtypeStruct((HALF + 2 * HD + 2 * rows, span), BF16),
            jax.ShapeDtypeStruct((2 * HALF, width), BF16),
            jax.ShapeDtypeStruct((HALF, span), BF16),
        ],
        name="prologue",
    )(meta, tokens, cotangent, keyval_weight, vectors)


def weights_kernel(where_ref, qw_ref, ow_ref, up_ref, down_ref, vec_ref, pack_ref, part_ref):
    count = qw_ref.shape[0]
    span = pack_ref.shape[1]
    total = pack_ref.shape[0]
    vectors = vec_ref[...]
    high = vectors.astype(BF16).astype(F32)
    both = jnp.concatenate([high, vectors - high], axis=0).astype(BF16)
    pack_ref[:count, :] = qw_ref[...]
    pack_ref[count : 2 * count, :] = ow_ref[...]
    pack_ref[2 * count : 2 * count + 16, :] = both
    pack_ref[2 * count + 16 : 2 * count + 32, :] = jnp.zeros((16, span), BF16)
    base = 2 * count + 32
    pack_ref[base : base + span, :] = up_ref[:, :span]
    pack_ref[base + span : base + 2 * span, :] = up_ref[:, span:]
    pack_ref[base + 2 * span :, :] = down_ref[...]
    side = lax.rem(where_ref[0] // 2, 2)
    part_ref[...] = pack_ref[pl.ds(pl.multiple_of(side * (total // 2), 16), total // 2), :]


def pack_weights(meta, query_t, output_weight, upward_weight, down_weight, vectors):
    span = output_weight.shape[1]
    total = 2 * query_t.shape[0] + 32 + 2 * upward_weight.shape[0] + down_weight.shape[0]
    vmem = pl.BlockSpec(memory_space=pltpu.VMEM)
    return pl.pallas_call(
        weights_kernel,
        in_specs=[pl.BlockSpec(memory_space=pltpu.SMEM)] + [vmem] * 5,
        out_specs=[vmem] * 2,
        out_shape=[
            jax.ShapeDtypeStruct((total, span), BF16),
            jax.ShapeDtypeStruct((total // 2, span), BF16),
        ],
        name="pack_weights",
    )(meta, query_t, output_weight, upward_weight, down_weight, vectors)


def own_kernel(
    x_ref, mine_ref, pack_ref, got_ref, vec_ref, cos_ref, sin_ref, bias_ref, pair_ref, both_ref, kvw_ref, full_ref
):
    span = mine_ref.shape[1]
    rows = vec_ref.shape[0]
    base = HALF + 2 * HD
    other = got_ref[base : base + 2 * rows, :].astype(F32)
    full = jnp.concatenate([vec_ref[...], other[:rows] + other[rows:]], axis=1)
    full_ref[...] = full
    both_ref[0] = x_ref[:HALF, :]
    both_ref[1, :, :span] = mine_ref[...]
    both_ref[1, :, span:] = got_ref[:HALF, :]
    kvw_ref[:, :span] = pack_ref[HALF:base, :]
    kvw_ref[:, span:] = got_ref[HALF:base, :]
    wide = x_ref[...].astype(F32)
    mean = jnp.mean(wide, axis=1, keepdims=True)
    spread = jnp.mean(wide * wide, axis=1, keepdims=True) - mean * mean
    normed = (wide - mean) * lax.rsqrt(spread + EPS)
    first = (normed * full[0:1, :] + full[1:2, :]).astype(BF16)
    pre_all = dot(first, kvw_ref[...], NT) + bias_ref[...]
    lanes = pre_all.shape[1]
    lane = lax.broadcasted_iota(jnp.int32, (HALF, lanes), 1)
    for i in (0, 1):
        pre = pre_all[i * HALF : (i + 1) * HALF, :]
        rolled = jnp.where(
            lane < ROT // 2, pltpu.roll(pre, lanes - ROT // 2, 1), pltpu.roll(pre, ROT // 2, 1)
        )
        pair_ref[0, i * HALF : (i + 1) * HALF, :] = (
            pre * cos_ref[4 * i] + rolled * sin_ref[4 * i]
        ).astype(BF16)


def own_pairs(x_own, mine, pack, got, vectors, cosine, sine, bias):
    width = x_own.shape[1]
    vmem = pl.BlockSpec(memory_space=pltpu.VMEM)
    return pl.pallas_call(
        own_kernel,
        in_specs=[vmem] * 8,
        out_specs=[vmem] * 4,
        out_shape=[
            jax.ShapeDtypeStruct((1, 2 * HALF, 2 * HD), BF16),
            jax.ShapeDtypeStruct((2, HALF, width), BF16),
            jax.ShapeDtypeStruct((2 * HD, width), BF16),
            jax.ShapeDtypeStruct((vectors.shape[0], width), F32),
        ],
        name="own_pairs",
    )(x_own, mine, pack, got, vectors, cosine, sine, bias)


def pairs_kernel(
    keep_ref, got_ref, cos_ref, sin_ref, first_ref, kvw_ref, vec_ref, stat_ref, ff_ref, dys_ref, mine_ref, send_ref
):
    span = mine_ref.shape[1]
    lanes = 2 * HD
    lane = lax.broadcasted_iota(jnp.int32, (HALF, lanes), 1)
    total = keep_ref[...] + got_ref[...].astype(F32)
    weight = jnp.zeros((lanes, 2 * span), F32)
    bias = jnp.zeros((1, lanes), F32)
    for i in (0, 1):
        part = total[i]
        rolled = jnp.where(
            lane < ROT // 2, pltpu.roll(part, lanes - ROT // 2, 1), pltpu.roll(part, ROT // 2, 1)
        )
        turned = part * cos_ref[i] - rolled * sin_ref[i]
        bias = bias + jnp.sum(turned, axis=0, keepdims=True)
        weight = weight + dot(turned.astype(BF16), first_ref[i], TN)
    kvw = kvw_ref[...].astype(F32)
    column = jnp.transpose(jnp.broadcast_to(bias, (8, lanes)))[:, 0:1]
    plain = jnp.sum(kvw * column, axis=0, keepdims=True)
    gain = (jnp.sum(kvw * weight, axis=0, keepdims=True) - vec_ref[1:2, :] * plain) / vec_ref[0:1, :]
    fill = jnp.zeros((1, span - lanes), F32)
    bias = jnp.concatenate([bias.astype(BF16).astype(F32), fill], axis=1)
    for i, target in enumerate((mine_ref, send_ref)):
        part = slice(i * span, (i + 1) * span)
        target[:lanes, :] = weight[:, part].astype(target.dtype)
        rows = jnp.concatenate(
            [
                stat_ref[0:1, part] + gain[:, part],
                stat_ref[1:2, part] + plain[:, part],
                ff_ref[0:2, part],
                bias,
                dys_ref[...] if i == 0 else jnp.zeros((1, span), F32),
                jnp.zeros((10, span), F32),
            ],
            axis=0,
        )
        target[lanes:, :] = rows.astype(target.dtype)


def pair_sums(keep, got, cosine, sine, first_in, keyval, vectors, stats, ff_stats, dy_sum):
    width = keyval.shape[1]
    vmem = pl.BlockSpec(memory_space=pltpu.VMEM)
    return pl.pallas_call(
        pairs_kernel,
        grid=(1,),
        in_specs=[vmem, vmem, head(cosine, 2), head(sine, 2), head(first_in, 2)] + [vmem] * 5,
        out_specs=[vmem] * 2,
        out_shape=[
            jax.ShapeDtypeStruct((2 * HD + 16, width // 2), F32),
            jax.ShapeDtypeStruct((2 * HD + 16, width // 2), BF16),
        ],
        name="pair_sums",
    )(keep, got, cosine, sine, first_in, keyval, vectors, stats, ff_stats, dy_sum)


def rows_kernel(
    own_ref,
    got_ref,
    cos_ref,
    sin_ref,
    kvw_ref,
    vec_ref,
    x_ref,
    dy_ref,
    keep_ref,
    core_ref,
    back_ref,
    mine_ref,
    send_ref,
):
    span = mine_ref.shape[2]
    lanes = 2 * HD
    lane = lax.broadcasted_iota(jnp.int32, (HALF, lanes), 1)
    part = own_ref[0] + got_ref[...].astype(F32)
    rolled = jnp.where(
        lane < ROT // 2, pltpu.roll(part, lanes - ROT // 2, 1), pltpu.roll(part, ROT // 2, 1)
    )
    turned = (part * cos_ref[0] - rolled * sin_ref[0]).astype(BF16)
    wide = x_ref[:HALF, :].astype(F32)
    mean = jnp.mean(wide, axis=1, keepdims=True)
    spread = jnp.mean(wide * wide, axis=1, keepdims=True) - mean * mean
    root = lax.rsqrt(spread + EPS)
    normed = (wide - mean) * root
    grad = keep_ref[0, 1] + core_ref[0, 1].astype(F32) + back_ref[1].astype(F32) + dot(turned, kvw_ref[...]) * vec_ref[0:1, :]
    one = jnp.mean(grad, axis=1, keepdims=True)
    two = jnp.mean(grad * normed, axis=1, keepdims=True)
    grad = dy_ref[0].astype(F32) + root * (grad - one - normed * two)
    out = wide + keep_ref[0, 0] + core_ref[0, 0].astype(F32) + back_ref[0].astype(F32) + vec_ref[4:5, :]
    for i, rows in enumerate((out.astype(BF16), grad.astype(BF16))):
        mine_ref[i] = rows[:, :span]
        send_ref[i] = rows[:, span:]


def head(array, count):
    rank = len(array.shape)
    return pl.BlockSpec((count,) + array.shape[1:], lambda i: (0,) * rank)


def own_rows(own, got, cosine, sine, keyval, vectors, x_block, dy, keep, core, back):
    width = keyval.shape[1]
    vmem = pl.BlockSpec(memory_space=pltpu.VMEM)
    half = jax.ShapeDtypeStruct((2, HALF, width // 2), BF16)
    return pl.pallas_call(
        rows_kernel,
        grid=(1,),
        in_specs=[vmem, vmem, head(cosine, 1), head(sine, 1), vmem, vmem, head(x_block, HALF)]
        + [head(dy, 1), head(keep, 1), head(core, 1), vmem],
        out_specs=[vmem] * 2,
        out_shape=[half, half],
        name="own_rows",
    )(own, got, cosine, sine, keyval, vectors, x_block, dy, keep, core, back)


def after(value, *others):
    return lax.optimization_barrier((value,) + others)[0]


def on_device(
    tokens,
    cotangent,
    lengths,
    block_order,
    attention_gain,
    attention_shift,
    feedforward_gain,
    feedforward_shift,
    query_weight,
    query_bias,
    keyval_weight,
    keyval_bias,
    upward_weight,
    upward_bias,
    output_weight,
    output_bias,
    down_weight,
    down_bias,
):
    seq_count = lax.axis_size("seq")
    row_count = lax.axis_size("row")
    col_count = lax.axis_size("col")
    seq_me = lax.axis_index("seq")
    row_me = lax.axis_index("row")
    col_me = lax.axis_index("col")
    block_total = block_order.shape[0]
    width = tokens.shape[1]
    span = width // 2
    heads = query_weight.shape[1] // HD
    head_width = heads * HD
    pair_width = 2 * HD

    shape = Shape(seq_count, row_count, lengths.shape[0], heads)
    meta = jnp.concatenate(
        [jnp.stack([seq_me, row_me, col_me]).astype(jnp.int32), lengths, block_order]
    )

    vectors = jnp.concatenate(
        [
            attention_gain,
            attention_shift,
            feedforward_gain,
            feedforward_shift,
            output_bias + down_bias,
            upward_bias,
            query_bias,
            jnp.zeros((span - head_width,), F32),
        ]
    ).reshape(8, span)
    pack, x_block, dy_mine = prologue(meta, tokens, cotangent, keyval_weight, vectors)
    received = swap(pack, "col", 1)
    weights, weights_half = pack_weights(
        after(meta, pack), jnp.transpose(query_weight), output_weight, upward_weight, down_weight, vectors
    )
    weights_z = swap_some(weights_half, "row", 2, 1)
    weights_even = swap_some(after(weights, received), "col", 1, 0)
    cosine, sine = tables(after(meta, weights), shape)

    pairs, both, keyval_full, vec_full = own_pairs(
        x_block, dy_mine, pack, received, vectors, cosine, sine, keyval_bias[None]
    )
    steps = [("row", 1), ("row", 2)]
    bit = 2
    while bit < seq_count:
        steps.append(("seq", bit))
        bit = bit * 2
    got = swap(pairs, "row", 1)
    weights_x = swap_some(after(weights_z, got), "seq", 2, 1)
    weights_odd0 = swap_some(after(weights_z, got), "col", 1, 1)
    both_got = swap(after(both, got), "row", 1)
    pairs = jnp.concatenate([pairs, got], axis=0)
    got = swap(pairs, "row", 2)
    weights_odd1 = swap_some(after(weights_x, got), "col", 1, 1)
    got = after(got, weights_x, weights_odd0, weights_even)
    for axis, bit in steps[2:]:
        pairs = jnp.concatenate([pairs, got], axis=0)
        got = swap(pairs, axis, bit)
    got = after(got, weights_odd1, both_got)
    both_two = swap(after(both, got), "seq", 1)
    both_three = swap(after(both_got, got), "seq", 1)
    pairs = jnp.concatenate([pairs, got], axis=0)
    pieces = (pairs, swap(pairs, "seq", 1))

    first_in, dy_all, ff_out, ff_grad, ff_grads, ff_stats, small0, small1 = feed_forward(
        meta,
        (both, both_got, both_two, both_three),
        vec_full,
        (weights, weights_even, weights_z, weights_x, weights_odd0, weights_odd1),
        2 * head_width + 32,
    )

    ff_z = swap_some(ff_grads, "row", 2, 1)
    stay, go, small_keep, small_send, stats, keep_pairs, send_pairs, cache_rows = attention(
        after(meta, ff_grads),
        first_in,
        dy_all,
        cosine,
        sine,
        (ff_out, ff_grad),
        vec_full,
        (small0, small1),
        ff_stats,
        pieces,
        shape,
    )

    got = swap(after(send_pairs, ff_z), "seq", 1)
    col_send = (keep_pairs[:, HALF:].astype(F32) + got[:, HALF:].astype(F32)).astype(BF16)
    col_got = swap(col_send, "col", 1)
    core_got = swap(after(go, col_send), "seq", 1)
    away = (stay[1] + core_got[1].astype(F32)).astype(BF16)
    back = swap(away, "row", 1)
    col_got = after(col_got, away)
    core = lax.rem(seq_me, 2)

    def core_halves(moved, axis=0):
        half = moved.shape[axis] // 2
        keep = lax.dynamic_slice_in_dim(moved, core * half, half, axis)
        return keep, lax.dynamic_slice_in_dim(moved, (1 - core) * half, half, axis)

    def over_seq(value):
        bit = 2
        while bit < seq_count:
            value = swap_add(value, "seq", bit)
            bit = bit * 2
        return value.astype(BF16)

    def both_halves(value):
        other = swap(value, "seq", 1)
        first = jnp.where(core == 0, value, other)
        second = jnp.where(core == 0, other, value)
        return jnp.concatenate([first, second], axis=0).astype(F32)

    ff_keep, ff_away = core_halves(jnp.where(core == 0, after(ff_grads, col_send), ff_z), 1)
    ff_core = swap(ff_away, "seq", 1)
    ff_col = swap(
        after((ff_keep[1].astype(F32) + ff_core[1].astype(F32)).astype(BF16), col_got), "col", 1
    )
    ff_sum = ff_keep[0].astype(F32) + ff_core[0].astype(F32) + ff_col.astype(F32)
    total = keep_pairs[:, :HALF].astype(F32) + got[:, :HALF].astype(F32) + col_got.astype(F32)
    small_got = swap(after(small_send, ff_col), "col", 1)
    small_sum = (small_keep.astype(F32) + small_got.astype(F32)).astype(BF16)
    for axis, bit in reversed(steps[2:]):
        half = total.shape[0] // 2
        total = total[:half] + swap(total[half:].astype(BF16), axis, bit).astype(F32)
    total = after(total, back)
    row_got = after(swap(total[2:].astype(BF16), "row", 2), ff_sum)
    small_moved = swap_odd_rows(after(small_sum, row_got))
    keep_two = total[:2]
    dy_sum = jnp.sum(cotangent.astype(F32), axis=0)[None]
    z_send = (keep_two[1] + row_got[1].astype(F32)).astype(BF16)
    z_got = swap(z_send, "row", 1)
    extra_mine, extra_send = pair_sums(
        keep_two, row_got, cosine, sine, first_in, keyval_full, vec_full, stats, ff_stats, dy_sum
    )
    extra = extra_mine + swap(extra_send, "col", 1).astype(F32)
    own_total = (keep_two[0] + row_got[0].astype(F32))[None]
    mine, away_rows = own_rows(
        own_total, z_got, cosine, sine, keyval_full, vec_full, x_block, dy_all, stay, core_got, back
    )
    other = swap(away_rows, "col", 1)
    first = jnp.where(col_me == 0, mine, other)
    second = jnp.where(col_me == 0, other, mine)
    layer_out = jnp.concatenate([first[0], second[0]], axis=0)
    grad_tokens = jnp.concatenate([first[1], second[1]], axis=0)

    sum_ff = both_halves(over_seq(ff_sum))
    sum_up = jnp.concatenate([sum_ff[:span], sum_ff[span : 2 * span]], axis=1)
    sum_down = sum_ff[2 * span :]
    keep, send = core_halves(small_moved)
    sum_small = both_halves(over_seq(keep.astype(F32) + swap(send, "seq", 1).astype(F32)))
    sum_query = jnp.transpose(sum_small[:head_width])
    sum_output = sum_small[head_width : 2 * head_width]
    base = 2 * head_width
    sum_bias_up = sum_small[base : base + 2].reshape(-1)
    sum_bias_query = sum_small[base + 2, :head_width]

    bit = 1
    while bit < seq_count:
        extra = swap_add(extra, "seq", bit)
        bit = bit * 2
    for bit in (1, 2):
        extra = swap_add(extra, "row", bit)
    part = pair_width // row_count
    keyval_weight_out = jnp.transpose(lax.dynamic_slice_in_dim(extra, row_me * part, part, 0))
    keyval_bias_out = lax.dynamic_slice_in_dim(extra[pair_width + 4], row_me * part, part, 0)
    bias_out_grad = extra[pair_width + 5]
    cache_rows = cache_rows.reshape(-1, pair_width)

    return (
        layer_out,
        cache_rows,
        grad_tokens,
        extra[pair_width],
        extra[pair_width + 1],
        extra[pair_width + 2],
        extra[pair_width + 3],
        sum_query,
        sum_bias_query,
        keyval_weight_out,
        keyval_bias_out,
        sum_up,
        sum_bias_up,
        sum_output,
        bias_out_grad,
        sum_down,
        bias_out_grad,
    )


def solution(mesh):
    in_specs = (
        P(("seq", "row"), None),
        P(("seq", "row"), "col"),
        P(),
        P(),
        P("col"),
        P("col"),
        P("col"),
        P("col"),
        P("col", "row"),
        P("row"),
        P("col", None),
        P(),
        P("col", "row"),
        P("row"),
        P("row", "col"),
        P("col"),
        P("row", "col"),
        P("col"),
    )
    out_specs = (
        P(("seq", "row"), "col"),
        P(("seq", "col"), None),
        P(("seq", "row"), "col"),
        P("col"),
        P("col"),
        P("col"),
        P("col"),
        P("col", "row"),
        P("row"),
        P("col", "row"),
        P("row"),
        P("col", "row"),
        P("row"),
        P("row", "col"),
        P("col"),
        P("row", "col"),
        P("col"),
    )
    return jax.shard_map(
        on_device, mesh=mesh, in_specs=in_specs, out_specs=out_specs, check_vma=False
    )
```

```python
import collections
import functools

import jax
import jax.numpy as jnp
from jax import lax
from jax.experimental import pallas as pl
from jax.experimental.pallas import tpu as pltpu
from jax.sharding import PartitionSpec as P

HD = 64
ROT = 16
BLOCK = 512
LONGEST = 16
VMEM = 60 * 1024 * 1024
Shape = collections.namedtuple("Shape", "seq_count row_count sequences heads")
HALF = 256
EPS = 1e-05
NEGATIVE = -1e30
F32 = jnp.float32
BF16 = jnp.bfloat16

NN = (((1,), (0,)), ((), ()))
NT = (((1,), (1,)), ((), ()))
TN = (((0,), (0,)), ((), ()))


def dot(left, right, dims=NN):
    return lax.dot_general(left, right, dims, preferred_element_type=F32)


def swap(value, axis, bit):
    count = lax.axis_size(axis)
    return lax.ppermute(value, axis, [(i, i ^ bit) for i in range(count)])


def swap_odd_rows(value):
    seq_count, row_count = lax.axis_size("seq"), lax.axis_size("row")
    pairs = []
    for s in range(1, seq_count, 2):
        for r in range(row_count):
            pairs.append((s * row_count + r, s * row_count + (r ^ 2)))
    moved = lax.ppermute(value, ("seq", "row"), pairs)
    return jnp.where(lax.rem(lax.axis_index("seq"), 2) == 0, value, moved)


def swap_some(value, axis, bit, parity):
    sizes = [lax.axis_size(name) for name in ("seq", "row", "col")]
    pairs = []
    for s in range(parity, sizes[0], 2):
        for r in range(sizes[1]):
            for c in range(sizes[2]):
                index = {"seq": s, "row": r, "col": c}
                source = (s * sizes[1] + r) * sizes[2] + c
                index[axis] ^= bit
                pairs.append((source, (index["seq"] * sizes[1] + index["row"]) * sizes[2] + index["col"]))
    return lax.ppermute(value, ("seq", "row", "col"), pairs)


def swap_add(value, axis, bit):
    rounded = lax.reduce_precision(value, 8, 7)
    return rounded + swap(rounded.astype(BF16), axis, bit).astype(F32)


def split_rows(vector):
    high = lax.reduce_precision(vector, 8, 7)
    return high.astype(BF16), (vector - high).astype(BF16)


def first_of(meta_ref, block, shape):
    start = jnp.int32(0)
    first = jnp.int32(0)
    for i in range(shape.sequences):
        first = jnp.where(start <= block, start, first)
        start = start + meta_ref[3 + i] // BLOCK
    return first


def attention_kernel(
    meta_ref,
    first_ref,
    dy_ref,
    cos_ref,
    sin_ref,
    ff_out_ref,
    ff_grad_ref,
    vec_ref,
    small0_ref,
    small1_ref,
    stats_ref,
    kv0_ref,
    kv1_ref,
    *rest,
    shape,
):
    heads = shape.heads
    stay_ref, go_ref, keep_ref, send_ref, stat_ref, dkv_out_ref, dkv_low_ref, cache_ref = rest[:8]
    dqw_ref, dow_ref, dqb_ref = rest[8:11]
    rest = rest[11:]
    (
        qd_ref,
        probs_ref,
        high_ref,
        sums_ref,
        dots_ref,
        acc_ref,
        dq_ref,
        dkv_ref,
        kv_ref,
        low_ref,
        zero_ref,
        qw_ref,
        ow_ref,
        copy_sem,
        late_sem,
    ) = rest
    blocks = kv_ref.shape[0]
    half = blocks // 2
    slot = pl.program_id(0)
    lanes = 2 * HD
    rows = heads * HALF
    seq, row, second_half = meta_ref[0], meta_ref[1], meta_ref[2]
    own_block = lax.bitwise_xor(seq, slot // 2) * shape.row_count + lax.bitwise_xor(row, slot % 2)
    first_block = first_of(meta_ref, own_block, shape)
    before = own_block - first_block

    def slot_of(block):
        apart_row = lax.bitwise_xor(lax.rem(block, shape.row_count), row)
        apart_seq = lax.bitwise_xor(block // shape.row_count, seq)
        return apart_row + shape.row_count * (
            apart_seq // 2 + (shape.seq_count // 2) * lax.rem(apart_seq, 2)
        )

    def put(index, rows):
        @pl.when(slot < 2)
        def _():
            stay_ref[slot, index] = rows

        @pl.when(slot >= 2)
        def _():
            go_ref[slot - 2, index] = rows.astype(BF16)

    def cache_copies(dealt, group):
        copies = []
        for i in range(dealt):
            owner = meta_ref[3 + shape.sequences + group * dealt + i]
            for part in (0, 1):
                take = jnp.where(second_half > 0, 1 - part, part) * HALF
                copies.append(
                    pltpu.make_async_copy(
                        kv_ref.at[slot_of(owner), pl.ds(take, HALF), :],
                        cache_ref.at[i, part * HALF : (part + 1) * HALF, :],
                        copy_sem.at[2 + 2 * i + part],
                    )
                )
        return copies

    pieces = [
        pltpu.make_async_copy(piece, kv_ref.at[i * half : (i + 1) * half], copy_sem.at[i])
        for i, piece in enumerate((kv0_ref, kv1_ref))
    ]
    late = [
        pltpu.make_async_copy(zero_ref, dkv_ref.at[i : i + 1], late_sem.at[i]) for i in range(blocks)
    ]

    @pl.when(slot == 0)
    def _():
        for copy in pieces:
            copy.start()
        zero_ref[...] = jnp.zeros_like(zero_ref)
        dqw_ref[...] = jnp.zeros_like(dqw_ref)
        dow_ref[...] = jnp.zeros_like(dow_ref)
        dqb_ref[...] = jnp.zeros_like(dqb_ref)
        for copy in late:
            copy.start()
        span = small0_ref.shape[1]
        count = heads * HD
        for i, small in enumerate((small0_ref, small1_ref)):
            part = slice(i * span, (i + 1) * span)
            qw_ref[:count, part] = small[:count, :]
            ow_ref[:count, part] = small[count : 2 * count, :]
        qw_ref[count:, :] = jnp.zeros_like(qw_ref[count:, :])
        ow_ref[count:, :] = jnp.zeros_like(ow_ref[count:, :])

    cosine = cos_ref[0]
    sine = sin_ref[0]
    lane = lax.broadcasted_iota(jnp.int32, (HALF, lanes), 1)
    front = lane < HD

    def rolled(values):
        return jnp.where(
            lane < ROT // 2,
            pltpu.roll(values, lanes - ROT // 2, 1),
            pltpu.roll(values, ROT // 2, 1),
        )

    def head_of(joined, h):
        return joined[:, (h // 2) * lanes : (h // 2 + 1) * lanes]

    def join(parts):
        tiles = []
        for h in range(0, heads, 2):
            other = parts[h + 1] if h + 1 < heads else jnp.zeros_like(parts[h])
            tiles.append(jnp.where(front, parts[h], other))
        return jnp.concatenate(tiles, axis=1)

    padded = qw_ref.shape[0]
    base = 2 * heads * HD + 7
    query_b = (
        small0_ref[base : base + 1, :padded].astype(F32)
        + small0_ref[base + 8 : base + 9, :padded].astype(F32)
    )
    pre_all = dot(first_ref[0], qw_ref[...], NT) + query_b
    d_all = dot(dy_ref[0], ow_ref[...], NT)
    for h in range(heads):
        pre = head_of(pre_all, h)
        grad = head_of(d_all, h)
        if h % 2:
            pre = pltpu.roll(pre, HD, 1)
        else:
            grad = pltpu.roll(grad, HD, 1)
        turned = jnp.where(front, pre * cosine + rolled(pre) * sine, 0.0)
        mine = slice(h * HALF, (h + 1) * HALF)
        qd_ref[mine, :] = turned.astype(BF16) * BF16(HD**-0.5)
        qd_ref[rows + h * HALF : rows + (h + 1) * HALF, :] = jnp.where(front, 0.0, grad).astype(BF16)

    @pl.when(slot == 0)
    def _():
        for copy in pieces:
            copy.wait()

    high_ref[...] = jnp.full_like(high_ref, NEGATIVE)
    sums_ref[...] = jnp.zeros_like(sums_ref)

    def block_at(step):
        return slot_of(first_block + step)

    def weigh(step, mask):
        scores = dot(kv_ref[block_at(step)], qd_ref[:rows, :], NT)
        if mask:
            row_in = lax.rem(lax.broadcasted_iota(jnp.int32, (BLOCK, rows), 1), HALF)
            key_in = lax.broadcasted_iota(jnp.int32, (BLOCK, rows), 0)
            limit = jnp.where(second_half > 0, BLOCK, 0)
            keep = (key_in <= row_in) | ((key_in >= HALF) & (key_in < limit))
            scores = jnp.where(keep, scores, NEGATIVE)
        high = jnp.max(scores, axis=0, keepdims=True)
        probs = jnp.exp(scores - high)
        probs_ref[step] = probs.astype(BF16)
        high_ref[pl.ds(step, 1), :] = high
        sums_ref[pl.ds(step, 1), :] = jnp.sum(probs, axis=0, keepdims=True)

    weigh(before, True)
    lax.fori_loop(0, before, lambda step, c: (weigh(step, False), c)[1], 0)

    share = jnp.exp(high_ref[...] - jnp.max(high_ref[...], axis=0, keepdims=True))
    high_ref[...] = share / jnp.sum(share * sums_ref[...], axis=0, keepdims=True)

    def mix(step, first):
        probs = (probs_ref[step].astype(F32) * high_ref[pl.ds(step, 1), :]).astype(BF16)
        probs_ref[step] = probs
        part = dot(probs, kv_ref[block_at(step)], TN)
        if first:
            acc_ref[...] = part
        else:
            acc_ref[...] += part

    mix(before, True)
    lax.fori_loop(0, before, lambda step, c: (mix(step, False), c)[1], 0)

    @pl.when(slot == 0)
    def _():
        for copy in late:
            copy.wait()

    parts = []
    for h in range(heads):
        mine = slice(h * HALF, (h + 1) * HALF)
        mixed = acc_ref[mine, :]
        grad = qd_ref[rows + h * HALF : rows + (h + 1) * HALF, :].astype(F32)
        dots_ref[:, mine] = jnp.sum(jnp.transpose(mixed * grad), axis=0, keepdims=True)
        parts.append(mixed if h % 2 else pltpu.roll(mixed, HD, 1))
    joined = join(parts).astype(BF16)
    put(0, ff_out_ref[0] + dot(joined, ow_ref[...]))
    dow_ref[...] += dot(joined, dy_ref[0], TN)

    def backward(step, first):
        where = block_at(step)
        block = kv_ref[where]
        probs = probs_ref[step]
        grad_probs = dot(block, qd_ref[rows:, :], NT)
        grad_scores = (probs.astype(F32) * (grad_probs - dots_ref[...])).astype(BF16)
        total = dot(jnp.concatenate([grad_scores, probs], axis=1), qd_ref[...])
        grad_q = dot(grad_scores, block, TN)
        if first:
            dq_ref[...] = grad_q
        else:
            dq_ref[...] += grad_q
        dkv_ref[where] = (dkv_ref[where].astype(F32) + total).astype(dkv_ref.dtype)

    backward(before, True)
    lax.fori_loop(0, before, lambda step, c: (backward(step, False), c)[1], 0)

    parts = []
    for h in range(heads):
        part = dq_ref[h * HALF : (h + 1) * HALF, :] * (HD**-0.5)
        part = part * cosine - rolled(part) * sine
        parts.append(pltpu.roll(part, HD, 1) if h % 2 else part)
    joined = join(parts)
    dqb_ref[...] += jnp.sum(joined, axis=0, keepdims=True)
    joined = joined.astype(BF16)
    put(1, ff_grad_ref[0] + dot(joined, qw_ref[...]) * vec_ref[0:1, :])
    dqw_ref[...] += dot(joined, first_ref[0], TN)

    @pl.when(slot == 0)
    def _():
        dealt = cache_ref.shape[0]
        group = seq * 2 + second_half
        for copy in cache_copies(dealt, group):
            copy.start()

    @pl.when(slot == 3)
    def _():
        copies = [pltpu.make_async_copy(dkv_ref.at[:half], dkv_out_ref, copy_sem.at[0])]
        copies[0].start()
        if dkv_ref.dtype == BF16:
            copies.append(pltpu.make_async_copy(dkv_ref.at[half:], dkv_low_ref, copy_sem.at[1]))
        else:
            low_ref[...] = dkv_ref[half:].astype(BF16)
            copies.append(pltpu.make_async_copy(low_ref, dkv_low_ref, copy_sem.at[1]))
        copies[1].start()
        copies += cache_copies(cache_ref.shape[0], seq * 2 + second_half)
        count = heads * HD
        span = small0_ref.shape[1]
        bias_up = stats_ref[2:3, :]
        bias_q = dqb_ref[...]
        for i, target in enumerate((keep_ref, send_ref)):
            part = slice(i * span, (i + 1) * span)
            target[:count, :] = dqw_ref[:count, part].astype(BF16)
            target[count : 2 * count, :] = dow_ref[:count, part].astype(BF16)
            rows_of = jnp.concatenate(
                [
                    bias_up[:, :span],
                    bias_up[:, span:],
                    jnp.concatenate([bias_q, jnp.zeros((1, span - padded), F32)], axis=1),
                    jnp.zeros((5, span), F32),
                ],
                axis=0,
            )
            target[2 * count :, :] = jnp.concatenate(
                [rows_of, jnp.zeros((target.shape[0] - 2 * count - 8, span), F32)], axis=0
            ).astype(BF16)
        weight = qw_ref[...].astype(F32)
        column = jnp.transpose(jnp.broadcast_to(bias_q, (8, padded)))[:, 0:1]
        plain = jnp.sum(weight * column, axis=0, keepdims=True)
        stat_ref[0:1, :] = (
            jnp.sum(weight * dqw_ref[...], axis=0, keepdims=True) - vec_ref[1:2, :] * plain
        ) / vec_ref[0:1, :]
        stat_ref[1:2, :] = plain
        stat_ref[2:8, :] = jnp.zeros((6, 2 * span), F32)
        for copy in copies:
            copy.wait()


def attention(meta, first_in, dy, cosine, sine, ff, vectors, small, stats, pieces, shape):
    _, _, width = first_in.shape
    half = pieces[0].shape[0]
    blocks = 2 * half
    lanes = 2 * HD
    heads = shape.heads
    padded = -(-heads // 2) * lanes
    rows = heads * HALF
    longest = min(LONGEST, blocks // 2)
    total_type = F32 if blocks <= 32 else BF16
    dealt = blocks // (2 * shape.seq_count)

    def per_slot(lanes):
        return pl.BlockSpec((1, HALF, lanes), lambda i, m: (i, 0, 0))

    def whole(array):
        return pl.BlockSpec(
            array.shape, lambda i, m: (0,) * len(array.shape), pipeline_mode=pl.Buffered(buffer_count=1)
        )

    far = pl.BlockSpec(memory_space=pltpu.MemorySpace.HBM)
    arrays = [first_in, dy, cosine, sine, *ff, vectors, *small, stats, *pieces]
    in_specs = [per_slot(width), per_slot(width), per_slot(lanes), per_slot(lanes)]
    in_specs += [per_slot(width)] * 2 + [whole(a) for a in (vectors, *small, stats)] + [far] * 2
    part = jax.ShapeDtypeStruct((2 * heads * HD + 32, width // 2), BF16)
    results = [
        jax.ShapeDtypeStruct((2, 2, HALF, width), F32),
        jax.ShapeDtypeStruct((2, 2, HALF, width), BF16),
        part,
        part,
        jax.ShapeDtypeStruct((8, width), F32),
    ]
    out_shape = [
        *results,
        jax.ShapeDtypeStruct((half, BLOCK, lanes), total_type),
        jax.ShapeDtypeStruct((half, BLOCK, lanes), BF16),
        jax.ShapeDtypeStruct((dealt, BLOCK, lanes), BF16),
    ]
    out_specs = [whole(a) for a in results] + [far] * 3
    return pl.pallas_call(
        functools.partial(attention_kernel, shape=shape),
        grid_spec=pltpu.PrefetchScalarGridSpec(
            num_scalar_prefetch=1,
            grid=(4,),
            in_specs=in_specs,
            out_specs=out_specs,
            scratch_shapes=[
                pltpu.VMEM((padded, width), F32),
                pltpu.VMEM((padded, width), F32),
                pltpu.VMEM((1, padded), F32),
                pltpu.VMEM((2 * rows, lanes), BF16),
                pltpu.VMEM((longest, BLOCK, rows), BF16),
                pltpu.VMEM((longest, rows), F32),
                pltpu.VMEM((longest, rows), F32),
                pltpu.VMEM((1, rows), F32),
                pltpu.VMEM((rows, lanes), F32),
                pltpu.VMEM((rows, lanes), F32),
                pltpu.VMEM((blocks, BLOCK, lanes), total_type),
                pltpu.VMEM((blocks, BLOCK, lanes), BF16),
                pltpu.VMEM((half if blocks <= 32 else 1, BLOCK, lanes), BF16),
                pltpu.VMEM((1, BLOCK, lanes), total_type),
                pltpu.VMEM((padded, width), BF16),
                pltpu.VMEM((padded, width), BF16),
                pltpu.SemaphoreType.DMA((2 + 2 * dealt,)),
                pltpu.SemaphoreType.DMA((blocks,)),
            ],
        ),
        out_shape=out_shape,
        cost_estimate=pl.CostEstimate(
            flops=24_000_000_000, bytes_accessed=30_000_000, transcendentals=30_000_000
        ),
        compiler_params=pltpu.CompilerParams(
            vmem_limit_bytes=67_043_328 if blocks > 32 else VMEM
        ),
        name="attention",
    )(meta, *arrays)


ORDER = (0, 1, 2, 3)


def tables_kernel(meta_ref, cos_ref, sin_ref, *, shape):
    seq, row, col = meta_ref[0], meta_ref[1], meta_ref[2]
    lane = lax.broadcasted_iota(jnp.int32, (HALF, 2 * HD), 1)
    inside = lax.broadcasted_iota(jnp.int32, (HALF, 2 * HD), 0)
    half_rot = ROT // 2
    exponent = lax.rem(lane, half_rot).astype(F32) * (1.0 / half_rot)
    frequency = jnp.where(lane < ROT, 1.0 / jnp.exp(exponent * jnp.log(jnp.full_like(exponent, 10000.0))), 0.0)
    insides = []
    for half in (col, 1 - col):
        angles = (inside + half * HALF).astype(F32) * frequency
        insides.append((jnp.cos(angles), jnp.sin(angles)))
    for i, slot in enumerate(ORDER + (0,)):
        block = lax.bitwise_xor(seq, slot // 2) * shape.row_count + lax.bitwise_xor(row, slot % 2)
        start = (block - first_of(meta_ref, block, shape)) * BLOCK
        angles = jnp.full((8, 2 * HD), start, jnp.int32).astype(F32) * frequency[:8, :]
        cos_start, sin_start = jnp.cos(angles)[0:1, :], jnp.sin(angles)[0:1, :]
        cos_in, sin_in = insides[i // 4]
        cos_ref[i] = cos_in * cos_start - sin_in * sin_start
        turned = sin_in * cos_start + cos_in * sin_start
        sin_ref[i] = jnp.where(lane < half_rot, -turned, jnp.where(lane < ROT, turned, 0.0))


def tables(meta, shape):
    table = jax.ShapeDtypeStruct((5, HALF, 2 * HD), F32)
    return pl.pallas_call(
        functools.partial(tables_kernel, shape=shape),
        in_specs=[pl.BlockSpec(memory_space=pltpu.SMEM)],
        out_specs=[pl.BlockSpec(memory_space=pltpu.VMEM)] * 2,
        out_shape=[table, table],
        name="tables",
    )(meta)


def forward_kernel(
    meta_ref,
    both0_ref,
    both1_ref,
    both2_ref,
    both3_ref,
    vec_ref,
    pack_ref,
    even_ref,
    z_ref,
    x_got_ref,
    odd0_ref,
    odd1_ref,
    first_ref,
    dy_ref,
    out_ref,
    dx_ref,
    grads_ref,
    stat_ref,
    small0_ref,
    small1_ref,
    x_ref,
    own_ref,
    other_ref,
    up_ref,
    down_ref,
    second_ref,
    hidden_ref,
    grad_ref,
    dys_ref,
    bias_ref,
    sem,
):
    step = pl.program_id(0)
    span = pack_ref.shape[1]
    total = pack_ref.shape[0]
    here = pl.ds(pl.multiple_of(step * HALF, HALF), HALF)
    core = lax.rem(meta_ref[0], 2)
    side = lax.rem(meta_ref[0] // 2, 2)

    def run(copies):
        for copy in copies:
            copy.start()
        for copy in copies:
            copy.wait()

    @pl.when((step == 0) & (core == 0))
    def _():
        run(
            [
                pltpu.make_async_copy(pack_ref, own_ref, sem.at[0]),
                pltpu.make_async_copy(even_ref, other_ref, sem.at[1]),
            ]
        )

    @pl.when((step == 0) & (core == 1))
    def _():
        half = total // 2
        near = pl.ds(pl.multiple_of(side * half, half), half)
        far = pl.ds(pl.multiple_of((1 - side) * half, half), half)
        run(
            [
                pltpu.make_async_copy(z_ref, own_ref.at[near, :], sem.at[0]),
                pltpu.make_async_copy(x_got_ref, own_ref.at[far, :], sem.at[1]),
                pltpu.make_async_copy(odd0_ref, other_ref.at[near, :], sem.at[2]),
                pltpu.make_async_copy(odd1_ref, other_ref.at[far, :], sem.at[3]),
            ]
        )

    @pl.when(step == 0)
    def _():
        base = small0_ref.shape[0]
        for i, held in enumerate((own_ref, other_ref)):
            part = slice(i * span, (i + 1) * span)
            (small0_ref, small1_ref)[i][...] = held[:base, :]
            up_ref[part, :span] = held[base : base + span, :]
            up_ref[part, span:] = held[base + span : base + 2 * span, :]
            down_ref[:, part] = held[base + 2 * span : base + 4 * span, :]
        bias_ref[...] = jnp.zeros_like(bias_ref)

    for i, piece in enumerate((both0_ref, both1_ref, both2_ref, both3_ref)):

        @pl.when(step == i)
        def _():
            x_ref[...] = piece[0]
            dys_ref[here, :] = piece[1]

    base = small0_ref.shape[0] - 32
    bias = own_ref[base : base + 8, :].astype(F32) + own_ref[base + 8 : base + 16, :].astype(F32)
    upward_b = jnp.concatenate([bias[5:6], bias[6:7]], axis=1)
    wide = x_ref[...].astype(F32)
    mean = jnp.mean(wide, axis=1, keepdims=True)
    spread = jnp.mean(wide * wide, axis=1, keepdims=True) - mean * mean
    normed = (wide - mean) * lax.rsqrt(spread + EPS)
    first_ref[0] = (normed * vec_ref[0:1, :] + vec_ref[1:2, :]).astype(BF16)
    second = (normed * vec_ref[2:3, :] + vec_ref[3:4, :]).astype(BF16)
    dy = dys_ref[here, :]
    dy_ref[0] = dy
    second_ref[here, :] = second
    upward = dot(second, up_ref[...]) + upward_b
    bell = lax.erf(upward * (2.0**-0.5)) * 0.5 + 0.5
    hidden = (upward * bell).astype(BF16)
    slope = bell + upward * jnp.exp(upward * upward * -0.5) * ((2.0 * 3.141592653589793) ** -0.5)
    grad = dot(dy, down_ref[...], NT) * slope
    bias_ref[0:1, :] += jnp.sum(grad, axis=0, keepdims=True)
    grad = grad.astype(BF16)
    hidden_ref[here, :] = hidden
    grad_ref[here, :] = grad
    out_ref[0] = dot(hidden, down_ref[...])
    dx_ref[0] = dot(grad, up_ref[...], NT) * vec_ref[2:3, :]

    @pl.when(step == 3)
    def _():
        down_grad = dot(hidden_ref[...], dys_ref[...], TN)
        grads_ref[0, 2 * span :, :] = down_grad[:, :span].astype(BF16)
        grads_ref[1, 2 * span :, :] = down_grad[:, span:].astype(BF16)
        up_grad = dot(second_ref[...], grad_ref[...], TN)
        for i in (0, 1):
            part = slice(i * span, (i + 1) * span)
            grads_ref[0, part, :] = up_grad[:span, part].astype(BF16)
            grads_ref[1, part, :] = up_grad[span:, part].astype(BF16)
        weight = up_ref[...].astype(F32)
        bias_grad = bias_ref[0:1, :]

        def as_row(values):
            column = jnp.sum(values, axis=1, keepdims=True)
            return jnp.transpose(jnp.broadcast_to(column, (2 * span, 128)))[0:1, :]

        plain = as_row(weight * bias_grad)
        stat_ref[0:1, :] = (as_row(weight * up_grad) - vec_ref[3:4, :] * plain) / vec_ref[2:3, :]
        stat_ref[1:2, :] = plain
        stat_ref[2:3, :] = bias_grad
        stat_ref[3:8, :] = jnp.zeros((5, 2 * span), F32)


def feed_forward(meta, both, vectors, weights, small_rows):
    width = vectors.shape[1]
    span = width // 2
    total = weights[0].shape[0]

    def whole(array):
        return pl.BlockSpec(
            array.shape, lambda i: (0,) * len(array.shape), pipeline_mode=pl.Buffered(buffer_count=1)
        )

    slot = pl.BlockSpec((1, HALF, width), lambda i: (i, 0, 0))
    arrays = [*both, vectors]
    grads = jax.ShapeDtypeStruct((2, 4 * span, span), BF16)
    stat = jax.ShapeDtypeStruct((8, width), F32)
    small = jax.ShapeDtypeStruct((small_rows, span), BF16)
    tokens = lambda kind: jax.ShapeDtypeStruct((4, HALF, width), kind)
    return pl.pallas_call(
        forward_kernel,
        grid=(4,),
        in_specs=[pl.BlockSpec(memory_space=pltpu.SMEM)]
        + [whole(a) for a in arrays]
        + [pl.BlockSpec(memory_space=pltpu.MemorySpace.HBM)] * len(weights),
        out_specs=[slot] * 4 + [whole(grads), whole(stat), whole(small), whole(small)],
        out_shape=[tokens(BF16), tokens(BF16), tokens(F32), tokens(F32), grads, stat, small, small],
        scratch_shapes=[
            pltpu.VMEM((HALF, width), BF16),
            pltpu.VMEM((total, span), BF16),
            pltpu.VMEM((total, span), BF16),
            pltpu.VMEM((width, width), BF16),
            pltpu.VMEM((width, width), BF16),
            pltpu.VMEM((4 * HALF, width), BF16),
            pltpu.VMEM((4 * HALF, width), BF16),
            pltpu.VMEM((4 * HALF, width), BF16),
            pltpu.VMEM((4 * HALF, width), BF16),
            pltpu.VMEM((8, width), F32),
            pltpu.SemaphoreType.DMA((4,)),
        ],
        cost_estimate=pl.CostEstimate(
            flops=7_000_000_000, bytes_accessed=20_000_000, transcendentals=3_000_000
        ),
        compiler_params=pltpu.CompilerParams(vmem_limit_bytes=VMEM),
        name="feed_forward",
    )(meta, *arrays, *weights)


def prologue_kernel(
    where_ref, tokens_ref, dy_ref, kvw_ref, vec_ref, pack_ref, x_ref, mine_ref
):
    col = where_ref[2]
    span = dy_ref.shape[1]
    width = tokens_ref.shape[1]
    here = pl.ds(pl.multiple_of(col * HALF, HALF), HALF)
    there = pl.ds(pl.multiple_of((1 - col) * HALF, HALF), HALF)
    pack_ref[:HALF, :] = dy_ref[there, :]
    base = HALF + 2 * HD
    pack_ref[HALF:base, :] = jnp.transpose(kvw_ref[...].astype(F32)).astype(BF16)
    vectors = vec_ref[...]
    high = vectors.astype(BF16).astype(F32)
    both = jnp.concatenate([high, vectors - high], axis=0).astype(BF16)
    pack_ref[base:, :] = both
    for i, rows in enumerate((here, there)):
        part = slice(i * HALF, (i + 1) * HALF)
        x_ref[part, :span] = tokens_ref[rows, pl.ds(pl.multiple_of(col * span, 128), span)]
        x_ref[part, span:] = tokens_ref[rows, pl.ds(pl.multiple_of((1 - col) * span, 128), span)]
    mine_ref[...] = dy_ref[here, :]


def prologue(meta, tokens, cotangent, keyval_weight, vectors):
    width = tokens.shape[1]
    span = width // 2
    rows = vectors.shape[0]
    vmem = pl.BlockSpec(memory_space=pltpu.VMEM)
    return pl.pallas_call(
        prologue_kernel,
        in_specs=[pl.BlockSpec(memory_space=pltpu.SMEM)] + [vmem] * 4,
        out_specs=[vmem] * 3,
        out_shape=[
            jax.ShapeDtypeStruct((HALF + 2 * HD + 2 * rows, span), BF16),
            jax.ShapeDtypeStruct((2 * HALF, width), BF16),
            jax.ShapeDtypeStruct((HALF, span), BF16),
        ],
        name="prologue",
    )(meta, tokens, cotangent, keyval_weight, vectors)


def weights_kernel(where_ref, qw_ref, ow_ref, up_ref, down_ref, vec_ref, pack_ref, part_ref):
    count = qw_ref.shape[0]
    span = pack_ref.shape[1]
    total = pack_ref.shape[0]
    vectors = vec_ref[...]
    high = vectors.astype(BF16).astype(F32)
    both = jnp.concatenate([high, vectors - high], axis=0).astype(BF16)
    pack_ref[:count, :] = qw_ref[...]
    pack_ref[count : 2 * count, :] = ow_ref[...]
    pack_ref[2 * count : 2 * count + 16, :] = both
    pack_ref[2 * count + 16 : 2 * count + 32, :] = jnp.zeros((16, span), BF16)
    base = 2 * count + 32
    pack_ref[base : base + span, :] = up_ref[:, :span]
    pack_ref[base + span : base + 2 * span, :] = up_ref[:, span:]
    pack_ref[base + 2 * span :, :] = down_ref[...]
    side = lax.rem(where_ref[0] // 2, 2)
    part_ref[...] = pack_ref[pl.ds(pl.multiple_of(side * (total // 2), 16), total // 2), :]


def pack_weights(meta, query_t, output_weight, upward_weight, down_weight, vectors):
    span = output_weight.shape[1]
    total = 2 * query_t.shape[0] + 32 + 2 * upward_weight.shape[0] + down_weight.shape[0]
    vmem = pl.BlockSpec(memory_space=pltpu.VMEM)
    return pl.pallas_call(
        weights_kernel,
        in_specs=[pl.BlockSpec(memory_space=pltpu.SMEM)] + [vmem] * 5,
        out_specs=[vmem] * 2,
        out_shape=[
            jax.ShapeDtypeStruct((total, span), BF16),
            jax.ShapeDtypeStruct((total // 2, span), BF16),
        ],
        name="pack_weights",
    )(meta, query_t, output_weight, upward_weight, down_weight, vectors)


def own_kernel(
    x_ref, mine_ref, pack_ref, got_ref, vec_ref, cos_ref, sin_ref, bias_ref, pair_ref, both_ref, kvw_ref, full_ref
):
    span = mine_ref.shape[1]
    rows = vec_ref.shape[0]
    base = HALF + 2 * HD
    other = got_ref[base : base + 2 * rows, :].astype(F32)
    full = jnp.concatenate([vec_ref[...], other[:rows] + other[rows:]], axis=1)
    full_ref[...] = full
    both_ref[0] = x_ref[:HALF, :]
    both_ref[1, :, :span] = mine_ref[...]
    both_ref[1, :, span:] = got_ref[:HALF, :]
    kvw_ref[:, :span] = pack_ref[HALF:base, :]
    kvw_ref[:, span:] = got_ref[HALF:base, :]
    wide = x_ref[...].astype(F32)
    mean = jnp.mean(wide, axis=1, keepdims=True)
    spread = jnp.mean(wide * wide, axis=1, keepdims=True) - mean * mean
    normed = (wide - mean) * lax.rsqrt(spread + EPS)
    first = (normed * full[0:1, :] + full[1:2, :]).astype(BF16)
    pre_all = dot(first, kvw_ref[...], NT) + bias_ref[...]
    lanes = pre_all.shape[1]
    lane = lax.broadcasted_iota(jnp.int32, (HALF, lanes), 1)
    for i in (0, 1):
        pre = pre_all[i * HALF : (i + 1) * HALF, :]
        rolled = jnp.where(
            lane < ROT // 2, pltpu.roll(pre, lanes - ROT // 2, 1), pltpu.roll(pre, ROT // 2, 1)
        )
        pair_ref[0, i * HALF : (i + 1) * HALF, :] = (
            pre * cos_ref[4 * i] + rolled * sin_ref[4 * i]
        ).astype(BF16)


def own_pairs(x_own, mine, pack, got, vectors, cosine, sine, bias):
    width = x_own.shape[1]
    vmem = pl.BlockSpec(memory_space=pltpu.VMEM)
    return pl.pallas_call(
        own_kernel,
        in_specs=[vmem] * 8,
        out_specs=[vmem] * 4,
        out_shape=[
            jax.ShapeDtypeStruct((1, 2 * HALF, 2 * HD), BF16),
            jax.ShapeDtypeStruct((2, HALF, width), BF16),
            jax.ShapeDtypeStruct((2 * HD, width), BF16),
            jax.ShapeDtypeStruct((vectors.shape[0], width), F32),
        ],
        name="own_pairs",
    )(x_own, mine, pack, got, vectors, cosine, sine, bias)


def pairs_kernel(
    keep_ref, got_ref, cos_ref, sin_ref, first_ref, kvw_ref, vec_ref, stat_ref, ff_ref, dys_ref, mine_ref, send_ref
):
    span = mine_ref.shape[1]
    lanes = 2 * HD
    lane = lax.broadcasted_iota(jnp.int32, (HALF, lanes), 1)
    total = keep_ref[...] + got_ref[...].astype(F32)
    weight = jnp.zeros((lanes, 2 * span), F32)
    bias = jnp.zeros((1, lanes), F32)
    for i in (0, 1):
        part = total[i]
        rolled = jnp.where(
            lane < ROT // 2, pltpu.roll(part, lanes - ROT // 2, 1), pltpu.roll(part, ROT // 2, 1)
        )
        turned = part * cos_ref[i] - rolled * sin_ref[i]
        bias = bias + jnp.sum(turned, axis=0, keepdims=True)
        weight = weight + dot(turned.astype(BF16), first_ref[i], TN)
    kvw = kvw_ref[...].astype(F32)
    column = jnp.transpose(jnp.broadcast_to(bias, (8, lanes)))[:, 0:1]
    plain = jnp.sum(kvw * column, axis=0, keepdims=True)
    gain = (jnp.sum(kvw * weight, axis=0, keepdims=True) - vec_ref[1:2, :] * plain) / vec_ref[0:1, :]
    fill = jnp.zeros((1, span - lanes), F32)
    bias = jnp.concatenate([bias.astype(BF16).astype(F32), fill], axis=1)
    for i, target in enumerate((mine_ref, send_ref)):
        part = slice(i * span, (i + 1) * span)
        target[:lanes, :] = weight[:, part].astype(target.dtype)
        rows = jnp.concatenate(
            [
                stat_ref[0:1, part] + gain[:, part],
                stat_ref[1:2, part] + plain[:, part],
                ff_ref[0:2, part],
                bias,
                dys_ref[...] if i == 0 else jnp.zeros((1, span), F32),
                jnp.zeros((10, span), F32),
            ],
            axis=0,
        )
        target[lanes:, :] = rows.astype(target.dtype)


def pair_sums(keep, got, cosine, sine, first_in, keyval, vectors, stats, ff_stats, dy_sum):
    width = keyval.shape[1]
    vmem = pl.BlockSpec(memory_space=pltpu.VMEM)
    return pl.pallas_call(
        pairs_kernel,
        grid=(1,),
        in_specs=[vmem, vmem, head(cosine, 2), head(sine, 2), head(first_in, 2)] + [vmem] * 5,
        out_specs=[vmem] * 2,
        out_shape=[
            jax.ShapeDtypeStruct((2 * HD + 16, width // 2), F32),
            jax.ShapeDtypeStruct((2 * HD + 16, width // 2), BF16),
        ],
        name="pair_sums",
    )(keep, got, cosine, sine, first_in, keyval, vectors, stats, ff_stats, dy_sum)


def rows_kernel(
    own_ref,
    got_ref,
    cos_ref,
    sin_ref,
    kvw_ref,
    vec_ref,
    x_ref,
    dy_ref,
    keep_ref,
    core_ref,
    back_ref,
    mine_ref,
    send_ref,
):
    span = mine_ref.shape[2]
    lanes = 2 * HD
    lane = lax.broadcasted_iota(jnp.int32, (HALF, lanes), 1)
    part = own_ref[0] + got_ref[...].astype(F32)
    rolled = jnp.where(
        lane < ROT // 2, pltpu.roll(part, lanes - ROT // 2, 1), pltpu.roll(part, ROT // 2, 1)
    )
    turned = (part * cos_ref[0] - rolled * sin_ref[0]).astype(BF16)
    wide = x_ref[:HALF, :].astype(F32)
    mean = jnp.mean(wide, axis=1, keepdims=True)
    spread = jnp.mean(wide * wide, axis=1, keepdims=True) - mean * mean
    root = lax.rsqrt(spread + EPS)
    normed = (wide - mean) * root
    grad = keep_ref[0, 1] + core_ref[0, 1].astype(F32) + back_ref[1].astype(F32) + dot(turned, kvw_ref[...]) * vec_ref[0:1, :]
    one = jnp.mean(grad, axis=1, keepdims=True)
    two = jnp.mean(grad * normed, axis=1, keepdims=True)
    grad = dy_ref[0].astype(F32) + root * (grad - one - normed * two)
    out = wide + keep_ref[0, 0] + core_ref[0, 0].astype(F32) + back_ref[0].astype(F32) + vec_ref[4:5, :]
    for i, rows in enumerate((out.astype(BF16), grad.astype(BF16))):
        mine_ref[i] = rows[:, :span]
        send_ref[i] = rows[:, span:]


def head(array, count):
    rank = len(array.shape)
    return pl.BlockSpec((count,) + array.shape[1:], lambda i: (0,) * rank)


def own_rows(own, got, cosine, sine, keyval, vectors, x_block, dy, keep, core, back):
    width = keyval.shape[1]
    vmem = pl.BlockSpec(memory_space=pltpu.VMEM)
    half = jax.ShapeDtypeStruct((2, HALF, width // 2), BF16)
    return pl.pallas_call(
        rows_kernel,
        grid=(1,),
        in_specs=[vmem, vmem, head(cosine, 1), head(sine, 1), vmem, vmem, head(x_block, HALF)]
        + [head(dy, 1), head(keep, 1), head(core, 1), vmem],
        out_specs=[vmem] * 2,
        out_shape=[half, half],
        name="own_rows",
    )(own, got, cosine, sine, keyval, vectors, x_block, dy, keep, core, back)


def after(value, *others):
    return lax.optimization_barrier((value,) + others)[0]


def on_device(
    tokens,
    cotangent,
    lengths,
    block_order,
    attention_gain,
    attention_shift,
    feedforward_gain,
    feedforward_shift,
    query_weight,
    query_bias,
    keyval_weight,
    keyval_bias,
    upward_weight,
    upward_bias,
    output_weight,
    output_bias,
    down_weight,
    down_bias,
):
    seq_count = lax.axis_size("seq")
    row_count = lax.axis_size("row")
    col_count = lax.axis_size("col")
    seq_me = lax.axis_index("seq")
    row_me = lax.axis_index("row")
    col_me = lax.axis_index("col")
    block_total = block_order.shape[0]
    width = tokens.shape[1]
    span = width // 2
    heads = query_weight.shape[1] // HD
    head_width = heads * HD
    pair_width = 2 * HD

    shape = Shape(seq_count, row_count, lengths.shape[0], heads)
    meta = jnp.concatenate(
        [jnp.stack([seq_me, row_me, col_me]).astype(jnp.int32), lengths, block_order]
    )

    vectors = jnp.concatenate(
        [
            attention_gain,
            attention_shift,
            feedforward_gain,
            feedforward_shift,
            output_bias + down_bias,
            upward_bias,
            query_bias,
            jnp.zeros((span - head_width,), F32),
        ]
    ).reshape(8, span)
    pack, x_block, dy_mine = prologue(meta, tokens, cotangent, keyval_weight, vectors)
    received = swap(pack, "col", 1)
    weights, weights_half = pack_weights(
        after(meta, pack), jnp.transpose(query_weight), output_weight, upward_weight, down_weight, vectors
    )
    weights_z = swap_some(weights_half, "row", 2, 1)
    weights_even = swap_some(after(weights, received), "col", 1, 0)
    cosine, sine = tables(after(meta, weights), shape)

    pairs, both, keyval_full, vec_full = own_pairs(
        x_block, dy_mine, pack, received, vectors, cosine, sine, keyval_bias[None]
    )
    steps = [("row", 1), ("row", 2)]
    bit = 2
    while bit < seq_count:
        steps.append(("seq", bit))
        bit = bit * 2
    got = swap(pairs, "row", 1)
    weights_x = swap_some(after(weights_z, got), "seq", 2, 1)
    weights_odd0 = swap_some(after(weights_z, got), "col", 1, 1)
    both_got = swap(after(both, got), "row", 1)
    pairs = jnp.concatenate([pairs, got], axis=0)
    got = swap(pairs, "row", 2)
    weights_odd1 = swap_some(after(weights_x, got), "col", 1, 1)
    got = after(got, weights_x, weights_odd0, weights_even)
    for axis, bit in steps[2:]:
        pairs = jnp.concatenate([pairs, got], axis=0)
        got = swap(pairs, axis, bit)
    got = after(got, weights_odd1, both_got)
    both_two = swap(after(both, got), "seq", 1)
    both_three = swap(after(both_got, got), "seq", 1)
    pairs = jnp.concatenate([pairs, got], axis=0)
    pieces = (pairs, swap(pairs, "seq", 1))

    first_in, dy_all, ff_out, ff_grad, ff_grads, ff_stats, small0, small1 = feed_forward(
        meta,
        (both, both_got, both_two, both_three),
        vec_full,
        (weights, weights_even, weights_z, weights_x, weights_odd0, weights_odd1),
        2 * head_width + 32,
    )

    ff_z = swap_some(ff_grads, "row", 2, 1)
    stay, go, small_keep, small_send, stats, keep_pairs, send_pairs, cache_rows = attention(
        after(meta, ff_grads),
        first_in,
        dy_all,
        cosine,
        sine,
        (ff_out, ff_grad),
        vec_full,
        (small0, small1),
        ff_stats,
        pieces,
        shape,
    )

    got = swap(after(send_pairs, ff_z), "seq", 1)
    col_send = (keep_pairs[:, HALF:].astype(F32) + got[:, HALF:].astype(F32)).astype(BF16)
    col_got = swap(col_send, "col", 1)
    core_got = swap(after(go, col_send), "seq", 1)
    away = (stay[1] + core_got[1].astype(F32)).astype(BF16)
    back = swap(away, "row", 1)
    col_got = after(col_got, away)
    core = lax.rem(seq_me, 2)

    def core_halves(moved, axis=0):
        half = moved.shape[axis] // 2
        keep = lax.dynamic_slice_in_dim(moved, core * half, half, axis)
        return keep, lax.dynamic_slice_in_dim(moved, (1 - core) * half, half, axis)

    def over_seq(value):
        bit = 2
        while bit < seq_count:
            value = swap_add(value, "seq", bit)
            bit = bit * 2
        return value.astype(BF16)

    def both_halves(value):
        other = swap(value, "seq", 1)
        first = jnp.where(core == 0, value, other)
        second = jnp.where(core == 0, other, value)
        return jnp.concatenate([first, second], axis=0).astype(F32)

    ff_keep, ff_away = core_halves(jnp.where(core == 0, after(ff_grads, col_send), ff_z), 1)
    ff_core = swap(ff_away, "seq", 1)
    ff_col = swap(
        after((ff_keep[1].astype(F32) + ff_core[1].astype(F32)).astype(BF16), col_got), "col", 1
    )
    ff_sum = ff_keep[0].astype(F32) + ff_core[0].astype(F32) + ff_col.astype(F32)
    total = keep_pairs[:, :HALF].astype(F32) + got[:, :HALF].astype(F32) + col_got.astype(F32)
    small_got = swap(after(small_send, ff_col), "col", 1)
    small_sum = (small_keep.astype(F32) + small_got.astype(F32)).astype(BF16)
    for axis, bit in reversed(steps[2:]):
        half = total.shape[0] // 2
        total = total[:half] + swap(total[half:].astype(BF16), axis, bit).astype(F32)
    total = after(total, back)
    row_got = after(swap(total[2:].astype(BF16), "row", 2), ff_sum)
    small_moved = swap_odd_rows(after(small_sum, row_got))
    keep_two = total[:2]
    dy_sum = jnp.sum(cotangent.astype(F32), axis=0)[None]
    z_send = (keep_two[1] + row_got[1].astype(F32)).astype(BF16)
    z_got = swap(z_send, "row", 1)
    extra_mine, extra_send = pair_sums(
        keep_two, row_got, cosine, sine, first_in, keyval_full, vec_full, stats, ff_stats, dy_sum
    )
    extra = extra_mine + swap(extra_send, "col", 1).astype(F32)
    own_total = (keep_two[0] + row_got[0].astype(F32))[None]
    mine, away_rows = own_rows(
        own_total, z_got, cosine, sine, keyval_full, vec_full, x_block, dy_all, stay, core_got, back
    )
    other = swap(away_rows, "col", 1)
    first = jnp.where(col_me == 0, mine, other)
    second = jnp.where(col_me == 0, other, mine)
    layer_out = jnp.concatenate([first[0], second[0]], axis=0)
    grad_tokens = jnp.concatenate([first[1], second[1]], axis=0)

    sum_ff = both_halves(over_seq(ff_sum))
    sum_up = jnp.concatenate([sum_ff[:span], sum_ff[span : 2 * span]], axis=1)
    sum_down = sum_ff[2 * span :]
    keep, send = core_halves(small_moved)
    sum_small = both_halves(over_seq(keep.astype(F32) + swap(send, "seq", 1).astype(F32)))
    sum_query = jnp.transpose(sum_small[:head_width])
    sum_output = sum_small[head_width : 2 * head_width]
    base = 2 * head_width
    sum_bias_up = sum_small[base : base + 2].reshape(-1)
    sum_bias_query = sum_small[base + 2, :head_width]

    bit = 1
    while bit < seq_count:
        extra = swap_add(extra, "seq", bit)
        bit = bit * 2
    for bit in (1, 2):
        extra = swap_add(extra, "row", bit)
    part = pair_width // row_count
    keyval_weight_out = jnp.transpose(lax.dynamic_slice_in_dim(extra, row_me * part, part, 0))
    keyval_bias_out = lax.dynamic_slice_in_dim(extra[pair_width + 4], row_me * part, part, 0)
    bias_out_grad = extra[pair_width + 5]
    cache_rows = cache_rows.reshape(-1, pair_width)

    return (
        layer_out,
        cache_rows,
        grad_tokens,
        extra[pair_width],
        extra[pair_width + 1],
        extra[pair_width + 2],
        extra[pair_width + 3],
        sum_query,
        sum_bias_query,
        keyval_weight_out,
        keyval_bias_out,
        sum_up,
        sum_bias_up,
        sum_output,
        bias_out_grad,
        sum_down,
        bias_out_grad,
    )


def solution(mesh):
    in_specs = (
        P(("seq", "row"), None),
        P(("seq", "row"), "col"),
        P(),
        P(),
        P("col"),
        P("col"),
        P("col"),
        P("col"),
        P("col", "row"),
        P("row"),
        P("col", None),
        P(),
        P("col", "row"),
        P("row"),
        P("row", "col"),
        P("col"),
        P("row", "col"),
        P("col"),
    )
    out_specs = (
        P(("seq", "row"), "col"),
        P(("seq", "col"), None),
        P(("seq", "row"), "col"),
        P("col"),
        P("col"),
        P("col"),
        P("col"),
        P("col", "row"),
        P("row"),
        P("col", "row"),
        P("row"),
        P("col", "row"),
        P("row"),
        P("row", "col"),
        P("col"),
        P("row", "col"),
        P("col"),
    )
    return jax.shard_map(
        on_device, mesh=mesh, in_specs=in_specs, out_specs=out_specs, check_vma=False
    )
```
